128 devices in a mesh: users: 16 (over y, x), seq: 8 (over z, core).
Axes of the slice: x: 4, y: 4, z: 4, core: 2. Of those that a mesh axis runs over, the one named last changes fastest.
Arguments:
- item_table: bfloat16 [262144, 512], P(('users', 'seq')), may hold values from -6 to 6
- item_ids: int32 [16, 3072], P('users', 'seq'), may hold values from 0 to 262143, as said below
- segment_ids: int32 [16, 3072], P('users', 'seq'), may hold values from 0 to 2, never falling along the last dimension, each value on 1 to 1536 neighbouring positions
- weight_in: bfloat16 [512, 2048], replicated, may hold values from -0.25 to 0.25
- weight_out: bfloat16 [512, 512], replicated, may hold values from -0.25 to 0.25
- gain_in: float32 [512], replicated, may hold values from 0.5 to 1.5
- gain_mid: float32 [512], replicated, may hold values from 0.5 to 1.5
- cotangent: bfloat16 [16, 3072, 512], P('users', 'seq'), may hold values from -6 to 6
Outputs:
- layer_out: bfloat16 [16, 3072, 512], P('users', 'seq')
- table_grad: float32 [262144, 512], P(('users', 'seq'))
- weight_in_grad: float32 [512, 2048], replicated
- weight_out_grad: float32 [512, 512], replicated
The draws below stay inside these ranges and needn't reach their ends.
Inputs may be any that keep to these rules, and one draw needn't show every extreme that they name: `item_ids`: row r is held by device r // 2048 counted over users then seq. The 384 events of one device name rows of at most 6 events for each holding device, and in every draw each device has exactly 6 events whose rows one device holds.
All inputs are finite; a program needn't handle non-finite values.
Results may differ from the reference program's by a relative error of at most 0.006.
The reference program's roundings to bfloat16 on the way count: a program that leaves them out, or rounds other values in their place, can miss the bound.
Values may be sent and summed in bfloat16 or wider, within the bound.
No kernel may reach another device: no remote copies, remote signals or barrier semaphores. Data moves between devices by JAX's collectives and lax.ppermute only.
A program may use at most 128 MiB of HBM per device.

```python
import math
import jax
import jax.numpy as jnp
import numpy as np
from jax import lax

HEADS = 8
HEAD_DIM = 64
D = 512
L_DEV = 384
ROWS_DEV = 2048
USERS = 16
LEN = 3072
ROWS = 262144
CAP = 6


def draw_item_ids(key, part):
    blocks = USERS * LEN // L_DEV
    slots = blocks * CAP

    def one_block(block_key):
        key_perm, key_owner, key_shuffle, key_rows = jax.random.split(block_key, 4)
        ranking = jax.random.permutation(key_perm, slots)
        favoured = jax.random.randint(key_owner, (), 0, blocks)
        owners_of = jnp.arange(slots) // CAP
        scores = jnp.where(owners_of == favoured, ranking - slots, ranking)
        picked = jnp.argsort(scores, stable=True)[:L_DEV]
        owners = (picked // CAP)[jax.random.permutation(key_shuffle, L_DEV)]
        within = jax.random.randint(key_rows, (L_DEV,), 0, ROWS_DEV)
        return (owners * ROWS_DEV + within).astype(jnp.int32)
    return jax.vmap(one_block)(jax.random.split(key, blocks)).reshape(USERS, LEN)


def level_of(key, dims, shards, low, high):
    def one(dim, blocks):
        steps = jax.random.uniform(jax.random.fold_in(jax.random.fold_in(key, 6), dim), (blocks,), jnp.float32, low / len(shards), high / len(shards))
        return jnp.repeat(jnp.exp(steps), dims[dim] // blocks).reshape((-1,) + (1,) * (len(dims) - dim - 1))

    loudness = one(*shards[0])
    for cut in shards[1:]:
        loudness = loudness * one(*cut)
    return loudness


def split_up(amount, total, limit, lean):
    weights = [(1 << 20) // math.isqrt(standing ** lean) + 1 for standing in range(2, amount + 1)]
    surplus, counts = total - limit - (amount - 1), [1] * (amount - 1)
    while surplus > 0:
        free = [i for i in range(amount - 1) if counts[i] < limit]
        mass, remaining = sum([weights[i] for i in free]), surplus
        for i in free:
            extra = min(limit - counts[i], max(1, remaining * weights[i] // mass), surplus)
            counts[i] = counts[i] + extra
            surplus = surplus - extra
    return np.array([limit] + counts)


def uneven_parts(own_key, number_of, total, reach, slope):
    if number_of == 2:
        one = jax.random.randint(own_key, (), max(1, total - reach), min(reach, total - 1) + 1)
        return jnp.stack([one, total - one])
    sizes = jnp.asarray(split_up(number_of, total, reach, slope), jnp.int32)
    twos = (number_of - 1) // 2
    giver, taker = sizes[1:1 + 2 * twos:2], sizes[2:2 + 2 * twos:2]
    room = jnp.minimum(giver - 1, reach - taker)
    passed = jax.random.randint(jax.random.fold_in(own_key, 1), (twos,), 0, 1 << 20) % (room + 1)
    sizes = sizes.at[1:1 + 2 * twos:2].set(giver - passed).at[2:2 + 2 * twos:2].set(taker + passed)
    return sizes[jax.random.permutation(jax.random.fold_in(own_key, 2), number_of)]


def gaussian(own_key, dims, scale, limit, cuts=(), held_as=jnp.bfloat16):
    loudness = level_of(own_key, dims, cuts, -0.22, 0.18) if cuts else 1.0
    entries = jax.random.normal(own_key, dims, jnp.float32) * scale * loudness
    return jnp.minimum(jnp.maximum(entries, -limit), limit).astype(held_as)


def setup_inputs(seed: int = 0) -> dict:
    key_of = jax.random.split(jax.random.key(seed), 9)
    return {
        "item_table": gaussian(key_of[0], (ROWS, D), 1.0, 6.0, ((0, 128),)),
        "item_ids": draw_item_ids(jax.random.fold_in(key_of[8], 71), 0),
        "segment_ids": jax.vmap(lambda own: jnp.searchsorted(jnp.cumsum(uneven_parts(own, 3, LEN, LEN // 2, 0)), jnp.arange(LEN), side="right"))(jax.random.split(key_of[2], USERS)).reshape((USERS, LEN)).astype(jnp.int32),
        "weight_in": gaussian(key_of[3], (D, 4 * D), D ** -0.5, 0.25),
        "weight_out": gaussian(key_of[4], (D, D), D ** -0.5, 0.25),
        "gain_in": jnp.clip(1.0 + 0.1 * jax.random.normal(key_of[5], (D,), jnp.float32), 0.5, 1.5),
        "gain_mid": jnp.clip(1.0 + 0.1 * jax.random.normal(key_of[6], (D,), jnp.float32), 0.5, 1.5),
        "cotangent": gaussian(key_of[7], (USERS, LEN, D), 1.0, 6.0, ((0, 16), (1, 8))),
    }


epsilon = 1e-05

def normalize(values):
    centred = values - lax.optimization_barrier(jnp.mean(values, axis=-1, keepdims=True))
    inverse = lax.rsqrt(lax.optimization_barrier(jnp.mean(centred * centred, axis=-1, keepdims=True)) + epsilon)
    return (centred * inverse, inverse)

def norm_back(grad_hat, normed, inverse):
    return inverse * (grad_hat - lax.optimization_barrier(jnp.mean(grad_hat, axis=-1, keepdims=True)) - normed * lax.optimization_barrier(jnp.mean(grad_hat * normed, axis=-1, keepdims=True)))

def silu_slope(values):
    sigma = jax.nn.sigmoid(values)
    return sigma * (1.0 + values * (1.0 - sigma))

def split_heads(matrix):
    return matrix.reshape(matrix.shape[0], HEADS, HEAD_DIM).transpose(1, 0, 2)

def join_heads(stacked):
    return stacked.transpose(1, 0, 2).reshape(stacked.shape[1], HEADS * HEAD_DIM)

def head_scores(query, keys, visible):
    scores = jnp.dot(query, keys.T, preferred_element_type=jnp.float32) * HEAD_DIM ** (-0.5)
    weights = jnp.where(visible, jax.nn.silu(scores), 0.0).astype(jnp.bfloat16)
    return (scores, weights)

def score_grads(scores, upstream, values, visible):
    dweights = jnp.dot(upstream, values.T, preferred_element_type=jnp.float32)
    return (jnp.where(visible, dweights * silu_slope(scores), 0.0) * HEAD_DIM ** (-0.5)).astype(jnp.bfloat16)

def reference(item_table, item_ids, segment_ids, weight_in, weight_out, gain_in, gain_mid, cotangent):
    width = weight_out.shape[0]

    def one_user(operands):
        user_ids, user_segments, upstream = operands
        length = user_ids.shape[0]
        fetched = item_table[user_ids]
        fetched_f = fetched.astype(jnp.float32)
        normed_in, inverse_in = normalize(fetched_f)
        normed_b = (normed_in * gain_in).astype(jnp.bfloat16)
        hidden_pre = jnp.dot(normed_b, weight_in, preferred_element_type=jnp.float32)
        hidden = jax.nn.silu(hidden_pre)
        gate_part = hidden[:, :width]
        value_b = hidden[:, width:2 * width].astype(jnp.bfloat16)
        query_b = hidden[:, 2 * width:3 * width].astype(jnp.bfloat16)
        key_b = hidden[:, 3 * width:].astype(jnp.bfloat16)
        position = jnp.arange(length, dtype=jnp.int32)
        visible = (position[None, :] <= position[:, None]) & (user_segments[None, :] == user_segments[:, None])

        def forward_head(triple):
            head_query, head_key, head_value = triple
            scores, weights = head_scores(head_query, head_key, visible)
            return jnp.dot(weights, head_value, preferred_element_type=jnp.float32)
        mixed = join_heads(lax.map(forward_head, (split_heads(query_b), split_heads(key_b), split_heads(value_b))))
        normed_mid, inverse_mid = normalize(mixed)
        scaled_mid = normed_mid * gain_mid
        gated = (scaled_mid * gate_part).astype(jnp.bfloat16)
        layer = (fetched_f + jnp.dot(gated, weight_out, preferred_element_type=jnp.float32)).astype(jnp.bfloat16)
        grad_wout = jnp.dot(gated.T, upstream, preferred_element_type=jnp.float32)
        grad_gated = jnp.dot(upstream, weight_out.T, preferred_element_type=jnp.float32)
        grad_gate = grad_gated * scaled_mid
        grad_mixed = norm_back(grad_gated * gate_part * gain_mid, normed_mid, inverse_mid).astype(jnp.bfloat16)

        def backward_head(quad):
            head_query, head_key, head_value, head_up = quad
            scores, weights = head_scores(head_query, head_key, visible)
            dscores = score_grads(scores, head_up, head_value, visible)
            grad_q = jnp.dot(dscores, head_key, preferred_element_type=jnp.float32)
            grad_k = jnp.dot(dscores.T, head_query, preferred_element_type=jnp.float32)
            grad_v = jnp.dot(weights.T, head_up, preferred_element_type=jnp.float32)
            return (grad_q, grad_k, grad_v)
        stacked_q, stacked_k, stacked_v = lax.map(backward_head, (split_heads(query_b), split_heads(key_b), split_heads(value_b), split_heads(grad_mixed)))
        grad_hidden = jnp.concatenate([grad_gate, join_heads(stacked_v), join_heads(stacked_q), join_heads(stacked_k)], axis=1)
        grad_pre = (grad_hidden * silu_slope(hidden_pre)).astype(jnp.bfloat16)
        grad_win = jnp.dot(normed_b.T, grad_pre, preferred_element_type=jnp.float32)
        grad_normed = jnp.dot(grad_pre, weight_in.T, preferred_element_type=jnp.float32)
        grad_rows = norm_back(grad_normed * gain_in, normed_in, inverse_in) + upstream.astype(jnp.float32)
        return (layer, grad_rows, grad_win, grad_wout)
    layer_out, grad_rows, grad_win, grad_wout = lax.map(one_user, (item_ids, segment_ids, cotangent))
    table_grad = jnp.zeros(item_table.shape, jnp.float32).at[item_ids.reshape(-1)].add(grad_rows.reshape(-1, grad_rows.shape[-1]))
    return (layer_out, table_grad, lax.optimization_barrier(jnp.sum(grad_win, axis=0)), lax.optimization_barrier(jnp.sum(grad_wout, axis=0)))
```

```python
import functools
import jax
import jax.numpy as jnp
from jax import lax
from jax.experimental import pallas as pl
from jax.experimental.pallas import tpu as pltpu
from jax.sharding import PartitionSpec as P

HEADS = 8
HEAD_DIM = 64
SLOTS = 8
CAP = 6
BLOCK = 512
EPSILON = 1e-05
BOTH = ("users", "seq")
ORDER = (0, 2, 1, 3)

f32 = jnp.float32
bf16 = jnp.bfloat16
i32 = jnp.int32


def iota(shape, dim):
    return lax.broadcasted_iota(i32, shape, dim)


def mm(a, b):
    return jnp.dot(a, b, preferred_element_type=f32)


def mm_nt(a, b):
    return lax.dot_general(a, b, (((1,), (1,)), ((), ())), preferred_element_type=f32)


def call(kernel, out_shape, args, *, name, grid=None, in_specs=None, out_specs=None, scratch=(), flops=0, moved=0):
    params = dict(vmem_limit_bytes=60 * 1024 * 1024)
    extra = {}
    if grid is not None:
        params["dimension_semantics"] = ("arbitrary",) * len(grid)
        extra["grid"] = grid
    if in_specs is not None:
        extra["in_specs"] = in_specs
    if out_specs is not None:
        extra["out_specs"] = out_specs
    return pl.pallas_call(
        kernel,
        out_shape=out_shape,
        scratch_shapes=scratch,
        name=name,
        compiler_params=pltpu.CompilerParams(**params),
        cost_estimate=pl.CostEstimate(flops=flops, bytes_accessed=moved, transcendentals=0),
        **extra,
    )(*args)


def normalize(values):
    centred = values - jnp.mean(values, axis=-1, keepdims=True)
    inverse = lax.rsqrt(jnp.mean(centred * centred, axis=-1, keepdims=True) + EPSILON)
    return centred * inverse, inverse


def slots_kernel(shard_rows, ids_ref, seg_ref, wanted_ref, row_ref, col_ref):
    devices, lanes = wanted_ref.shape
    count = ids_ref.shape[1]
    ids = ids_ref[...]
    owner = lax.shift_right_logical(ids, shard_rows.bit_length() - 1)
    local = (ids & (shard_rows - 1)).astype(f32)
    held = owner == iota((devices, count), 0)
    hit = jnp.where(held, 1.0, 0.0)
    earlier = jnp.where(iota((count, count), 0) < iota((count, count), 1), 1.0, 0.0)
    rank = mm(hit.astype(bf16), earlier.astype(bf16))
    marked = jnp.where(held, rank, -1.0)
    lane = iota((devices, lanes), 1)
    wanted = jnp.zeros((devices, lanes), f32)
    for c in range(CAP):
        column = jnp.sum(jnp.where(marked == float(c), local, 0.0), axis=1, keepdims=True)
        wanted = jnp.where(lane == c, column, wanted)
    seg = seg_ref[...]
    below1 = jnp.sum(jnp.where(seg < 1, 1.0, 0.0), axis=1, keepdims=True)
    below2 = jnp.sum(jnp.where(seg < 2, 1.0, 0.0), axis=1, keepdims=True)
    wanted = jnp.where(lane == CAP, below1, wanted)
    wanted = jnp.where(lane == CAP + 1, below2, wanted)
    wanted_ref[...] = wanted.astype(i32)
    slot = owner.astype(f32) * float(SLOTS) + jnp.sum(hit * rank, axis=0, keepdims=True)
    row_ref[...] = jnp.broadcast_to(slot, row_ref.shape).astype(i32)
    col_ref[...] = jnp.transpose(jnp.broadcast_to(slot, (lanes, count))).astype(i32)


def serve_kernel(asked_ref, table_ref, served_ref, row_ref, bounds_ref, col_ref):
    step = pl.program_id(0)
    block = served_ref.shape[0]
    devices, lanes = asked_ref.shape

    @pl.when(step == 0)
    def _():
        asked = asked_ref[...].astype(f32)
        wide = jnp.broadcast_to(asked[:, None, :], (devices, SLOTS, lanes))
        sub = iota((devices, SLOTS, lanes), 1)
        lane = iota((devices, SLOTS, lanes), 2)
        column = jnp.sum(jnp.where(sub == lane, wide, 0.0), axis=2, keepdims=True)
        column = jnp.where(iota((devices, SLOTS, 1), 1) < CAP, column, -1.0)
        column = jnp.broadcast_to(column, (devices, SLOTS, lanes)).reshape(devices * SLOTS, lanes)
        col_ref[...] = column
        row_ref[...] = jnp.transpose(column)[: row_ref.shape[0]].astype(i32)
        group = lax.axis_index("users")
        mine = lax.div(iota((devices, lanes), 0), SLOTS) == group
        bounds = jnp.sum(jnp.where(mine, asked, 0.0), axis=0, keepdims=True)
        bounds_ref[...] = jnp.broadcast_to(bounds, bounds_ref.shape).astype(i32)

    column = col_ref[pl.ds(pl.multiple_of(step * block, block), block), :].astype(i32)
    parts = []
    for at in range(table_ref.shape[0] // lanes):
        parts.append(jnp.where(column == iota((block, lanes), 1) + at * lanes, 1.0, 0.0).astype(bf16))
    served_ref[...] = mm(jnp.concatenate(parts, axis=1), table_ref[...]).astype(bf16)


def arrange_kernel(got_ref, col_ref, gain_ref, fetched_ref, xin_ref):
    slot = col_ref[...]
    count, lanes = slot.shape
    parts = []
    for at in range(got_ref.shape[0] // lanes):
        parts.append(jnp.where(slot == iota((count, lanes), 1) + at * lanes, 1.0, 0.0).astype(bf16))
    fetched = mm(jnp.concatenate(parts, axis=1), got_ref[...])
    fetched_ref[...] = fetched.astype(bf16)
    normed, _ = normalize(fetched)
    xin_ref[...] = (normed * gain_ref[...]).astype(bf16)


def seg_start(position, one, two):
    return jnp.where(position < one, 0, jnp.where(position < two, one, two))


def visible(i, j, one, two):
    where_q = iota((1, BLOCK), 1) + i * BLOCK
    start = seg_start(where_q, one, two)
    where_k = iota((BLOCK, BLOCK), 0) + j * BLOCK
    return (where_k >= start) & (where_k <= where_q)


def forward_kernel(
    xin_ref, cot_ref, win_ref, wout_ref, gain_ref, bounds_ref,
    q_ref, k_ref, vk_ref, slope_ref, u_ref, dg_ref, mixed_ref, stats_ref,
    q_all, v_all, vk_all,
):
    i = pl.program_id(0)
    one, two = bounds_ref[0, CAP], bounds_ref[0, CAP + 1]
    here = pl.ds(pl.multiple_of(i * BLOCK, BLOCK), BLOCK)
    pre = mm_nt(win_ref[...], xin_ref[...])
    tanh = jnp.tanh(pre * 0.5)
    plus = 1.0 + tanh
    hidden = (0.5 * pre) * plus
    slope_ref[...] = 0.5 * (plus + hidden * (1.0 - tanh))
    d = HEAD_DIM
    u = hidden[:d]
    query = (hidden[d : 2 * d].astype(bf16).astype(f32) * 0.0625).astype(bf16)
    vk = hidden[2 * d :]
    vk_t = vk.astype(bf16)
    turned = jnp.transpose(vk).astype(bf16)
    u_ref[...] = u
    q_ref[...] = query
    k_ref[...] = vk_t[d:]
    vk_ref[...] = turned
    q_all[:d, :] = jnp.zeros((d, BLOCK), bf16)
    q_all[d:, :] = query
    v_all[:, here] = vk_t[:d]
    vk_all[here, :] = turned
    mixed_ref[...] = jnp.zeros(mixed_ref.shape, f32)

    def pair(j, carry):
        there = pl.ds(pl.multiple_of(j * BLOCK, BLOCK), BLOCK)
        half = mm(vk_all[there, :], q_all[...])
        weights = half + half * jnp.tanh(half)
        weights = jnp.where(visible(i, j, one, two), weights, 0.0).astype(bf16)
        mixed_ref[...] += mm(v_all[:, there], weights)
        return carry

    first = lax.div(seg_start(i * BLOCK, one, two), BLOCK)
    lax.fori_loop(first, i + 1, pair, 0)
    dg = mm_nt(wout_ref[...], cot_ref[...])
    dg_ref[...] = dg
    mixed = mixed_ref[...]
    e = dg * u * gain_ref[:, :1]
    mean = jnp.sum(mixed, axis=0, keepdims=True) * (1.0 / d)
    centred = mixed - mean
    stats_ref[0:1, :] = mean
    stats_ref[1:2, :] = jnp.sum(centred * centred, axis=0, keepdims=True)
    stats_ref[2:3, :] = jnp.sum(e, axis=0, keepdims=True)
    stats_ref[3:4, :] = jnp.sum(e * centred, axis=0, keepdims=True)


def middle_kernel(stats_ref, mixed_ref, dg_ref, u_ref, slope_ref, gain_ref, gated_ref, dm_ref, dpre_ref):
    width = HEADS * HEAD_DIM
    stats = stats_ref[...]
    means = [stats[h, 0:1] for h in range(HEADS)]
    mean = functools.reduce(jnp.add, means) * (1.0 / HEADS)
    var, m_e, m_em = 0.0, 0.0, 0.0
    for h in range(HEADS):
        off = means[h] - mean
        var = var + stats[h, 1:2] + HEAD_DIM * off * off
        m_e = m_e + stats[h, 2:3]
        m_em = m_em + stats[h, 3:4] + off * stats[h, 2:3]
    inverse = lax.rsqrt(var * (1.0 / width) + EPSILON)
    m_e = m_e * (1.0 / width)
    m_eh = m_em * inverse * (1.0 / width)
    gain = gain_ref[:, :1]
    hat = (mixed_ref[...] - mean) * inverse
    scaled = hat * gain
    u = u_ref[...]
    dg = dg_ref[...]
    gated_ref[0] = (scaled * u).astype(bf16)
    e = dg * u * gain
    dm = (inverse * (e - m_e - hat * m_eh)).astype(bf16)
    dm_ref[...] = (dm.astype(f32) * 0.0625).astype(bf16)
    dpre_ref[0] = (dg * scaled * slope_ref[...]).astype(bf16)


def backward_kernel(
    steps, q_ref, k_ref, vk_ref, dm_ref, bounds_ref, xin_ref, cot_ref, slope_ref, gated_ref, dpu_ref,
    dpre_ref, dw_ref, dq_all, dk_all, dv_all, win_acc, wout_acc,
):
    g = pl.program_id(0)
    one, two = bounds_ref[0, CAP], bounds_ref[0, CAP + 1]
    d = HEAD_DIM

    @pl.when(g == 0)
    def _():
        dk_all[...] = jnp.zeros(dk_all.shape, f32)
        dv_all[...] = jnp.zeros(dv_all.shape, f32)
        dq_all[...] = jnp.zeros(dq_all.shape, f32)
        win_acc[...] = jnp.zeros(win_acc.shape, f32)
        wout_acc[...] = jnp.zeros(wout_acc.shape, f32)

    @pl.when(g < steps)
    def _():
        here = pl.ds(pl.multiple_of(g * BLOCK, BLOCK), BLOCK)
        blank = jnp.zeros((d, BLOCK), bf16)
        query = q_ref[:, here]
        up = dm_ref[:, here]
        query2 = jnp.concatenate([blank, query], axis=0)
        up2 = jnp.concatenate([up, blank], axis=0)

        def pair(j, carry):
            there = pl.ds(pl.multiple_of(j * BLOCK, BLOCK), BLOCK)
            vk = vk_ref[there, :]
            half = mm(vk, query2)
            upper = mm(vk, up2)
            tanh = jnp.tanh(half)
            plus = 1.0 + tanh
            weights = half * plus
            dscores = upper * (plus + weights * (1.0 - tanh))
            seen = visible(g, j, one, two)
            weights = jnp.where(seen, weights, 0.0).astype(bf16)
            dscores = jnp.where(seen, dscores, 0.0).astype(bf16)
            dv_all[:, there] += mm_nt(up, weights)
            dk_all[:, there] += mm_nt(query, dscores)
            dq_all[:, here] += mm(k_ref[:, there], dscores)
            return carry

        first = lax.div(seg_start(g * BLOCK, one, two), BLOCK)
        lax.fori_loop(first, g + 1, pair, 0)

    @pl.when(g >= steps)
    def _():
        s = g - steps
        count = xin_ref.shape[0]
        here = pl.ds(pl.multiple_of(s * count, count), count)
        slope = slope_ref[...]
        dpre = jnp.concatenate(
            [
                dpu_ref[0],
                (dq_all[:, here] * slope[d : 2 * d]).astype(bf16),
                (dv_all[:, here] * 16.0 * slope[2 * d : 3 * d]).astype(bf16),
                (dk_all[:, here] * 16.0 * slope[3 * d :]).astype(bf16),
            ],
            axis=0,
        )
        dpre_ref[0] = dpre
        win_acc[...] += mm(dpre, xin_ref[...])
        wout_acc[...] += mm(gated_ref[0], cot_ref[...])

    @pl.when(g == pl.num_programs(0) - 1)
    def _():
        parts = dw_ref.shape[0]
        turned = jnp.transpose(win_acc[...])
        rows = turned.shape[0] // parts
        for p in range(parts):
            dw_ref[p, :rows, :] = turned[p * rows : (p + 1) * rows]
            dw_ref[p, rows:, :] = wout_acc[8 * (p // 2) : 8 * (p // 2) + 8, 256 * (p % 2) : 256 * (p % 2) + 256]


def rows_kernel(dpre_ref, win_ref, gain_ref, fetched_ref, cot_ref, row_ref, out_ref, whole):
    d = HEAD_DIM
    width = fetched_ref.shape[1]
    for h in range(HEADS):
        for at, block in enumerate(ORDER):
            whole[block * width + h * d : block * width + (h + 1) * d, :] = dpre_ref[h, at * d : (at + 1) * d, :]
    dxin = jnp.transpose(mm(win_ref[...], whole[...]))
    normed, inverse = normalize(fetched_ref[...].astype(f32))
    f = dxin * gain_ref[...]
    drow = inverse * (
        f - jnp.mean(f, axis=-1, keepdims=True) - normed * jnp.mean(f * normed, axis=-1, keepdims=True)
    ) + cot_ref[...].astype(f32)
    drow = drow.astype(bf16)
    slots = out_ref.shape[0]
    count = drow.shape[0]
    pick = jnp.where(row_ref[0:1, :] == iota((slots, count), 0), 1.0, 0.0).astype(bf16)
    out_ref[...] = mm(pick, drow).astype(bf16)


def table_kernel(row_ref, got_ref, out_ref):
    block = out_ref.shape[0]
    slots = got_ref.shape[0]
    at = pl.program_id(0) * block
    pick = jnp.where(row_ref[0:1, :] == iota((block, slots), 0) + at, 1.0, 0.0).astype(bf16)
    out_ref[...] = mm(pick, got_ref[...])


def weights_kernel(got_ref, win_ref, wout_ref):
    d = HEAD_DIM
    rows, columns = win_ref.shape
    width = columns // 4
    for at, block in enumerate(ORDER):
        for pair in range(HEADS // 2):
            left = got_ref[0, 2 * pair, :rows, at * d : (at + 1) * d]
            right = got_ref[0, 2 * pair + 1, :rows, at * d : (at + 1) * d]
            start = block * width + pair * 2 * d
            win_ref[:, start : start + 2 * d] = jnp.concatenate([left, right], axis=1)
    for h in range(HEADS):
        wout_ref[h, 0] = got_ref[0, h, rows:, :]


def exchange(x, axis):
    return lax.all_to_all(x, axis, split_axis=0, concat_axis=0, tiled=True)


def struct(shape, dtype):
    return jax.ShapeDtypeStruct(shape, dtype)


def body(item_table, item_ids, segment_ids, weight_in, weight_out, gain_in, gain_mid, cotangent):
    shard_rows, width = item_table.shape
    count = item_ids.shape[1]
    users, seq = lax.axis_size("users"), lax.axis_size("seq")
    devices = users * seq
    length = count * seq
    d = HEAD_DIM
    slots = devices * SLOTS
    upstream = cotangent[0]
    gain_row = gain_in.reshape(1, width)
    head = lax.axis_index("seq")

    cot_all = lax.all_gather(upstream, "seq", axis=0, tiled=True)
    wanted, slot_row, slot_col = call(
        functools.partial(slots_kernel, shard_rows),
        (struct((devices, 128), i32), struct((8, count), i32), struct((count, 128), i32)),
        (item_ids, segment_ids),
        name="slots", flops=2 * devices * count * count, moved=1 << 19,
    )
    asked = exchange(wanted.reshape(devices, 1, 128), BOTH).reshape(devices, 128)
    steps = 4
    whole = lambda *shape: pl.BlockSpec(shape, lambda g: (0,) * len(shape))
    smem = pl.BlockSpec(memory_space=pltpu.SMEM)
    served, asked_row, bounds = call(
        serve_kernel,
        (struct((slots, width), bf16), struct((8, slots), i32), struct((8, 128), i32)),
        (asked, item_table),
        name="serve", grid=(steps,),
        in_specs=[whole(devices, 128), whole(shard_rows, width)],
        out_specs=[pl.BlockSpec((slots // steps, width), lambda g: (g, 0)), whole(8, slots), whole(8, 128)],
        scratch=[pltpu.VMEM((slots, 128), f32)],
        flops=2 * slots * shard_rows * width, moved=4 << 20,
    )
    got = exchange(served.reshape(devices, SLOTS, width), BOTH).reshape(slots, width)
    fetched, xin = call(
        arrange_kernel,
        (struct((count, width), bf16), struct((count, width), bf16)),
        (got, slot_col, gain_row),
        name="arrange", flops=2 * count * slots * width, moved=2 << 20,
    )
    xin_all = lax.all_gather(xin, "seq", axis=0, tiled=True)

    mine = lax.dynamic_index_in_dim(weight_in.reshape(width, 4, HEADS, d), head, 2, keepdims=False)
    win_t = jnp.stack([mine[:, b] for b in ORDER], axis=1).reshape(width, 4 * d).T
    wout_h = lax.dynamic_slice_in_dim(weight_out, head * d, d, axis=0)
    gain_h = jnp.broadcast_to(lax.dynamic_slice_in_dim(gain_mid, head * d, d)[:, None], (d, 128))

    blocks = length // BLOCK
    lane = lambda rows: pl.BlockSpec((rows, BLOCK), lambda g: (0, g))
    rowed = lambda columns: pl.BlockSpec((BLOCK, columns), lambda g: (g, 0))
    q_t, k_t, vk, slope, u, dg, mixed, stats = call(
        forward_kernel,
        (
            struct((d, length), bf16), struct((d, length), bf16), struct((length, 2 * d), bf16),
            struct((4 * d, length), f32), struct((d, length), f32), struct((d, length), f32),
            struct((d, length), f32), struct((4, length), f32),
        ),
        (xin_all, cot_all, win_t, wout_h, gain_h, bounds),
        name="forward", grid=(blocks,),
        in_specs=[rowed(width), rowed(width), whole(4 * d, width), whole(d, width), whole(d, 128), smem],
        out_specs=[lane(d), lane(d), rowed(2 * d), lane(4 * d), lane(d), lane(d), lane(d), lane(4)],
        scratch=[pltpu.VMEM((2 * d, BLOCK), bf16), pltpu.VMEM((d, length), bf16), pltpu.VMEM((length, 2 * d), bf16)],
        flops=1 << 33, moved=12 << 20,
    )
    stats_all = lax.all_gather(stats, "seq", axis=0, tiled=False)

    part = lambda rows: pl.BlockSpec((rows, count), lambda g: (0, g))
    gated, dm, dpre_u = call(
        middle_kernel,
        (struct((seq, d, count), bf16), struct((d, length), bf16), struct((seq, d, count), bf16)),
        (stats_all, mixed, dg, u, slope, gain_h),
        name="middle", grid=(seq,),
        in_specs=[pl.BlockSpec((seq, 4, count), lambda g: (0, 0, g)), part(d), part(d), part(d), part(d), whole(d, 128)],
        out_specs=[
            pl.BlockSpec((1, d, count), lambda g: (g, 0, 0)), part(d), pl.BlockSpec((1, d, count), lambda g: (g, 0, 0)),
        ],
        flops=1 << 24, moved=5 << 20,
    )
    gated_mine = exchange(gated, "seq").reshape(width, count)
    layer = (
        fetched.astype(f32)
        + lax.dot_general(gated_mine, weight_out, (((0,), (0,)), ((), ())), preferred_element_type=f32)
    ).astype(bf16)

    late = lambda g: jnp.maximum(g - blocks, 0)
    dpre, dw = call(
        functools.partial(backward_kernel, blocks),
        (struct((seq, 4 * d, count), bf16), struct((users, width // users + 8, 4 * d), f32)),
        (q_t, k_t, vk, dm, bounds, xin_all, cot_all, slope, gated, dpre_u),
        name="backward", grid=(blocks + seq,),
        in_specs=[
            whole(d, length), whole(d, length), whole(length, 2 * d), whole(d, length), smem,
            pl.BlockSpec((count, width), lambda g: (late(g), 0)),
            pl.BlockSpec((count, width), lambda g: (late(g), 0)),
            pl.BlockSpec((4 * d, count), lambda g: (0, late(g))),
            pl.BlockSpec((1, d, count), lambda g: (late(g), 0, 0)),
            pl.BlockSpec((1, d, count), lambda g: (late(g), 0, 0)),
        ],
        out_specs=[pl.BlockSpec((1, 4 * d, count), lambda g: (late(g), 0, 0)), whole(users, width // users + 8, 4 * d)],
        scratch=[pltpu.VMEM((d, length), f32)] * 3 + [pltpu.VMEM((4 * d, width), f32), pltpu.VMEM((d, width), f32)],
        flops=1 << 35, moved=16 << 20,
    )
    dw_sum = jnp.sum(exchange(dw, "users"), axis=0)
    dw_all = lax.all_gather(dw_sum, BOTH, axis=0, tiled=False)
    dpre_mine = exchange(dpre, "seq")
    outgoing = call(
        rows_kernel,
        struct((slots, width), bf16),
        (dpre_mine, weight_in, gain_row, fetched, upstream, slot_row),
        name="rows", scratch=[pltpu.VMEM((4 * width, count), bf16)],
        flops=2 * count * width * 4 * width, moved=6 << 20,
    )
    incoming = exchange(outgoing.reshape(devices, SLOTS, width), BOTH).reshape(slots, width)
    tiles = 8
    table_grad = call(
        table_kernel,
        struct((shard_rows, width), f32),
        (asked_row, incoming),
        name="table", grid=(tiles,),
        in_specs=[whole(8, slots), whole(slots, width)],
        out_specs=pl.BlockSpec((shard_rows // tiles, width), lambda g: (g, 0)),
        flops=2 * slots * shard_rows * width, moved=6 << 20,
    )
    rows = width // users
    win_grad, wout_grad = call(
        weights_kernel,
        (struct((width, 4 * width), f32), struct((HEADS, width // d, 8, width), f32)),
        (dw_all.reshape(users, seq, rows + 8, 4 * d),),
        name="weights", grid=(users,),
        in_specs=[pl.BlockSpec((1, seq, rows + 8, 4 * d), lambda g: (g, 0, 0, 0))],
        out_specs=[
            pl.BlockSpec((rows, 4 * width), lambda g: (g, 0)),
            pl.BlockSpec((HEADS, 1, 8, width // 2), lambda g: (0, g // 2, 0, g % 2)),
        ],
        flops=1 << 20, moved=11 << 20,
    )
    return (layer[None], table_grad, win_grad, wout_grad.reshape(width, width))


def solution(mesh):
    in_specs = (
        P(BOTH, None),
        P("users", "seq"),
        P("users", "seq"),
        P(),
        P(),
        P(),
        P(),
        P("users", "seq", None),
    )
    out_specs = (P("users", "seq", None), P(BOTH, None), P(), P())
    return jax.shard_map(body, mesh=mesh, in_specs=in_specs, out_specs=out_specs, check_vma=False)
```

```python
import functools
import jax
import jax.numpy as jnp
from jax import lax
from jax.experimental import pallas as pl
from jax.experimental.pallas import tpu as pltpu
from jax.sharding import PartitionSpec as P


HEADS = 8
HEAD_DIM = 64
SLOTS = 8
CAP = 6
BLOCK = 512
EPSILON = 1e-05
BOTH = ("users", "seq")
ORDER = (0, 2, 1, 3)

f32 = jnp.float32
bf16 = jnp.bfloat16
i32 = jnp.int32


def iota(shape, dim):
    return lax.broadcasted_iota(i32, shape, dim)


def mm(a, b):
    return jnp.dot(a, b, preferred_element_type=f32)


def mm_nt(a, b):
    return lax.dot_general(a, b, (((1,), (1,)), ((), ())), preferred_element_type=f32)


def call(kernel, out_shape, args, *, grid=None, in_specs=None, out_specs=None, scratch=(), flops=0, moved=0):
    params = dict(vmem_limit_bytes=60 * 1024 * 1024)
    extra = {}
    if grid is not None:
        params["dimension_semantics"] = ("arbitrary",) * len(grid)
        extra["grid"] = grid
    if in_specs is not None:
        extra["in_specs"] = in_specs
    if out_specs is not None:
        extra["out_specs"] = out_specs
    return pl.pallas_call(
        kernel,
        out_shape=out_shape,
        scratch_shapes=scratch,
        compiler_params=pltpu.CompilerParams(**params),
        cost_estimate=pl.CostEstimate(flops=flops, bytes_accessed=moved, transcendentals=0),
        **extra,
    )(*args)


def normalize(values):
    centred = values - jnp.mean(values, axis=-1, keepdims=True)
    inverse = lax.rsqrt(jnp.mean(centred * centred, axis=-1, keepdims=True) + EPSILON)
    return centred * inverse, inverse


def slots_kernel(shard_rows, ids_ref, seg_ref, wanted_ref, row_ref, col_ref):
    devices, lanes = wanted_ref.shape
    count = ids_ref.shape[1]
    ids = ids_ref[...]
    owner = lax.shift_right_logical(ids, shard_rows.bit_length() - 1)
    local = (ids & (shard_rows - 1)).astype(f32)
    held = owner == iota((devices, count), 0)
    hit = jnp.where(held, 1.0, 0.0)
    earlier = jnp.where(iota((count, count), 0) < iota((count, count), 1), 1.0, 0.0)
    rank = mm(hit.astype(bf16), earlier.astype(bf16))
    marked = jnp.where(held, rank, -1.0)
    lane = iota((devices, lanes), 1)
    wanted = jnp.zeros((devices, lanes), f32)
    for c in range(CAP):
        column = jnp.sum(jnp.where(marked == float(c), local, 0.0), axis=1, keepdims=True)
        wanted = jnp.where(lane == c, column, wanted)
    seg = seg_ref[...]
    below1 = jnp.sum(jnp.where(seg < 1, 1.0, 0.0), axis=1, keepdims=True)
    below2 = jnp.sum(jnp.where(seg < 2, 1.0, 0.0), axis=1, keepdims=True)
    wanted = jnp.where(lane == CAP, below1, wanted)
    wanted = jnp.where(lane == CAP + 1, below2, wanted)
    wanted_ref[...] = wanted.astype(i32)
    slot = owner.astype(f32) * float(SLOTS) + jnp.sum(hit * rank, axis=0, keepdims=True)
    row_ref[...] = jnp.broadcast_to(slot, row_ref.shape).astype(i32)
    col_ref[...] = jnp.transpose(jnp.broadcast_to(slot, (lanes, count))).astype(i32)


def serve_kernel(asked_ref, table_ref, served_ref, row_ref, bounds_ref, col_ref):
    step = pl.program_id(0)
    block = served_ref.shape[0]
    devices, lanes = asked_ref.shape

    @pl.when(step == 0)
    def _():
        asked = asked_ref[...].astype(f32)
        wide = jnp.broadcast_to(asked[:, None, :], (devices, SLOTS, lanes))
        sub = iota((devices, SLOTS, lanes), 1)
        lane = iota((devices, SLOTS, lanes), 2)
        column = jnp.sum(jnp.where(sub == lane, wide, 0.0), axis=2, keepdims=True)
        column = jnp.where(iota((devices, SLOTS, 1), 1) < CAP, column, -1.0)
        column = jnp.broadcast_to(column, (devices, SLOTS, lanes)).reshape(devices * SLOTS, lanes)
        col_ref[...] = column
        row_ref[...] = jnp.transpose(column)[: row_ref.shape[0]].astype(i32)
        group = lax.axis_index("users")
        mine = lax.div(iota((devices, lanes), 0), SLOTS) == group
        bounds = jnp.sum(jnp.where(mine, asked, 0.0), axis=0, keepdims=True)
        bounds = jnp.broadcast_to(bounds, bounds_ref.shape).astype(i32)
        bounds_ref[...] = jnp.where(iota(bounds_ref.shape, 1) == SLOTS, lax.axis_index("seq"), bounds)

    column = col_ref[pl.ds(pl.multiple_of(step * block, block), block), :].astype(i32)
    parts = []
    for at in range(table_ref.shape[0] // lanes):
        parts.append(jnp.where(column == iota((block, lanes), 1) + at * lanes, 1.0, 0.0).astype(bf16))
    served_ref[...] = mm(jnp.concatenate(parts, axis=1), table_ref[...]).astype(bf16)


def arrange_kernel(got_ref, col_ref, gain_ref, fetched_ref, xin_ref):
    slot = col_ref[...]
    count, lanes = slot.shape
    parts = []
    for at in range(got_ref.shape[0] // lanes):
        parts.append(jnp.where(slot == iota((count, lanes), 1) + at * lanes, 1.0, 0.0).astype(bf16))
    fetched = mm(jnp.concatenate(parts, axis=1), got_ref[...])
    fetched_ref[...] = fetched.astype(bf16)
    normed, _ = normalize(fetched)
    xin_ref[...] = (normed * gain_ref[...]).astype(bf16)


def seg_start(position, one, two):
    return jnp.where(position < one, 0, jnp.where(position < two, one, two))


def visible(i, j, one, two):
    where_q = iota((1, BLOCK), 1) + i * BLOCK
    start = seg_start(where_q, one, two)
    where_k = iota((BLOCK, BLOCK), 0) + j * BLOCK
    return (where_k >= start) & (where_k <= where_q)


def forward_kernel(
    xin_ref, cot_ref, win_ref, wout_ref, gain_ref, bounds_ref,
    q_ref, k_ref, vk_ref, slope_ref, u_ref, dg_ref, mixed_ref, stats_ref,
    q_all, v_all, vk_all,
):
    i = pl.program_id(0)
    one, two = bounds_ref[0, CAP], bounds_ref[0, CAP + 1]
    here = pl.ds(pl.multiple_of(i * BLOCK, BLOCK), BLOCK)
    pre = mm_nt(win_ref[...], xin_ref[...])
    tanh = jnp.tanh(pre * 0.5)
    plus = 1.0 + tanh
    hidden = (0.5 * pre) * plus
    slope_ref[...] = 0.5 * (plus + hidden * (1.0 - tanh))
    d = HEAD_DIM
    u = hidden[:d]
    query = (hidden[d : 2 * d].astype(bf16).astype(f32) * 0.0625).astype(bf16)
    vk = hidden[2 * d :]
    vk_t = vk.astype(bf16)
    turned = jnp.transpose(vk).astype(bf16)
    u_ref[...] = u
    q_ref[...] = query
    k_ref[...] = vk_t[d:]
    vk_ref[...] = turned
    q_all[:d, :] = jnp.zeros((d, BLOCK), bf16)
    q_all[d:, :] = query
    v_all[:, here] = vk_t[:d]
    vk_all[here, :] = turned
    mixed_ref[...] = jnp.zeros(mixed_ref.shape, f32)

    def pair(j, carry):
        there = pl.ds(pl.multiple_of(j * BLOCK, BLOCK), BLOCK)
        half = mm(vk_all[there, :], q_all[...])
        weights = half + half * jnp.tanh(half)
        weights = jnp.where(visible(i, j, one, two), weights, 0.0).astype(bf16)
        mixed_ref[...] += mm(v_all[:, there], weights)
        return carry

    first = lax.div(seg_start(i * BLOCK, one, two), BLOCK)
    lax.fori_loop(first, i + 1, pair, 0)
    dg = mm_nt(wout_ref[...], cot_ref[...])
    dg_ref[...] = dg
    mixed = mixed_ref[...]
    e = dg * u * gain_ref[:, :1]
    mean = jnp.sum(mixed, axis=0, keepdims=True) * (1.0 / d)
    centred = mixed - mean
    stats_ref[0:1, :] = mean
    stats_ref[1:2, :] = jnp.sum(centred * centred, axis=0, keepdims=True)
    stats_ref[2:3, :] = jnp.sum(e, axis=0, keepdims=True)
    stats_ref[3:4, :] = jnp.sum(e * centred, axis=0, keepdims=True)


def middle(stats, mixed, dg, u, gain):
    width = HEADS * HEAD_DIM
    means = [stats[h, 0:1] for h in range(HEADS)]
    mean = functools.reduce(jnp.add, means) * (1.0 / HEADS)
    var, m_e, m_em = 0.0, 0.0, 0.0
    for h in range(HEADS):
        off = means[h] - mean
        var = var + stats[h, 1:2] + HEAD_DIM * off * off
        m_e = m_e + stats[h, 2:3]
        m_em = m_em + stats[h, 3:4] + off * stats[h, 2:3]
    inverse = lax.rsqrt(var * (1.0 / width) + EPSILON)
    m_e = m_e * (1.0 / width)
    m_eh = m_em * inverse * (1.0 / width)
    hat = (mixed - mean) * inverse
    scaled = hat * gain
    e = dg * u * gain
    up = (inverse * (e - m_e - hat * m_eh)).astype(bf16)
    return (scaled * u).astype(bf16), (up.astype(f32) * 0.0625).astype(bf16), dg * scaled


def backward_kernel(
    steps, bounds_ref, q_ref, k_ref, vk_ref, stats_ref, mixed_ref, dg_ref, u_ref, gain_ref, xin_ref, cot_ref, slope_ref,
    *rest,
):
    outs, (dw_ref, k_all, vk_all, gated_all, du_all, dq_all, dk_all, dv_all, win_acc, wout_acc, sent, sems) = (
        rest[:HEADS],
        rest[HEADS:],
    )
    g = pl.program_id(0)
    one, two, me = bounds_ref[0, CAP], bounds_ref[0, CAP + 1], bounds_ref[0, SLOTS]
    d = HEAD_DIM

    @pl.when(g == 0)
    def _():
        dk_all[...] = jnp.zeros(dk_all.shape, f32)
        dv_all[...] = jnp.zeros(dv_all.shape, f32)
        dq_all[...] = jnp.zeros(dq_all.shape, f32)
        win_acc[...] = jnp.zeros(win_acc.shape, f32)
        wout_acc[...] = jnp.zeros(wout_acc.shape, f32)

    @pl.when(g < steps)
    def _():
        here = pl.ds(pl.multiple_of(g * BLOCK, BLOCK), BLOCK)
        blank = jnp.zeros((d, BLOCK), bf16)
        gated, up, du = middle(stats_ref[...], mixed_ref[...], dg_ref[...], u_ref[...], gain_ref[:, :1])
        gated_all[:, here] = gated
        du_all[:, here] = du
        k_all[:, here] = k_ref[...]
        vk_all[here, :] = vk_ref[...]
        query = q_ref[...]
        query2 = jnp.concatenate([blank, query], axis=0)
        up2 = jnp.concatenate([up, blank], axis=0)

        def pair(j, carry):
            there = pl.ds(pl.multiple_of(j * BLOCK, BLOCK), BLOCK)
            vk = vk_all[there, :]
            half = mm(vk, query2)
            upper = mm(vk, up2)
            tanh = jnp.tanh(half)
            plus = 1.0 + tanh
            weights = half * plus
            dscores = upper * (plus + weights * (1.0 - tanh))
            seen = visible(g, j, one, two)
            weights = jnp.where(seen, weights, 0.0).astype(bf16)
            dscores = jnp.where(seen, dscores, 0.0).astype(bf16)
            dv_all[:, there] += mm_nt(up, weights)
            dk_all[:, there] += mm_nt(query, dscores)
            dq_all[:, here] += mm(k_all[:, there], dscores)
            return carry

        first = lax.div(seg_start(g * BLOCK, one, two), BLOCK)
        lax.fori_loop(first, g + 1, pair, 0)

    @pl.when(g >= steps)
    def _():
        s = g - steps
        count = xin_ref.shape[0]
        here = pl.ds(pl.multiple_of(lax.rem(me + s, HEADS) * count, 128), count)
        slope = slope_ref[...]
        gated = gated_all[:, here]
        dpre = jnp.concatenate(
            [
                (du_all[:, here] * slope[:d]).astype(bf16),
                (dq_all[:, here] * slope[d : 2 * d]).astype(bf16),
                (dv_all[:, here] * 16.0 * slope[2 * d : 3 * d]).astype(bf16),
                (dk_all[:, here] * 16.0 * slope[3 * d :]).astype(bf16),
            ],
            axis=0,
        )
        sent[s, : 4 * d, :] = dpre
        sent[s, 4 * d :, :] = gated
        for at in range(HEADS):

            @pl.when(s == at)
            def _():
                pltpu.make_async_copy(sent.at[at], outs[at], sems.at[at]).start()

        win_acc[...] += mm(dpre, xin_ref[...])
        wout_acc[...] += mm(gated, cot_ref[...])

    @pl.when(g == pl.num_programs(0) - 1)
    def _():
        parts = dw_ref.shape[0]
        turned = jnp.transpose(win_acc[...])
        rows = turned.shape[0] // parts
        for p in range(parts):
            dw_ref[p, :rows, :] = turned[p * rows : (p + 1) * rows]
            dw_ref[p, rows:, :] = wout_acc[8 * (p // 2) : 8 * (p // 2) + 8, 256 * (p % 2) : 256 * (p % 2) + 256]
        for at in range(HEADS):
            pltpu.make_async_copy(sent.at[at], outs[at], sems.at[at]).wait()


def rows_kernel(*refs):
    got = refs[:HEADS]
    win_ref, gain_ref, fetched_ref, cot_ref, row_ref, out_ref, gated_ref, whole = refs[HEADS:]
    d = HEAD_DIM
    width = fetched_ref.shape[1]
    me = lax.axis_index("seq")
    for s in range(HEADS):
        at_head = pl.multiple_of(lax.rem(me + HEADS - s, HEADS) * d, d)
        for at, block in enumerate(ORDER):
            whole[pl.ds(block * width + at_head, d), :] = got[s][at * d : (at + 1) * d, :]
        gated_ref[pl.ds(at_head, d), :] = got[s][4 * d :, :]
    dxin = jnp.transpose(mm(win_ref[...], whole[...]))
    normed, inverse = normalize(fetched_ref[...].astype(f32))
    f = dxin * gain_ref[...]
    drow = inverse * (
        f - jnp.mean(f, axis=-1, keepdims=True) - normed * jnp.mean(f * normed, axis=-1, keepdims=True)
    ) + cot_ref[...].astype(f32)
    drow = drow.astype(bf16)
    slots = out_ref.shape[0]
    count = drow.shape[0]
    pick = jnp.where(row_ref[0:1, :] == iota((slots, count), 0), 1.0, 0.0).astype(bf16)
    out_ref[...] = mm(pick, drow).astype(bf16)


def table_kernel(row_ref, got_ref, out_ref):
    block = out_ref.shape[0]
    slots = got_ref.shape[0]
    at = pl.program_id(0) * block
    pick = jnp.where(row_ref[0:1, :] == iota((block, slots), 0) + at, 1.0, 0.0).astype(bf16)
    out_ref[...] = mm(pick, got_ref[...])


def weights_kernel(got_ref, win_ref, wout_ref):
    d = HEAD_DIM
    parts = got_ref.shape[1]
    rows = win_ref.shape[0] // parts
    width = win_ref.shape[1] // 4
    for p in range(parts):
        here = slice(p * rows, (p + 1) * rows)
        for at, block in enumerate(ORDER):
            for pair in range(HEADS // 2):
                left = got_ref[2 * pair, p, :rows, at * d : (at + 1) * d].astype(f32)
                right = got_ref[2 * pair + 1, p, :rows, at * d : (at + 1) * d].astype(f32)
                start = block * width + pair * 2 * d
                win_ref[here, start : start + 2 * d] = jnp.concatenate([left, right], axis=1)
        for h in range(HEADS):
            wout_ref[h, p // 2, :, 256 * (p % 2) : 256 * (p % 2) + 256] = got_ref[h, p, rows:, :].astype(f32)


def exchange(x, axis):
    return lax.all_to_all(x, axis, split_axis=0, concat_axis=0, tiled=True)


def struct(shape, dtype):
    return jax.ShapeDtypeStruct(shape, dtype)


def layer_step(item_table, item_ids, segment_ids, weight_in, weight_out, gain_in, gain_mid, cotangent):
    shard_rows, width = item_table.shape
    count = item_ids.shape[1]
    users, seq = lax.axis_size("users"), lax.axis_size("seq")
    devices = users * seq
    length = count * seq
    d = HEAD_DIM
    slots = devices * SLOTS
    upstream = cotangent[0]
    gain_row = gain_in.reshape(1, width)
    head = lax.axis_index("seq")

    cot_all = lax.all_gather(upstream, "seq", axis=0, tiled=True)
    wanted, slot_row, slot_col = call(
        functools.partial(slots_kernel, shard_rows),
        (struct((devices, 128), i32), struct((8, count), i32), struct((count, 128), i32)),
        (item_ids, segment_ids),
        flops=2 * devices * count * count, moved=1 << 19,
    )
    asked = exchange(wanted.reshape(devices, 1, 128), BOTH).reshape(devices, 128)
    steps = 4
    whole = lambda *shape: pl.BlockSpec(shape, lambda g: (0,) * len(shape))
    smem = pl.BlockSpec(memory_space=pltpu.SMEM)
    served, asked_row, bounds = call(
        serve_kernel,
        (struct((slots, width), bf16), struct((8, slots), i32), struct((8, 128), i32)),
        (asked, item_table),
        grid=(steps,),
        in_specs=[whole(devices, 128), whole(shard_rows, width)],
        out_specs=[pl.BlockSpec((slots // steps, width), lambda g: (g, 0)), whole(8, slots), whole(8, 128)],
        scratch=[pltpu.VMEM((slots, 128), f32)],
        flops=2 * slots * shard_rows * width, moved=4 << 20,
    )
    got = exchange(served.reshape(devices, SLOTS, width), BOTH).reshape(slots, width)
    fetched, xin = call(
        arrange_kernel,
        (struct((count, width), bf16), struct((count, width), bf16)),
        (got, slot_col, gain_row),
        flops=2 * count * slots * width, moved=2 << 20,
    )
    xin_all = lax.all_gather(xin, "seq", axis=0, tiled=True)

    mine = lax.dynamic_index_in_dim(weight_in.reshape(width, 4, HEADS, d), head, 2, keepdims=False)
    win_t = jnp.stack([mine[:, b] for b in ORDER], axis=1).reshape(width, 4 * d).T
    wout_h = lax.dynamic_slice_in_dim(weight_out, head * d, d, axis=0)
    gain_h = jnp.broadcast_to(lax.dynamic_slice_in_dim(gain_mid, head * d, d)[:, None], (d, 128))

    blocks = length // BLOCK
    lane = lambda rows: pl.BlockSpec((rows, BLOCK), lambda g: (0, g))
    rowed = lambda columns: pl.BlockSpec((BLOCK, columns), lambda g: (g, 0))
    q_t, k_t, vk, slope, u, dg, mixed, stats = call(
        forward_kernel,
        (
            struct((d, length), bf16), struct((d, length), bf16), struct((length, 2 * d), bf16),
            struct((4 * d, length), f32), struct((d, length), f32), struct((d, length), f32),
            struct((d, length), f32), struct((4, length), f32),
        ),
        (xin_all, cot_all, win_t, wout_h, gain_h, bounds),
        grid=(blocks,),
        in_specs=[rowed(width), rowed(width), whole(4 * d, width), whole(d, width), whole(d, 128), smem],
        out_specs=[lane(d), lane(d), rowed(2 * d), lane(4 * d), lane(d), lane(d), lane(d), lane(4)],
        scratch=[pltpu.VMEM((2 * d, BLOCK), bf16), pltpu.VMEM((d, length), bf16), pltpu.VMEM((length, 2 * d), bf16)],
        flops=1 << 33, moved=12 << 20,
    )
    stats_all = lax.all_gather(stats, "seq", axis=0, tiled=False)

    late = lambda g, b: lax.rem(b[0, SLOTS] + jnp.maximum(g - blocks, 0), seq)
    early = lambda g: jnp.minimum(g, blocks - 1)
    fixed = lambda *shape: pl.BlockSpec(shape, lambda g, b: (0,) * len(shape))
    lanes = lambda rows: pl.BlockSpec((rows, BLOCK), lambda g, b: (0, early(g)))
    rows = width // users
    result = pl.pallas_call(
        functools.partial(backward_kernel, blocks),
        out_shape=[struct((5 * d, count), bf16)] * HEADS + [struct((users, rows + 8, 4 * d), f32)],
        grid_spec=pltpu.PrefetchScalarGridSpec(
            num_scalar_prefetch=1,
            grid=(blocks + seq,),
            in_specs=[
                lanes(d), lanes(d), pl.BlockSpec((BLOCK, 2 * d), lambda g, b: (early(g), 0)),
                pl.BlockSpec((seq, 4, BLOCK), lambda g, b: (0, 0, early(g))),
                lanes(d), lanes(d), lanes(d), fixed(d, 128),
                pl.BlockSpec((count, width), lambda g, b: (late(g, b), 0)),
                pl.BlockSpec((count, width), lambda g, b: (late(g, b), 0)),
                pl.BlockSpec((4 * d, count), lambda g, b: (0, late(g, b))),
            ],
            out_specs=[pl.BlockSpec(memory_space=pl.ANY)] * HEADS + [fixed(users, rows + 8, 4 * d)],
            scratch_shapes=[
                pltpu.VMEM((d, length), bf16), pltpu.VMEM((length, 2 * d), bf16), pltpu.VMEM((d, length), bf16),
                pltpu.VMEM((d, length), f32), pltpu.VMEM((d, length), f32), pltpu.VMEM((d, length), f32),
                pltpu.VMEM((d, length), f32), pltpu.VMEM((4 * d, width), f32), pltpu.VMEM((d, width), f32),
                pltpu.VMEM((HEADS, 5 * d, count), bf16), pltpu.SemaphoreType.DMA((HEADS,)),
            ],
        ),
        name="backward",
        compiler_params=pltpu.CompilerParams(
            vmem_limit_bytes=60 * 1024 * 1024, dimension_semantics=("arbitrary",)
        ),
        cost_estimate=pl.CostEstimate(flops=1 << 35, bytes_accessed=16 << 20, transcendentals=0),
    )(bounds, q_t, k_t, vk, stats_all, mixed, dg, u, gain_h, xin_all, cot_all, slope)
    dw = result[HEADS]
    pieces = [result[0]]
    for s in range(1, seq):
        pieces.append(lax.ppermute(result[s], "seq", [(i, (i + s) % seq) for i in range(seq)]))
    dw_got = exchange(dw, "users")
    dw_sum = jnp.sum(dw_got, axis=0).astype(bf16)
    dw_wide = jnp.broadcast_to(dw_sum[None], (users, rows + 8, 4 * d))
    dw_head = exchange(dw_wide, "users")
    dw_all = lax.all_gather(dw_head, "seq", axis=0, tiled=False)
    outgoing, gated_mine = call(
        rows_kernel,
        (struct((slots, width), bf16), struct((width, count), bf16)),
        (*pieces, weight_in, gain_row, fetched, upstream, slot_row),
        scratch=[pltpu.VMEM((4 * width, count), bf16)],
        flops=2 * count * width * 4 * width, moved=6 << 20,
    )
    layer = (
        fetched.astype(f32)
        + lax.dot_general(gated_mine, weight_out, (((0,), (0,)), ((), ())), preferred_element_type=f32)
    ).astype(bf16)
    incoming = exchange(outgoing.reshape(devices, SLOTS, width), BOTH)
    incoming = incoming.reshape(slots, width)
    tiles = 8
    table_grad = call(
        table_kernel,
        struct((shard_rows, width), f32),
        (asked_row, incoming),
        grid=(tiles,),
        in_specs=[whole(8, slots), whole(slots, width)],
        out_specs=pl.BlockSpec((shard_rows // tiles, width), lambda g: (g, 0)),
        flops=2 * slots * shard_rows * width, moved=6 << 20,
    )
    group = 4
    win_grad, wout_grad = call(
        weights_kernel,
        (struct((width, 4 * width), f32), struct((HEADS, width // d, 8, width), f32)),
        (dw_all,),
        grid=(users // group,),
        in_specs=[pl.BlockSpec((seq, group, rows + 8, 4 * d), lambda g: (0, g, 0, 0))],
        out_specs=[
            pl.BlockSpec((group * rows, 4 * width), lambda g: (g, 0)),
            pl.BlockSpec((HEADS, group // 2, 8, width), lambda g: (0, g, 0, 0)),
        ],
        flops=1 << 20, moved=8 << 20,
    )
    return (layer[None], table_grad, win_grad, wout_grad.reshape(width, width))


def solution(mesh):
    in_specs = (
        P(BOTH, None),
        P("users", "seq"),
        P("users", "seq"),
        P(),
        P(),
        P(),
        P(),
        P("users", "seq", None),
    )
    out_specs = (P("users", "seq", None), P(BOTH, None), P(), P())
    return jax.shard_map(layer_step, mesh=mesh, in_specs=in_specs, out_specs=out_specs, check_vma=False)
```

```python
import functools
import jax
import jax.numpy as jnp
from jax import lax
from jax.experimental import pallas as pl
from jax.experimental.pallas import tpu as pltpu
from jax.sharding import PartitionSpec as P


HEADS = 8
HEAD_DIM = 64
SLOTS = 8
CAP = 6
BLOCK = 768
TILE = 256
EPSILON = 1e-05
BOTH = ("users", "seq")
ORDER = (0, 2, 1, 3)

f32 = jnp.float32
bf16 = jnp.bfloat16
i32 = jnp.int32


def iota(shape, dim):
    return lax.broadcasted_iota(i32, shape, dim)


def mm(a, b):
    return jnp.dot(a, b, preferred_element_type=f32)


def mm_nt(a, b):
    return lax.dot_general(a, b, (((1,), (1,)), ((), ())), preferred_element_type=f32)


def call(kernel, out_shape, args, *, grid=None, in_specs=None, out_specs=None, scratch=(), flops=0, moved=0, mib=60):
    params = dict(vmem_limit_bytes=mib * 1024 * 1024)
    extra = {}
    if grid is not None:
        params["dimension_semantics"] = ("arbitrary",) * len(grid)
        extra["grid"] = grid
    if in_specs is not None:
        extra["in_specs"] = in_specs
    if out_specs is not None:
        extra["out_specs"] = out_specs
    return pl.pallas_call(
        kernel,
        out_shape=out_shape,
        scratch_shapes=scratch,
        compiler_params=pltpu.CompilerParams(**params),
        cost_estimate=pl.CostEstimate(flops=flops, bytes_accessed=moved, transcendentals=0),
        **extra,
    )(*args)


def normalize(values):
    centred = values - jnp.mean(values, axis=-1, keepdims=True)
    inverse = lax.rsqrt(jnp.mean(centred * centred, axis=-1, keepdims=True) + EPSILON)
    return centred * inverse, inverse


def slots_kernel(shard_rows, ids_ref, seg_ref, wanted_ref, row_ref, col_ref):
    devices, lanes = wanted_ref.shape
    count = ids_ref.shape[1]
    ids = ids_ref[...]
    owner = lax.shift_right_logical(ids, shard_rows.bit_length() - 1)
    local = (ids & (shard_rows - 1)).astype(f32)
    held = owner == iota((devices, count), 0)
    hit = jnp.where(held, 1.0, 0.0)
    earlier = jnp.where(iota((count, count), 0) < iota((count, count), 1), 1.0, 0.0)
    rank = mm(hit.astype(bf16), earlier.astype(bf16))
    marked = jnp.where(held, rank, -1.0)
    lane = iota((devices, lanes), 1)
    wanted = jnp.zeros((devices, lanes), f32)
    for c in range(CAP):
        column = jnp.sum(jnp.where(marked == float(c), local, 0.0), axis=1, keepdims=True)
        wanted = jnp.where(lane == c, column, wanted)
    seg = seg_ref[...]
    below1 = jnp.sum(jnp.where(seg < 1, 1.0, 0.0), axis=1, keepdims=True)
    below2 = jnp.sum(jnp.where(seg < 2, 1.0, 0.0), axis=1, keepdims=True)
    wanted = jnp.where(lane == CAP, below1, wanted)
    wanted = jnp.where(lane == CAP + 1, below2, wanted)
    wanted_ref[...] = wanted.astype(i32)
    slot = owner.astype(f32) * float(SLOTS) + jnp.sum(hit * rank, axis=0, keepdims=True)
    row_ref[...] = jnp.broadcast_to(slot, row_ref.shape).astype(i32)
    col_ref[...] = jnp.transpose(jnp.broadcast_to(slot, (lanes, count))).astype(i32)


def serve_kernel(asked_ref, table_ref, gain_ref, served_ref, row_ref, bounds_ref, mid_ref, col_ref, turn_ref):
    step = pl.program_id(0)
    block = served_ref.shape[0]
    devices, lanes = asked_ref.shape

    @pl.when(step == 0)
    def _():
        asked = asked_ref[...].astype(f32)
        wide = jnp.broadcast_to(asked[:, None, :], (devices, SLOTS, lanes))
        sub = iota((devices, SLOTS, lanes), 1)
        lane = iota((devices, SLOTS, lanes), 2)
        column = jnp.sum(jnp.where(sub == lane, wide, 0.0), axis=2, keepdims=True)
        column = jnp.where(iota((devices, SLOTS, 1), 1) < CAP, column, -1.0)
        column = jnp.broadcast_to(column, (devices, SLOTS, lanes)).reshape(devices * SLOTS, lanes)
        col_ref[...] = column
        row_ref[...] = jnp.transpose(column)[: row_ref.shape[0]].astype(i32)
        group = lax.axis_index("users")
        mine = lax.div(iota((devices, lanes), 0), SLOTS) == group
        bounds = jnp.sum(jnp.where(mine, asked, 0.0), axis=0, keepdims=True)
        bounds = jnp.broadcast_to(bounds, bounds_ref.shape).astype(i32)
        me = lax.axis_index("seq")
        bounds_ref[...] = jnp.where(iota(bounds_ref.shape, 1) == SLOTS, me, bounds)
        turn_ref[...] = jnp.transpose(jnp.broadcast_to(gain_ref[...], (lanes, gain_ref.shape[1])))
        d = mid_ref.shape[0]
        mid_ref[...] = turn_ref[pl.ds(pl.multiple_of(me * d, d), d), :]

    column = col_ref[pl.ds(pl.multiple_of(step * block, block), block), :].astype(i32)
    parts = []
    for at in range(table_ref.shape[0] // lanes):
        parts.append(jnp.where(column == iota((block, lanes), 1) + at * lanes, 1.0, 0.0).astype(bf16))
    served_ref[...] = mm(jnp.concatenate(parts, axis=1), table_ref[...]).astype(bf16)


def arrange_kernel(got_ref, col_ref, gain_ref, fetched_ref, xin_ref):
    slot = col_ref[...]
    count, lanes = slot.shape
    parts = []
    for at in range(got_ref.shape[0] // lanes):
        parts.append(jnp.where(slot == iota((count, lanes), 1) + at * lanes, 1.0, 0.0).astype(bf16))
    fetched = mm(jnp.concatenate(parts, axis=1), got_ref[...])
    fetched_ref[...] = fetched.astype(bf16)
    normed, _ = normalize(fetched)
    xin_ref[...] = (normed * gain_ref[...]).astype(bf16)


def seg_start(position, one, two):
    return jnp.where(position < one, 0, jnp.where(position < two, one, two))


def visible(i, j, one, two, block):
    where_q = iota((1, block), 1) + i * block
    start = seg_start(where_q, one, two)
    where_k = iota((block, block), 0) + j * block
    return (where_k >= start) & (where_k <= where_q)


def pair_of(p, base, one, two):
    first = lax.div(seg_start(base * TILE, one, two), TILE)
    i, j = base, first + p
    passed = base - first + 1
    for step in range(1, BLOCK // TILE):
        first = lax.div(seg_start((base + step) * TILE, one, two), TILE)
        later = p >= passed
        i = jnp.where(later, base + step, i)
        j = jnp.where(later, first + p - passed, j)
        passed = passed + base + step - first + 1
    return i, j, passed


def forward_kernel(
    xin_ref, dg_ref, win_ref, gain_ref, bounds_ref,
    q_ref, k_ref, vk_ref, slope_ref, u_ref, mixed_ref, stats_ref,
    q_all, v_all, vk_all,
):
    i = pl.program_id(0)
    one, two = bounds_ref[0, CAP], bounds_ref[0, CAP + 1]
    here = pl.ds(pl.multiple_of(i * BLOCK, BLOCK), BLOCK)
    pre = mm_nt(win_ref[...], xin_ref[...])
    tanh = jnp.tanh(pre * 0.5)
    plus = 1.0 + tanh
    hidden = (0.5 * pre) * plus
    slope_ref[...] = 0.5 * (plus + hidden * (1.0 - tanh))
    d = HEAD_DIM
    u = hidden[:d]
    query = (hidden[d : 2 * d].astype(bf16).astype(f32) * 0.0625).astype(bf16)
    vk = hidden[2 * d :]
    vk_t = vk.astype(bf16)
    turned = jnp.transpose(vk).astype(bf16)
    u_ref[...] = u
    q_ref[...] = query
    k_ref[...] = vk_t[d:]
    vk_ref[...] = turned
    q_all[:d, :] = jnp.zeros((d, BLOCK), bf16)
    q_all[d:, :] = query
    v_all[:, here] = vk_t[:d]
    vk_all[here, :] = turned
    mixed_ref[...] = jnp.zeros(mixed_ref.shape, f32)

    def pair(j, carry):
        there = pl.ds(pl.multiple_of(j * BLOCK, BLOCK), BLOCK)
        half = mm(vk_all[there, :], q_all[...])
        weights = half + half * jnp.tanh(half)
        weights = jnp.where(visible(i, j, one, two, BLOCK), weights, 0.0).astype(bf16)
        mixed_ref[...] += mm(v_all[:, there], weights)
        return carry

    first = lax.div(seg_start(i * BLOCK, one, two), BLOCK)
    lax.fori_loop(first, i + 1, pair, 0)
    dg = dg_ref[...]
    mixed = mixed_ref[...]
    e = dg * u * gain_ref[:, :1]
    mean = jnp.sum(mixed, axis=0, keepdims=True) * (1.0 / d)
    centred = mixed - mean
    spread = jnp.sum(centred * centred, axis=0, keepdims=True)
    sum_e = jnp.sum(e, axis=0, keepdims=True)
    sum_em = jnp.sum(e * centred, axis=0, keepdims=True)
    for h in range(HEADS):
        stats_ref[h, 0:1, :] = mean
        stats_ref[h, 1:2, :] = spread
        stats_ref[h, 2:3, :] = sum_e
        stats_ref[h, 3:4, :] = sum_em


def middle(stats, mixed, dg, u, gain):
    width = HEADS * HEAD_DIM
    means = [stats[h, 0:1] for h in range(HEADS)]
    mean = functools.reduce(jnp.add, means) * (1.0 / HEADS)
    var, m_e, m_em = 0.0, 0.0, 0.0
    for h in range(HEADS):
        off = means[h] - mean
        var = var + stats[h, 1:2] + HEAD_DIM * off * off
        m_e = m_e + stats[h, 2:3]
        m_em = m_em + stats[h, 3:4] + off * stats[h, 2:3]
    inverse = lax.rsqrt(var * (1.0 / width) + EPSILON)
    m_e = m_e * (1.0 / width)
    m_eh = m_em * inverse * (1.0 / width)
    hat = (mixed - mean) * inverse
    scaled = hat * gain
    e = dg * u * gain
    up = (inverse * (e - m_e - hat * m_eh)).astype(bf16)
    return (scaled * u).astype(bf16), (up.astype(f32) * 0.0625).astype(bf16), dg * scaled


def backward_kernel(
    steps, bounds_ref, q_ref, k_ref, vk_ref, stats_ref, mixed_ref, dg_ref, u_ref, gain_ref, xin_hbm, cot_hbm, slope_hbm,
    *rest,
):
    outs, rest = rest[:HEADS], rest[HEADS:]
    dw_ref, k_all, vk_all, gated_all, du_all, dq_all, dk_all, dv_all, win_acc, wout_acc, sent, sems = rest[:12]
    query2, up2, half0, upper0, half1, upper1, xin_ref, cot_ref, slope_ref, loaded = rest[12:]
    loads = [
        pltpu.make_async_copy(source, target, loaded.at[at])
        for at, (source, target) in enumerate(((xin_hbm, xin_ref), (cot_hbm, cot_ref), (slope_hbm, slope_ref)))
    ]
    g = pl.program_id(0)
    one, two, me = bounds_ref[0, CAP], bounds_ref[0, CAP + 1], bounds_ref[0, SLOTS]
    d = HEAD_DIM

    @pl.when(g == 0)
    def _():
        for load in loads:
            load.start()
        dk_all[...] = jnp.zeros(dk_all.shape, f32)
        dv_all[...] = jnp.zeros(dv_all.shape, f32)
        dq_all[...] = jnp.zeros(dq_all.shape, f32)
        win_acc[...] = jnp.zeros(win_acc.shape, f32)
        wout_acc[...] = jnp.zeros(wout_acc.shape, f32)
        query2[...] = jnp.zeros(query2.shape, bf16)
        up2[...] = jnp.zeros(up2.shape, bf16)

    @pl.when(g < steps)
    def _():
        here = pl.ds(pl.multiple_of(g * BLOCK, BLOCK), BLOCK)
        gated, up, du = middle(stats_ref[...], mixed_ref[...], dg_ref[...], u_ref[...], gain_ref[:, :1])
        gated_all[:, here] = gated
        du_all[:, here] = du
        k_all[:, here] = k_ref[...]
        vk_all[here, :] = vk_ref[...]
        query2[d:, :] = q_ref[...]
        up2[:d, :] = up
        base = g * (BLOCK // TILE)
        total = pair_of(0, base, one, two)[2]

        def front(i, j):
            at = pl.ds(pl.multiple_of((i - base) * TILE, TILE), TILE)
            vk = vk_all[pl.ds(pl.multiple_of(j * TILE, TILE), TILE), :]
            return mm(vk, query2[:, at]), mm(vk, up2[:, at])

        def back(i, j, half, upper, live):
            at = pl.ds(pl.multiple_of((i - base) * TILE, TILE), TILE)
            here = pl.ds(pl.multiple_of(i * TILE, TILE), TILE)
            there = pl.ds(pl.multiple_of(j * TILE, TILE), TILE)
            tanh = jnp.tanh(half)
            plus = 1.0 + tanh
            weights = half * plus
            dscores = upper * (plus + weights * (1.0 - tanh))
            seen = visible(i, jnp.where(live, j, dq_all.shape[1]), one, two, TILE)
            weights = jnp.where(seen, weights, 0.0).astype(bf16)
            dscores = jnp.where(seen, dscores, 0.0).astype(bf16)
            dv_all[:, there] += mm_nt(up2[:d, at], weights)
            dk_all[:, there] += mm_nt(query2[d:, at], dscores)
            dq_all[:, here] += mm(k_all[:, there], dscores)

        half0[...], upper0[...] = front(*pair_of(0, base, one, two)[:2])

        def two_pairs(t, carry):
            p = 2 * t
            now, odd, after = [
                pair_of(jnp.minimum(p + step, total - 1), base, one, two)[:2] for step in range(3)
            ]
            half1[...], upper1[...] = front(*odd)
            back(*now, half0[...], upper0[...], True)
            half0[...], upper0[...] = front(*after)
            back(*odd, half1[...], upper1[...], p + 1 < total)
            return carry

        lax.fori_loop(0, lax.div(total + 1, 2), two_pairs, 0)

    @pl.when(g == steps)
    def _():
        for load in loads:
            load.wait()
        count = sent.shape[2]
        for s in range(HEADS):
            start = pl.multiple_of(lax.rem(me + s, HEADS) * count, 128)
            here = pl.ds(start, count)
            gated = gated_all[:, here]
            dpre = jnp.concatenate(
                [
                    (du_all[:, here] * slope_ref[:d, here]).astype(bf16),
                    (dq_all[:, here] * slope_ref[d : 2 * d, here]).astype(bf16),
                    (dv_all[:, here] * 16.0 * slope_ref[2 * d : 3 * d, here]).astype(bf16),
                    (dk_all[:, here] * 16.0 * slope_ref[3 * d :, here]).astype(bf16),
                ],
                axis=0,
            )
            sent[s, : 4 * d, :] = dpre
            sent[s, 4 * d :, :] = gated
            pltpu.make_async_copy(sent.at[s], outs[s], sems.at[s]).start()
            win_acc[...] += mm(dpre, xin_ref[here, :])
            wout_acc[...] += mm(gated, cot_ref[here, :])
        parts = dw_ref.shape[0]
        turned = jnp.transpose(win_acc[...])
        rows = turned.shape[0] // parts
        for p in range(parts):
            dw_ref[p, :rows, :] = turned[p * rows : (p + 1) * rows]
            dw_ref[p, rows:, :] = wout_acc[8 * (p // 2) : 8 * (p // 2) + 8, 256 * (p % 2) : 256 * (p % 2) + 256]
        for at in range(HEADS):
            pltpu.make_async_copy(sent.at[at], outs[at], sems.at[at]).wait()


def rows_kernel(*refs):
    got = refs[:HEADS]
    win_ref, gain_ref, fetched_ref, cot_ref, row_ref, out_ref, gated_ref, whole = refs[HEADS:]
    d = HEAD_DIM
    width = fetched_ref.shape[1]
    me = lax.axis_index("seq")
    for s in range(HEADS):
        at_head = pl.multiple_of(lax.rem(me + HEADS - s, HEADS) * d, d)
        for at, block in enumerate(ORDER):
            whole[pl.ds(block * width + at_head, d), :] = got[s][at * d : (at + 1) * d, :]
        gated_ref[pl.ds(at_head, d), :] = got[s][4 * d :, :]
    dxin = jnp.transpose(mm(win_ref[...], whole[...]))
    normed, inverse = normalize(fetched_ref[...].astype(f32))
    f = dxin * gain_ref[...]
    drow = inverse * (
        f - jnp.mean(f, axis=-1, keepdims=True) - normed * jnp.mean(f * normed, axis=-1, keepdims=True)
    ) + cot_ref[...].astype(f32)
    drow = drow.astype(bf16)
    slots = out_ref.shape[0]
    count = drow.shape[0]
    pick = jnp.where(row_ref[0:1, :] == iota((slots, count), 0), 1.0, 0.0).astype(bf16)
    out_ref[...] = mm(pick, drow).astype(bf16)


def table_kernel(row_ref, got_ref, out_ref):
    block = out_ref.shape[0]
    slots = got_ref.shape[0]
    at = pl.program_id(0) * block
    pick = jnp.where(row_ref[0:1, :] == iota((block, slots), 0) + at, 1.0, 0.0).astype(bf16)
    out_ref[...] = mm(pick, got_ref[...])


def weights_kernel(got_ref, win_ref, wout_ref):
    d = HEAD_DIM
    parts = got_ref.shape[1]
    rows = win_ref.shape[0] // parts
    width = win_ref.shape[1] // 4
    for p in range(parts):
        here = slice(p * rows, (p + 1) * rows)
        for at, block in enumerate(ORDER):
            for pair in range(HEADS // 2):
                left = got_ref[2 * pair, p, :rows, at * d : (at + 1) * d].astype(f32)
                right = got_ref[2 * pair + 1, p, :rows, at * d : (at + 1) * d].astype(f32)
                start = block * width + pair * 2 * d
                win_ref[here, start : start + 2 * d] = jnp.concatenate([left, right], axis=1)
        for h in range(HEADS):
            wout_ref[h, p // 2, :, 256 * (p % 2) : 256 * (p % 2) + 256] = got_ref[h, p, rows:, :].astype(f32)


def exchange(x, axis):
    return lax.all_to_all(x, axis, split_axis=0, concat_axis=0, tiled=True)


def struct(shape, dtype):
    return jax.ShapeDtypeStruct(shape, dtype)


def layer_step(item_table, item_ids, segment_ids, weight_in, weight_out, gain_in, gain_mid, cotangent):
    shard_rows, width = item_table.shape
    count = item_ids.shape[1]
    users, seq = lax.axis_size("users"), lax.axis_size("seq")
    devices = users * seq
    length = count * seq
    d = HEAD_DIM
    slots = devices * SLOTS
    upstream = cotangent[0]
    gain_row = gain_in.reshape(1, width)
    head = lax.axis_index("seq")

    cot_all = lax.all_gather(upstream, "seq", axis=0, tiled=True)
    wanted, slot_row, slot_col = call(
        functools.partial(slots_kernel, shard_rows),
        (struct((devices, 128), i32), struct((8, count), i32), struct((count, 128), i32)),
        (item_ids, segment_ids),
        flops=2 * devices * count * count, moved=1 << 19,
    )
    asked = exchange(wanted.reshape(devices, 1, 128), BOTH).reshape(devices, 128)
    steps = 4
    whole = lambda *shape: pl.BlockSpec(shape, lambda g: (0,) * len(shape))
    smem = pl.BlockSpec(memory_space=pltpu.SMEM)
    served, asked_row, bounds, gain_h = call(
        serve_kernel,
        (struct((slots, width), bf16), struct((8, slots), i32), struct((8, 128), i32), struct((d, 128), f32)),
        (asked, item_table, gain_mid.reshape(1, width)),
        grid=(steps,),
        in_specs=[whole(devices, 128), whole(shard_rows, width), whole(1, width)],
        out_specs=[
            pl.BlockSpec((slots // steps, width), lambda g: (g, 0)), whole(8, slots), whole(8, 128), whole(d, 128),
        ],
        scratch=[pltpu.VMEM((slots, 128), f32), pltpu.VMEM((width, 128), f32)],
        flops=2 * slots * shard_rows * width, moved=4 << 20,
    )
    got = exchange(served.reshape(devices, SLOTS, width), BOTH).reshape(slots, width)
    fetched, xin = call(
        arrange_kernel,
        (struct((count, width), bf16), struct((count, width), bf16)),
        (got, slot_col, gain_row),
        flops=2 * count * slots * width, moved=2 << 20,
    )
    xin_all = lax.all_gather(xin, "seq", axis=0, tiled=True)

    mine = lax.dynamic_index_in_dim(weight_in.reshape(width, 4, HEADS, d), head, 2, keepdims=False)
    win_t = jnp.stack([mine[:, b] for b in ORDER], axis=1).reshape(width, 4 * d).T
    wout_h = lax.dynamic_slice_in_dim(weight_out, head * d, d, axis=0)

    blocks = length // BLOCK
    lane = lambda rows: pl.BlockSpec((rows, BLOCK), lambda g: (0, g))
    rowed = lambda columns: pl.BlockSpec((BLOCK, columns), lambda g: (g, 0))
    dg = mm_nt(wout_h, cot_all)
    q_t, k_t, vk, slope, u, mixed, stats = call(
        forward_kernel,
        (
            struct((d, length), bf16), struct((d, length), bf16), struct((length, 2 * d), bf16),
            struct((4 * d, length), f32), struct((d, length), f32),
            struct((d, length), f32), struct((seq, 4, length), f32),
        ),
        (xin_all, dg, win_t, gain_h, bounds),
        mib=60, grid=(blocks,),
        in_specs=[rowed(width), lane(d), whole(4 * d, width), whole(d, 128), smem],
        out_specs=[lane(d), lane(d), rowed(2 * d), lane(4 * d), lane(d), lane(d),
            pl.BlockSpec((seq, 4, BLOCK), lambda g: (0, 0, g)),
        ],
        scratch=[pltpu.VMEM((2 * d, BLOCK), bf16), pltpu.VMEM((d, length), bf16), pltpu.VMEM((length, 2 * d), bf16)],
        flops=1 << 33, moved=12 << 20,
    )
    stats_all = exchange(stats, "seq")

    early = lambda g: jnp.minimum(g, blocks - 1)
    fixed = lambda *shape: pl.BlockSpec(shape, lambda g, b: (0,) * len(shape))
    lanes = lambda rows: pl.BlockSpec((rows, BLOCK), lambda g, b: (0, early(g)))
    rows = width // users
    result = pl.pallas_call(
        functools.partial(backward_kernel, blocks),
        out_shape=[struct((5 * d, count), bf16)] * HEADS + [struct((users, rows + 8, 4 * d), f32)],
        grid_spec=pltpu.PrefetchScalarGridSpec(
            num_scalar_prefetch=1,
            grid=(blocks + 1,),
            in_specs=[
                lanes(d), lanes(d), pl.BlockSpec((BLOCK, 2 * d), lambda g, b: (early(g), 0)),
                pl.BlockSpec((seq, 4, BLOCK), lambda g, b: (0, 0, early(g))),
                lanes(d), lanes(d), lanes(d), fixed(d, 128),
                *[pl.BlockSpec(memory_space=pl.ANY)] * 3,
            ],
            out_specs=[pl.BlockSpec(memory_space=pl.ANY)] * HEADS + [fixed(users, rows + 8, 4 * d)],
            scratch_shapes=[
                pltpu.VMEM((d, length), bf16), pltpu.VMEM((length, 2 * d), bf16), pltpu.VMEM((d, length), bf16),
                pltpu.VMEM((d, length), f32), pltpu.VMEM((d, length), f32), pltpu.VMEM((d, length), f32),
                pltpu.VMEM((d, length), f32), pltpu.VMEM((4 * d, width), f32), pltpu.VMEM((d, width), f32),
                pltpu.VMEM((HEADS, 5 * d, count), bf16), pltpu.SemaphoreType.DMA((HEADS,)),
                pltpu.VMEM((2 * d, BLOCK), bf16), pltpu.VMEM((2 * d, BLOCK), bf16),
                *[pltpu.VMEM((TILE, TILE), f32)] * 4,
                pltpu.VMEM((length, width), bf16), pltpu.VMEM((length, width), bf16), pltpu.VMEM((4 * d, length), f32),
                pltpu.SemaphoreType.DMA((3,)),
            ],
        ),
        name="backward",
        compiler_params=pltpu.CompilerParams(
            vmem_limit_bytes=60 * 1024 * 1024, dimension_semantics=("arbitrary",)
        ),
        cost_estimate=pl.CostEstimate(flops=1 << 35, bytes_accessed=16 << 20, transcendentals=0),
    )(bounds, q_t, k_t, vk, stats_all, mixed, dg, u, gain_h, xin_all, cot_all, slope)
    dw = result[HEADS]
    pieces = [result[0]]
    for s in range(1, seq):
        pieces.append(lax.ppermute(result[s], "seq", [(i, (i + s) % seq) for i in range(seq)]))
    dw_got = exchange(dw, "users")
    dw_sum = jnp.sum(dw_got, axis=0).astype(bf16)
    dw_wide = jnp.broadcast_to(dw_sum[None], (users, rows + 8, 4 * d))
    dw_head = exchange(dw_wide, "users")
    dw_all = lax.all_gather(dw_head, "seq", axis=0, tiled=False)
    outgoing, gated_mine = call(
        rows_kernel,
        (struct((slots, width), bf16), struct((width, count), bf16)),
        (*pieces, weight_in, gain_row, fetched, upstream, slot_row),
        mib=24, in_specs=[pl.BlockSpec(memory_space=pltpu.VMEM)] * (HEADS + 5), scratch=[pltpu.VMEM((4 * width, count), bf16)],
        flops=2 * count * width * 4 * width, moved=6 << 20,
    )
    layer = (
        fetched.astype(f32)
        + lax.dot_general(gated_mine, weight_out, (((0,), (0,)), ((), ())), preferred_element_type=f32)
    ).astype(bf16)
    incoming = exchange(outgoing.reshape(devices, SLOTS, width), BOTH)
    incoming = incoming.reshape(slots, width)
    tiles = 8
    table_grad = call(
        table_kernel,
        struct((shard_rows, width), f32),
        (asked_row, incoming),
        mib=24, grid=(tiles,),
        in_specs=[whole(8, slots), pl.BlockSpec(memory_space=pltpu.VMEM)],
        out_specs=pl.BlockSpec((shard_rows // tiles, width), lambda g: (g, 0)),
        flops=2 * slots * shard_rows * width, moved=6 << 20,
    )
    group = 4
    win_grad, wout_grad = call(
        weights_kernel,
        (struct((width, 4 * width), f32), struct((HEADS, width // d, 8, width), f32)),
        (dw_all,),
        grid=(users // group,),
        in_specs=[pl.BlockSpec((seq, group, rows + 8, 4 * d), lambda g: (0, g, 0, 0))],
        out_specs=[
            pl.BlockSpec((group * rows, 4 * width), lambda g: (g, 0)),
            pl.BlockSpec((HEADS, group // 2, 8, width), lambda g: (0, g, 0, 0)),
        ],
        flops=1 << 20, moved=8 << 20,
    )
    return (layer[None], table_grad, win_grad, wout_grad.reshape(width, width))


def solution(mesh):
    in_specs = (
        P(BOTH, None),
        P("users", "seq"),
        P("users", "seq"),
        P(),
        P(),
        P(),
        P(),
        P("users", "seq", None),
    )
    out_specs = (P("users", "seq", None), P(BOTH, None), P(), P())
    return jax.shard_map(layer_step, mesh=mesh, in_specs=in_specs, out_specs=out_specs, check_vma=False)
```

```python
import functools
import jax
import jax.numpy as jnp
from jax import lax
from jax.experimental import pallas as pl
from jax.experimental.pallas import tpu as pltpu
from jax.sharding import PartitionSpec as P


HEADS = 8
HEAD_DIM = 64
SLOTS = 8
CAP = 6
BLOCK = 768
TILE = 256
EPSILON = 1e-05
BOTH = ("users", "seq")
ORDER = (0, 2, 1, 3)

f32 = jnp.float32
bf16 = jnp.bfloat16
i32 = jnp.int32


def iota(shape, dim):
    return lax.broadcasted_iota(i32, shape, dim)


def mm(a, b):
    return jnp.dot(a, b, preferred_element_type=f32)


def mm_nt(a, b):
    return lax.dot_general(a, b, (((1,), (1,)), ((), ())), preferred_element_type=f32)


def call(kernel, out_shape, args, *, grid=None, in_specs=None, out_specs=None, scratch=(), flops=0, moved=0, mib=60):
    params = dict(vmem_limit_bytes=mib * 1024 * 1024)
    extra = {}
    if grid is not None:
        params["dimension_semantics"] = ("arbitrary",) * len(grid)
        extra["grid"] = grid
    if in_specs is not None:
        extra["in_specs"] = in_specs
    if out_specs is not None:
        extra["out_specs"] = out_specs
    return pl.pallas_call(
        kernel,
        out_shape=out_shape,
        scratch_shapes=scratch,
        compiler_params=pltpu.CompilerParams(**params),
        cost_estimate=pl.CostEstimate(flops=flops, bytes_accessed=moved, transcendentals=0),
        **extra,
    )(*args)


def normalize(values):
    centred = values - jnp.mean(values, axis=-1, keepdims=True)
    inverse = lax.rsqrt(jnp.mean(centred * centred, axis=-1, keepdims=True) + EPSILON)
    return centred * inverse, inverse


def slots_kernel(shard_rows, ids_ref, seg_ref, wanted_ref, row_ref, col_ref):
    devices, lanes = wanted_ref.shape
    count = ids_ref.shape[1]
    ids = ids_ref[...]
    owner = lax.shift_right_logical(ids, shard_rows.bit_length() - 1)
    local = (ids & (shard_rows - 1)).astype(f32)
    held = owner == iota((devices, count), 0)
    hit = jnp.where(held, 1.0, 0.0)
    earlier = jnp.where(iota((count, count), 0) < iota((count, count), 1), 1.0, 0.0)
    rank = mm(hit.astype(bf16), earlier.astype(bf16))
    marked = jnp.where(held, rank, -1.0)
    lane = iota((devices, lanes), 1)
    wanted = jnp.zeros((devices, lanes), f32)
    for c in range(CAP):
        column = jnp.sum(jnp.where(marked == float(c), local, 0.0), axis=1, keepdims=True)
        wanted = jnp.where(lane == c, column, wanted)
    seg = seg_ref[...]
    below1 = jnp.sum(jnp.where(seg < 1, 1.0, 0.0), axis=1, keepdims=True)
    below2 = jnp.sum(jnp.where(seg < 2, 1.0, 0.0), axis=1, keepdims=True)
    wanted = jnp.where(lane == CAP, below1, wanted)
    wanted = jnp.where(lane == CAP + 1, below2, wanted)
    wanted_ref[...] = wanted.astype(i32)
    slot = owner.astype(f32) * float(SLOTS) + jnp.sum(hit * rank, axis=0, keepdims=True)
    row_ref[...] = jnp.broadcast_to(slot, row_ref.shape).astype(i32)
    col_ref[...] = jnp.transpose(jnp.broadcast_to(slot, (lanes, count))).astype(i32)


def serve_kernel(
    asked_ref, table_hbm, gain_ref, served_ref, row_ref, bounds_ref, mid_ref, col_ref, turn_ref, table_ref, sems
):
    step = pl.program_id(0)
    block = served_ref.shape[0]
    devices, lanes = asked_ref.shape
    chunks = sems.shape[0]
    tall = table_ref.shape[0] // chunks
    loads = [
        pltpu.make_async_copy(table_hbm.at[pl.ds(c * tall, tall)], table_ref.at[pl.ds(c * tall, tall)], sems.at[c])
        for c in range(chunks)
    ]

    @pl.when(step == 0)
    def _():
        for load in loads:
            load.start()
        asked = asked_ref[...].astype(f32)
        wide = jnp.broadcast_to(asked[:, None, :], (devices, SLOTS, lanes))
        sub = iota((devices, SLOTS, lanes), 1)
        lane = iota((devices, SLOTS, lanes), 2)
        column = jnp.sum(jnp.where(sub == lane, wide, 0.0), axis=2, keepdims=True)
        column = jnp.where(iota((devices, SLOTS, 1), 1) < CAP, column, -1.0)
        column = jnp.broadcast_to(column, (devices, SLOTS, lanes)).reshape(devices * SLOTS, lanes)
        col_ref[...] = column
        row_ref[...] = jnp.transpose(column)[: row_ref.shape[0]].astype(i32)
        group = lax.axis_index("users")
        mine = lax.div(iota((devices, lanes), 0), SLOTS) == group
        bounds = jnp.sum(jnp.where(mine, asked, 0.0), axis=0, keepdims=True)
        bounds = jnp.broadcast_to(bounds, bounds_ref.shape).astype(i32)
        me = lax.axis_index("seq")
        bounds_ref[...] = jnp.where(iota(bounds_ref.shape, 1) == SLOTS, me, bounds)
        turn_ref[...] = jnp.transpose(jnp.broadcast_to(gain_ref[...], (lanes, gain_ref.shape[1])))
        d = mid_ref.shape[0]
        mid_ref[...] = turn_ref[pl.ds(pl.multiple_of(me * d, d), d), :]

    column = col_ref[pl.ds(pl.multiple_of(step * block, block), block), :].astype(i32)
    served = None
    for c in range(chunks):
        parts = []
        for at in range(c * tall, (c + 1) * tall, lanes):
            parts.append(jnp.where(column == iota((block, lanes), 1) + at, 1.0, 0.0).astype(bf16))

        @pl.when(step == 0)
        def _():
            loads[c].wait()

        product = mm(jnp.concatenate(parts, axis=1), table_ref[c * tall : (c + 1) * tall, :])
        served = product if served is None else served + product
    served_ref[...] = served.astype(bf16)


def arrange_kernel(got_ref, col_ref, gain_ref, fetched_ref, xin_ref):
    slot = col_ref[...]
    count, lanes = slot.shape
    parts = []
    for at in range(got_ref.shape[0] // lanes):
        parts.append(jnp.where(slot == iota((count, lanes), 1) + at * lanes, 1.0, 0.0).astype(bf16))
    fetched = mm(jnp.concatenate(parts, axis=1), got_ref[...])
    fetched_ref[...] = fetched.astype(bf16)
    normed, _ = normalize(fetched)
    xin_ref[...] = (normed * gain_ref[...]).astype(bf16)


def seg_start(position, one, two):
    return jnp.where(position < one, 0, jnp.where(position < two, one, two))


def visible(i, j, one, two, block):
    where_q = iota((1, block), 1) + i * block
    start = seg_start(where_q, one, two)
    where_k = iota((block, block), 0) + j * block
    return (where_k >= start) & (where_k <= where_q)


def pair_of(p, base, one, two):
    first = lax.div(seg_start(base * TILE, one, two), TILE)
    i, j = base, first + p
    passed = base - first + 1
    for step in range(1, BLOCK // TILE):
        first = lax.div(seg_start((base + step) * TILE, one, two), TILE)
        later = p >= passed
        i = jnp.where(later, base + step, i)
        j = jnp.where(later, first + p - passed, j)
        passed = passed + base + step - first + 1
    return i, j, passed


def forward_kernel(
    xin_ref, dg_ref, win_ref, gain_ref, bounds_ref,
    q_ref, k_ref, vk_ref, slope_ref, u_ref, mixed_ref, stats_ref,
    q_all, v_all, vk_all,
):
    i = pl.program_id(0)
    one, two = bounds_ref[0, CAP], bounds_ref[0, CAP + 1]
    here = pl.ds(pl.multiple_of(i * BLOCK, BLOCK), BLOCK)
    pre = mm_nt(win_ref[...], xin_ref[...])
    tanh = jnp.tanh(pre * 0.5)
    plus = 1.0 + tanh
    hidden = (0.5 * pre) * plus
    slope_ref[...] = 0.5 * (plus + hidden * (1.0 - tanh))
    d = HEAD_DIM
    u = hidden[:d]
    query = (hidden[d : 2 * d].astype(bf16).astype(f32) * 0.0625).astype(bf16)
    vk = hidden[2 * d :]
    vk_t = vk.astype(bf16)
    turned = jnp.transpose(vk).astype(bf16)
    u_ref[...] = u
    q_ref[...] = query
    k_ref[...] = vk_t[d:]
    vk_ref[...] = turned
    q_all[:d, :] = jnp.zeros((d, BLOCK), bf16)
    q_all[d:, :] = query
    v_all[:, here] = vk_t[:d]
    vk_all[here, :] = turned
    mixed_ref[...] = jnp.zeros(mixed_ref.shape, f32)

    def pair(j, carry):
        there = pl.ds(pl.multiple_of(j * BLOCK, BLOCK), BLOCK)
        half = mm(vk_all[there, :], q_all[...])
        weights = half + half * jnp.tanh(half)
        weights = jnp.where(visible(i, j, one, two, BLOCK), weights, 0.0).astype(bf16)
        mixed_ref[...] += mm(v_all[:, there], weights)
        return carry

    first = lax.div(seg_start(i * BLOCK, one, two), BLOCK)
    lax.fori_loop(first, i + 1, pair, 0)
    dg = dg_ref[...]
    mixed = mixed_ref[...]
    e = dg * u * gain_ref[:, :1]
    mean = jnp.sum(mixed, axis=0, keepdims=True) * (1.0 / d)
    centred = mixed - mean
    spread = jnp.sum(centred * centred, axis=0, keepdims=True)
    sum_e = jnp.sum(e, axis=0, keepdims=True)
    sum_em = jnp.sum(e * centred, axis=0, keepdims=True)
    for h in range(HEADS):
        stats_ref[h, 0:1, :] = mean
        stats_ref[h, 1:2, :] = spread
        stats_ref[h, 2:3, :] = sum_e
        stats_ref[h, 3:4, :] = sum_em


def middle(stats, mixed, dg, u, gain):
    width = HEADS * HEAD_DIM
    means = [stats[h, 0:1] for h in range(HEADS)]
    mean = functools.reduce(jnp.add, means) * (1.0 / HEADS)
    var, m_e, m_em = 0.0, 0.0, 0.0
    for h in range(HEADS):
        off = means[h] - mean
        var = var + stats[h, 1:2] + HEAD_DIM * off * off
        m_e = m_e + stats[h, 2:3]
        m_em = m_em + stats[h, 3:4] + off * stats[h, 2:3]
    inverse = lax.rsqrt(var * (1.0 / width) + EPSILON)
    m_e = m_e * (1.0 / width)
    m_eh = m_em * inverse * (1.0 / width)
    hat = (mixed - mean) * inverse
    scaled = hat * gain
    e = dg * u * gain
    up = (inverse * (e - m_e - hat * m_eh)).astype(bf16)
    return (scaled * u).astype(bf16), (up.astype(f32) * 0.0625).astype(bf16), dg * scaled


def backward_kernel(
    steps, bounds_ref, q_ref, k_ref, vk_ref, stats_ref, mixed_ref, dg_ref, u_ref, gain_ref, xin_hbm, cot_hbm, slope_hbm,
    *rest,
):
    outs, rest = rest[:HEADS], rest[HEADS:]
    dw_ref, k_all, vk_all, gated_all, du_all, dq_all, dk_all, dv_all, win_acc, wout_acc, sent, sems = rest[:12]
    query2, up2, half0, upper0, half1, upper1, xin_ref, cot_ref, slope_ref, loaded = rest[12:]
    loads = [
        pltpu.make_async_copy(source, target, loaded.at[at])
        for at, (source, target) in enumerate(((xin_hbm, xin_ref), (cot_hbm, cot_ref), (slope_hbm, slope_ref)))
    ]
    g = pl.program_id(0)
    one, two, me = bounds_ref[0, CAP], bounds_ref[0, CAP + 1], bounds_ref[0, SLOTS]
    d = HEAD_DIM

    @pl.when(g == 0)
    def _():
        for load in loads:
            load.start()
        dk_all[...] = jnp.zeros(dk_all.shape, f32)
        dv_all[...] = jnp.zeros(dv_all.shape, f32)
        dq_all[...] = jnp.zeros(dq_all.shape, f32)
        win_acc[...] = jnp.zeros(win_acc.shape, f32)
        wout_acc[...] = jnp.zeros(wout_acc.shape, f32)
        query2[...] = jnp.zeros(query2.shape, bf16)
        up2[...] = jnp.zeros(up2.shape, bf16)

    @pl.when(g < steps)
    def _():
        here = pl.ds(pl.multiple_of(g * BLOCK, BLOCK), BLOCK)
        gated, up, du = middle(stats_ref[...], mixed_ref[...], dg_ref[...], u_ref[...], gain_ref[:, :1])
        gated_all[:, here] = gated
        du_all[:, here] = du
        k_all[:, here] = k_ref[...]
        vk_all[here, :] = vk_ref[...]
        query2[d:, :] = q_ref[...]
        up2[:d, :] = up
        base = g * (BLOCK // TILE)
        total = pair_of(0, base, one, two)[2]

        def front(i, j):
            at = pl.ds(pl.multiple_of((i - base) * TILE, TILE), TILE)
            vk = vk_all[pl.ds(pl.multiple_of(j * TILE, TILE), TILE), :]
            return mm(vk, query2[:, at]), mm(vk, up2[:, at])

        def back(i, j, half, upper, live):
            at = pl.ds(pl.multiple_of((i - base) * TILE, TILE), TILE)
            here = pl.ds(pl.multiple_of(i * TILE, TILE), TILE)
            there = pl.ds(pl.multiple_of(j * TILE, TILE), TILE)
            tanh = jnp.tanh(half)
            plus = 1.0 + tanh
            weights = half * plus
            dscores = upper * (plus + weights * (1.0 - tanh))
            seen = visible(i, jnp.where(live, j, dq_all.shape[1]), one, two, TILE)
            weights = jnp.where(seen, weights, 0.0).astype(bf16)
            dscores = jnp.where(seen, dscores, 0.0).astype(bf16)
            dv_all[:, there] += mm_nt(up2[:d, at], weights)
            dk_all[:, there] += mm_nt(query2[d:, at], dscores)
            dq_all[:, here] += mm(k_all[:, there], dscores)

        half0[...], upper0[...] = front(*pair_of(0, base, one, two)[:2])

        def two_pairs(t, carry):
            p = 2 * t
            now, odd, after = [
                pair_of(jnp.minimum(p + step, total - 1), base, one, two)[:2] for step in range(3)
            ]
            half1[...], upper1[...] = front(*odd)
            back(*now, half0[...], upper0[...], True)
            half0[...], upper0[...] = front(*after)
            back(*odd, half1[...], upper1[...], p + 1 < total)
            return carry

        lax.fori_loop(0, lax.div(total + 1, 2), two_pairs, 0)

    @pl.when(g == steps)
    def _():
        for load in loads:
            load.wait()
        count = sent.shape[2]
        for s in range(HEADS):
            start = pl.multiple_of(lax.rem(me + s, HEADS) * count, 128)
            here = pl.ds(start, count)
            gated = gated_all[:, here]
            dpre = jnp.concatenate(
                [
                    (du_all[:, here] * slope_ref[:d, here]).astype(bf16),
                    (dq_all[:, here] * slope_ref[d : 2 * d, here]).astype(bf16),
                    (dv_all[:, here] * 16.0 * slope_ref[2 * d : 3 * d, here]).astype(bf16),
                    (dk_all[:, here] * 16.0 * slope_ref[3 * d :, here]).astype(bf16),
                ],
                axis=0,
            )
            sent[s, : 4 * d, :] = dpre
            sent[s, 4 * d :, :] = gated
            pltpu.make_async_copy(sent.at[s], outs[s], sems.at[s]).start()
            win_acc[...] += mm(dpre, xin_ref[here, :])
            wout_acc[...] += mm(gated, cot_ref[here, :])
        parts = dw_ref.shape[0]
        turned = jnp.transpose(win_acc[...])
        rows = turned.shape[0] // parts
        for p in range(parts):
            dw_ref[p, :rows, :] = turned[p * rows : (p + 1) * rows]
            dw_ref[p, rows:, :] = wout_acc[8 * (p // 2) : 8 * (p // 2) + 8, 256 * (p % 2) : 256 * (p % 2) + 256]
        for at in range(HEADS):
            pltpu.make_async_copy(sent.at[at], outs[at], sems.at[at]).wait()


def rows_kernel(*refs):
    got = refs[:HEADS]
    win_ref, gain_ref, fetched_ref, cot_ref, row_ref, out_hbm, gated_hbm, whole, gated_ref, out_ref, sems = refs[HEADS:]
    d = HEAD_DIM
    width = fetched_ref.shape[1]
    me = lax.axis_index("seq")
    own = pl.multiple_of(me * d, d)
    targets = [whole.at[pl.ds(block * width + own, d)] for block in ORDER] + [gated_ref.at[pl.ds(own, d)]]
    loads = [
        pltpu.make_async_copy(got[0].at[pl.ds(at * d, d)], target, sems.at[5 + at]) for at, target in enumerate(targets)
    ]
    for load in loads:
        load.start()
    for s in range(1, HEADS):
        at_head = pl.multiple_of(lax.rem(me + HEADS - s, HEADS) * d, d)
        for at, block in enumerate(ORDER):
            whole[pl.ds(block * width + at_head, d), :] = got[s][at * d : (at + 1) * d, :]
        gated_ref[pl.ds(at_head, d), :] = got[s][4 * d :, :]
    for load in loads:
        load.wait()
    copies = [pltpu.make_async_copy(gated_ref, gated_hbm, sems.at[0])]
    copies[0].start()
    dxin = jnp.transpose(mm(win_ref[...], whole[...]))
    normed, inverse = normalize(fetched_ref[...].astype(f32))
    f = dxin * gain_ref[...]
    drow = inverse * (
        f - jnp.mean(f, axis=-1, keepdims=True) - normed * jnp.mean(f * normed, axis=-1, keepdims=True)
    ) + cot_ref[...].astype(f32)
    drow = drow.astype(bf16)
    slots = out_ref.shape[0]
    count = drow.shape[0]
    block = slots // 4
    for at in range(4):
        pick = jnp.where(row_ref[0:1, :] == iota((block, count), 0) + at * block, 1.0, 0.0).astype(bf16)
        here = pl.ds(at * block, block)
        out_ref[here, :] = mm(pick, drow).astype(bf16)
        copies.append(pltpu.make_async_copy(out_ref.at[here], out_hbm.at[here], sems.at[at + 1]))
        copies[-1].start()
    for copy in copies:
        copy.wait()


def table_kernel(row_ref, got_ref, out_ref):
    block = out_ref.shape[0]
    slots = got_ref.shape[0]
    at = pl.program_id(0) * block
    pick = jnp.where(row_ref[0:1, :] == iota((block, slots), 0) + at, 1.0, 0.0).astype(bf16)
    out_ref[...] = mm(pick, got_ref[...])


def weights_kernel(got_ref, win_ref, wout_ref):
    d = HEAD_DIM
    parts = got_ref.shape[1]
    rows = win_ref.shape[0] // parts
    width = win_ref.shape[1] // 4
    for p in range(parts):
        here = slice(p * rows, (p + 1) * rows)
        for at, block in enumerate(ORDER):
            for pair in range(HEADS // 2):
                left = got_ref[2 * pair, p, :rows, at * d : (at + 1) * d].astype(f32)
                right = got_ref[2 * pair + 1, p, :rows, at * d : (at + 1) * d].astype(f32)
                start = block * width + pair * 2 * d
                win_ref[here, start : start + 2 * d] = jnp.concatenate([left, right], axis=1)
        for h in range(HEADS):
            wout_ref[h, p // 2, :, 256 * (p % 2) : 256 * (p % 2) + 256] = got_ref[h, p, rows:, :].astype(f32)


def exchange(x, axis):
    return lax.all_to_all(x, axis, split_axis=0, concat_axis=0, tiled=True)


def struct(shape, dtype):
    return jax.ShapeDtypeStruct(shape, dtype)


def layer_step(item_table, item_ids, segment_ids, weight_in, weight_out, gain_in, gain_mid, cotangent):
    shard_rows, width = item_table.shape
    count = item_ids.shape[1]
    users, seq = lax.axis_size("users"), lax.axis_size("seq")
    devices = users * seq
    length = count * seq
    d = HEAD_DIM
    slots = devices * SLOTS
    upstream = cotangent[0]
    gain_row = gain_in.reshape(1, width)
    head = lax.axis_index("seq")

    cot_all = lax.all_gather(upstream, "seq", axis=0, tiled=True)
    wanted, slot_row, slot_col = call(
        functools.partial(slots_kernel, shard_rows),
        (struct((devices, 128), i32), struct((8, count), i32), struct((count, 128), i32)),
        (item_ids, segment_ids),
        flops=2 * devices * count * count, moved=1 << 19,
    )
    asked = exchange(wanted.reshape(devices, 1, 128), BOTH).reshape(devices, 128)
    steps = 4
    whole = lambda *shape: pl.BlockSpec(shape, lambda g: (0,) * len(shape))
    smem = pl.BlockSpec(memory_space=pltpu.SMEM)
    served, asked_row, bounds, gain_h = call(
        serve_kernel,
        (struct((slots, width), bf16), struct((8, slots), i32), struct((8, 128), i32), struct((d, 128), f32)),
        (asked, item_table, gain_mid.reshape(1, width)),
        grid=(steps,),
        in_specs=[whole(devices, 128), pl.BlockSpec(memory_space=pl.ANY), whole(1, width)],
        out_specs=[
            pl.BlockSpec((slots // steps, width), lambda g: (g, 0)), whole(8, slots), whole(8, 128), whole(d, 128),
        ],
        scratch=[
            pltpu.VMEM((slots, 128), f32), pltpu.VMEM((width, 128), f32), pltpu.VMEM((shard_rows, width), bf16),
            pltpu.SemaphoreType.DMA((4,)),
        ],
        flops=2 * slots * shard_rows * width, moved=4 << 20,
    )
    got = exchange(served.reshape(devices, SLOTS, width), BOTH).reshape(slots, width)
    fetched, xin = call(
        arrange_kernel,
        (struct((count, width), bf16), struct((count, width), bf16)),
        (got, slot_col, gain_row),
        flops=2 * count * slots * width, moved=2 << 20,
    )
    xin_all = lax.all_gather(xin, "seq", axis=0, tiled=True)

    mine = lax.dynamic_index_in_dim(weight_in.reshape(width, 4, HEADS, d), head, 2, keepdims=False)
    win_t = jnp.stack([mine[:, b] for b in ORDER], axis=1).reshape(width, 4 * d).T
    wout_h = lax.dynamic_slice_in_dim(weight_out, head * d, d, axis=0)

    blocks = length // BLOCK
    lane = lambda rows: pl.BlockSpec((rows, BLOCK), lambda g: (0, g))
    rowed = lambda columns: pl.BlockSpec((BLOCK, columns), lambda g: (g, 0))
    dg = mm_nt(wout_h, cot_all)
    q_t, k_t, vk, slope, u, mixed, stats = call(
        forward_kernel,
        (
            struct((d, length), bf16), struct((d, length), bf16), struct((length, 2 * d), bf16),
            struct((4 * d, length), f32), struct((d, length), f32),
            struct((d, length), f32), struct((seq, 4, length), f32),
        ),
        (xin_all, dg, win_t, gain_h, bounds),
        mib=60, grid=(blocks,),
        in_specs=[rowed(width), lane(d), whole(4 * d, width), whole(d, 128), smem],
        out_specs=[lane(d), lane(d), rowed(2 * d), lane(4 * d), lane(d), lane(d),
            pl.BlockSpec((seq, 4, BLOCK), lambda g: (0, 0, g)),
        ],
        scratch=[pltpu.VMEM((2 * d, BLOCK), bf16), pltpu.VMEM((d, length), bf16), pltpu.VMEM((length, 2 * d), bf16)],
        flops=1 << 33, moved=12 << 20,
    )
    stats_all = exchange(stats, "seq")

    early = lambda g: jnp.minimum(g, blocks - 1)
    fixed = lambda *shape: pl.BlockSpec(shape, lambda g, b: (0,) * len(shape))
    lanes = lambda rows: pl.BlockSpec((rows, BLOCK), lambda g, b: (0, early(g)))
    rows = width // users
    result = pl.pallas_call(
        functools.partial(backward_kernel, blocks),
        out_shape=[struct((5 * d, count), bf16)] * HEADS + [struct((users, rows + 8, 4 * d), f32)],
        grid_spec=pltpu.PrefetchScalarGridSpec(
            num_scalar_prefetch=1,
            grid=(blocks + 1,),
            in_specs=[
                lanes(d), lanes(d), pl.BlockSpec((BLOCK, 2 * d), lambda g, b: (early(g), 0)),
                pl.BlockSpec((seq, 4, BLOCK), lambda g, b: (0, 0, early(g))),
                lanes(d), lanes(d), lanes(d), fixed(d, 128),
                *[pl.BlockSpec(memory_space=pl.ANY)] * 3,
            ],
            out_specs=[pl.BlockSpec(memory_space=pl.ANY)] * HEADS + [fixed(users, rows + 8, 4 * d)],
            scratch_shapes=[
                pltpu.VMEM((d, length), bf16), pltpu.VMEM((length, 2 * d), bf16), pltpu.VMEM((d, length), bf16),
                pltpu.VMEM((d, length), f32), pltpu.VMEM((d, length), f32), pltpu.VMEM((d, length), f32),
                pltpu.VMEM((d, length), f32), pltpu.VMEM((4 * d, width), f32), pltpu.VMEM((d, width), f32),
                pltpu.VMEM((HEADS, 5 * d, count), bf16), pltpu.SemaphoreType.DMA((HEADS,)),
                pltpu.VMEM((2 * d, BLOCK), bf16), pltpu.VMEM((2 * d, BLOCK), bf16),
                *[pltpu.VMEM((TILE, TILE), f32)] * 4,
                pltpu.VMEM((length, width), bf16), pltpu.VMEM((length, width), bf16), pltpu.VMEM((4 * d, length), f32),
                pltpu.SemaphoreType.DMA((3,)),
            ],
        ),
        name="backward",
        compiler_params=pltpu.CompilerParams(
            vmem_limit_bytes=60 * 1024 * 1024, dimension_semantics=("arbitrary",)
        ),
        cost_estimate=pl.CostEstimate(flops=1 << 35, bytes_accessed=16 << 20, transcendentals=0),
    )(bounds, q_t, k_t, vk, stats_all, mixed, dg, u, gain_h, xin_all, cot_all, slope)
    dw = result[HEADS]
    pieces = [result[0]]
    for s in range(1, seq):
        pieces.append(lax.ppermute(result[s], "seq", [(i, (i + s) % seq) for i in range(seq)]))
    dw_got = exchange(dw, "users")
    dw_sum = jnp.sum(dw_got, axis=0).astype(bf16)
    dw_wide = jnp.broadcast_to(dw_sum[None], (users, rows + 8, 4 * d))
    dw_head = exchange(dw_wide, "users")
    dw_all = lax.all_gather(dw_head, "seq", axis=0, tiled=False)
    outgoing, gated_mine = call(
        rows_kernel,
        (pltpu.HBM((slots, width), bf16), pltpu.HBM((width, count), bf16)),
        (*pieces, weight_in, gain_row, fetched, upstream, slot_row),
        mib=24, in_specs=[pl.BlockSpec(memory_space=pl.ANY)] + [pl.BlockSpec(memory_space=pltpu.VMEM)] * (HEADS + 4),
        out_specs=[pl.BlockSpec(memory_space=pltpu.HBM)] * 2,
        scratch=[
            pltpu.VMEM((4 * width, count), bf16), pltpu.VMEM((width, count), bf16), pltpu.VMEM((slots, width), bf16),
            pltpu.SemaphoreType.DMA((10,)),
        ],
        flops=2 * count * width * 4 * width, moved=6 << 20,
    )
    layer = (
        fetched.astype(f32)
        + lax.dot_general(gated_mine, weight_out, (((0,), (0,)), ((), ())), preferred_element_type=f32)
    ).astype(bf16)
    incoming = exchange(outgoing.reshape(devices, SLOTS, width), BOTH)
    incoming = incoming.reshape(slots, width)
    tiles = 8
    table_grad = call(
        table_kernel,
        struct((shard_rows, width), f32),
        (asked_row, incoming),
        mib=24, grid=(tiles,),
        in_specs=[whole(8, slots), pl.BlockSpec(memory_space=pltpu.VMEM)],
        out_specs=pl.BlockSpec((shard_rows // tiles, width), lambda g: (g, 0)),
        flops=2 * slots * shard_rows * width, moved=6 << 20,
    )
    group = 4
    win_grad, wout_grad = call(
        weights_kernel,
        (struct((width, 4 * width), f32), struct((HEADS, width // d, 8, width), f32)),
        (dw_all,),
        grid=(users // group,),
        in_specs=[pl.BlockSpec((seq, group, rows + 8, 4 * d), lambda g: (0, g, 0, 0))],
        out_specs=[
            pl.BlockSpec((group * rows, 4 * width), lambda g: (g, 0)),
            pl.BlockSpec((HEADS, group // 2, 8, width), lambda g: (0, g, 0, 0)),
        ],
        flops=1 << 20, moved=8 << 20,
    )
    return (layer[None], table_grad, win_grad, wout_grad.reshape(width, width))


def solution(mesh):
    in_specs = (
        P(BOTH, None),
        P("users", "seq"),
        P("users", "seq"),
        P(),
        P(),
        P(),
        P(),
        P("users", "seq", None),
    )
    out_specs = (P("users", "seq", None), P(BOTH, None), P(), P())
    return jax.shard_map(layer_step, mesh=mesh, in_specs=in_specs, out_specs=out_specs, check_vma=False)
```

```python
import functools
import jax
import jax.numpy as jnp
from jax import lax
from jax.experimental import pallas as pl
from jax.experimental.pallas import tpu as pltpu
from jax.sharding import PartitionSpec as P


HEADS = 8
HEAD_DIM = 64
SLOTS = 8
CAP = 6
BLOCK = 768
TILE = 256
EPSILON = 1e-05
BOTH = ("users", "seq")
ORDER = (0, 2, 1, 3)

f32 = jnp.float32
bf16 = jnp.bfloat16
i32 = jnp.int32


def iota(shape, dim):
    return lax.broadcasted_iota(i32, shape, dim)


def mm(a, b):
    return jnp.dot(a, b, preferred_element_type=f32)


def mm_nt(a, b):
    return lax.dot_general(a, b, (((1,), (1,)), ((), ())), preferred_element_type=f32)


def call(kernel, out_shape, args, *, grid=None, in_specs=None, out_specs=None, scratch=(), flops=0, moved=0, mib=60):
    params = dict(vmem_limit_bytes=mib * 1024 * 1024)
    extra = {}
    if grid is not None:
        params["dimension_semantics"] = ("arbitrary",) * len(grid)
        extra["grid"] = grid
    if in_specs is not None:
        extra["in_specs"] = in_specs
    if out_specs is not None:
        extra["out_specs"] = out_specs
    return pl.pallas_call(
        kernel,
        out_shape=out_shape,
        scratch_shapes=scratch,
        compiler_params=pltpu.CompilerParams(**params),
        cost_estimate=pl.CostEstimate(flops=flops, bytes_accessed=moved, transcendentals=0),
        **extra,
    )(*args)


def normalize(values):
    centred = values - jnp.mean(values, axis=-1, keepdims=True)
    inverse = lax.rsqrt(jnp.mean(centred * centred, axis=-1, keepdims=True) + EPSILON)
    return centred * inverse, inverse


def slots_kernel(shard_rows, ids_ref, seg_ref, wanted_ref, row_ref, col_ref):
    devices, lanes = wanted_ref.shape
    count = ids_ref.shape[1]
    ids = ids_ref[...]
    owner = lax.shift_right_logical(ids, shard_rows.bit_length() - 1)
    local = (ids & (shard_rows - 1)).astype(f32)
    held = owner == iota((devices, count), 0)
    hit = jnp.where(held, 1.0, 0.0)
    earlier = jnp.where(iota((count, count), 0) < iota((count, count), 1), 1.0, 0.0)
    rank = mm(hit.astype(bf16), earlier.astype(bf16))
    marked = jnp.where(held, rank, -1.0)
    lane = iota((devices, lanes), 1)
    wanted = jnp.zeros((devices, lanes), f32)
    for c in range(CAP):
        column = jnp.sum(jnp.where(marked == float(c), local, 0.0), axis=1, keepdims=True)
        wanted = jnp.where(lane == c, column, wanted)
    seg = seg_ref[...]
    below1 = jnp.sum(jnp.where(seg < 1, 1.0, 0.0), axis=1, keepdims=True)
    below2 = jnp.sum(jnp.where(seg < 2, 1.0, 0.0), axis=1, keepdims=True)
    wanted = jnp.where(lane == CAP, below1, wanted)
    wanted = jnp.where(lane == CAP + 1, below2, wanted)
    wanted_ref[...] = wanted.astype(i32)
    slot = owner.astype(f32) * float(SLOTS) + jnp.sum(hit * rank, axis=0, keepdims=True)
    row_ref[...] = jnp.broadcast_to(slot, row_ref.shape).astype(i32)
    col_ref[...] = jnp.transpose(jnp.broadcast_to(slot, (lanes, count))).astype(i32)


def serve_kernel(asked_ref, table_ref, gain_ref, served_ref, row_ref, bounds_ref, mid_ref, col_ref, turn_ref):
    step = pl.program_id(0)
    block = served_ref.shape[0]
    devices, lanes = asked_ref.shape

    @pl.when(step == 0)
    def _():
        asked = asked_ref[...].astype(f32)
        wide = jnp.broadcast_to(asked[:, None, :], (devices, SLOTS, lanes))
        sub = iota((devices, SLOTS, lanes), 1)
        lane = iota((devices, SLOTS, lanes), 2)
        column = jnp.sum(jnp.where(sub == lane, wide, 0.0), axis=2, keepdims=True)
        column = jnp.where(iota((devices, SLOTS, 1), 1) < CAP, column, -1.0)
        column = jnp.broadcast_to(column, (devices, SLOTS, lanes)).reshape(devices * SLOTS, lanes)
        col_ref[...] = column
        row_ref[...] = jnp.transpose(column)[: row_ref.shape[0]].astype(i32)
        group = lax.axis_index("users")
        mine = lax.div(iota((devices, lanes), 0), SLOTS) == group
        bounds = jnp.sum(jnp.where(mine, asked, 0.0), axis=0, keepdims=True)
        bounds = jnp.broadcast_to(bounds, bounds_ref.shape).astype(i32)
        me = lax.axis_index("seq")
        bounds_ref[...] = jnp.where(iota(bounds_ref.shape, 1) == SLOTS, me, bounds)
        turn_ref[...] = jnp.transpose(jnp.broadcast_to(gain_ref[...], (lanes, gain_ref.shape[1])))
        d = mid_ref.shape[0]
        mid_ref[...] = turn_ref[pl.ds(pl.multiple_of(me * d, d), d), :]

    column = col_ref[pl.ds(pl.multiple_of(step * block, block), block), :].astype(i32)
    parts = []
    for at in range(table_ref.shape[0] // lanes):
        parts.append(jnp.where(column == iota((block, lanes), 1) + at * lanes, 1.0, 0.0).astype(bf16))
    served_ref[...] = mm(jnp.concatenate(parts, axis=1), table_ref[...]).astype(bf16)


def arrange_kernel(got_ref, col_ref, gain_ref, fetched_hbm, xin_hbm, fetched_ref, xin_ref, sems):
    slot = col_ref[...]
    count, lanes = slot.shape
    parts = []
    for at in range(got_ref.shape[0] // lanes):
        parts.append(jnp.where(slot == iota((count, lanes), 1) + at * lanes, 1.0, 0.0).astype(bf16))
    fetched = mm(jnp.concatenate(parts, axis=1), got_ref[...])
    fetched_ref[...] = fetched.astype(bf16)
    normed, _ = normalize(fetched)
    xin_ref[...] = (normed * gain_ref[...]).astype(bf16)
    copies = [
        pltpu.make_async_copy(xin_ref, xin_hbm, sems.at[0]), pltpu.make_async_copy(fetched_ref, fetched_hbm, sems.at[1]),
    ]
    for copy in copies:
        copy.start()
    for copy in copies:
        copy.wait()


def seg_start(position, one, two):
    return jnp.where(position < one, 0, jnp.where(position < two, one, two))


def visible(i, j, one, two, block):
    where_q = iota((1, block), 1) + i * block
    start = seg_start(where_q, one, two)
    where_k = iota((block, block), 0) + j * block
    return (where_k >= start) & (where_k <= where_q)


def pair_of(p, base, one, two):
    first = lax.div(seg_start(base * TILE, one, two), TILE)
    i, j = base, first + p
    passed = base - first + 1
    for step in range(1, BLOCK // TILE):
        first = lax.div(seg_start((base + step) * TILE, one, two), TILE)
        later = p >= passed
        i = jnp.where(later, base + step, i)
        j = jnp.where(later, first + p - passed, j)
        passed = passed + base + step - first + 1
    return i, j, passed


def forward_kernel(
    xin_ref, dg_ref, win_ref, gain_ref, bounds_ref,
    q_ref, k_ref, vk_ref, slope_ref, u_ref, mixed_ref, stats_ref,
    q_all, v_all, vk_all,
):
    i = pl.program_id(0)
    one, two = bounds_ref[0, CAP], bounds_ref[0, CAP + 1]
    here = pl.ds(pl.multiple_of(i * BLOCK, BLOCK), BLOCK)
    pre = mm_nt(win_ref[...], xin_ref[...])
    tanh = jnp.tanh(pre * 0.5)
    plus = 1.0 + tanh
    hidden = (0.5 * pre) * plus
    slope_ref[...] = 0.5 * (plus + hidden * (1.0 - tanh))
    d = HEAD_DIM
    u = hidden[:d]
    query = (hidden[d : 2 * d].astype(bf16).astype(f32) * 0.0625).astype(bf16)
    vk = hidden[2 * d :]
    vk_t = vk.astype(bf16)
    turned = jnp.transpose(vk).astype(bf16)
    u_ref[...] = u
    q_ref[...] = query
    k_ref[...] = vk_t[d:]
    vk_ref[...] = turned
    q_all[:d, :] = jnp.zeros((d, BLOCK), bf16)
    q_all[d:, :] = query
    v_all[:, here] = vk_t[:d]
    vk_all[here, :] = turned
    mixed_ref[...] = jnp.zeros(mixed_ref.shape, f32)

    def pair(j, carry):
        there = pl.ds(pl.multiple_of(j * BLOCK, BLOCK), BLOCK)
        half = mm(vk_all[there, :], q_all[...])
        weights = half + half * jnp.tanh(half)
        weights = jnp.where(visible(i, j, one, two, BLOCK), weights, 0.0).astype(bf16)
        mixed_ref[...] += mm(v_all[:, there], weights)
        return carry

    first = lax.div(seg_start(i * BLOCK, one, two), BLOCK)
    lax.fori_loop(first, i + 1, pair, 0)
    dg = dg_ref[...]
    mixed = mixed_ref[...]
    e = dg * u * gain_ref[:, :1]
    mean = jnp.sum(mixed, axis=0, keepdims=True) * (1.0 / d)
    centred = mixed - mean
    spread = jnp.sum(centred * centred, axis=0, keepdims=True)
    sum_e = jnp.sum(e, axis=0, keepdims=True)
    sum_em = jnp.sum(e * centred, axis=0, keepdims=True)
    for h in range(HEADS):
        stats_ref[h, 0:1, :] = mean
        stats_ref[h, 1:2, :] = spread
        stats_ref[h, 2:3, :] = sum_e
        stats_ref[h, 3:4, :] = sum_em


def middle(stats, mixed, dg, u, gain):
    width = HEADS * HEAD_DIM
    means = [stats[h, 0:1] for h in range(HEADS)]
    mean = functools.reduce(jnp.add, means) * (1.0 / HEADS)
    var, m_e, m_em = 0.0, 0.0, 0.0
    for h in range(HEADS):
        off = means[h] - mean
        var = var + stats[h, 1:2] + HEAD_DIM * off * off
        m_e = m_e + stats[h, 2:3]
        m_em = m_em + stats[h, 3:4] + off * stats[h, 2:3]
    inverse = lax.rsqrt(var * (1.0 / width) + EPSILON)
    m_e = m_e * (1.0 / width)
    m_eh = m_em * inverse * (1.0 / width)
    hat = (mixed - mean) * inverse
    scaled = hat * gain
    e = dg * u * gain
    up = (inverse * (e - m_e - hat * m_eh)).astype(bf16)
    return (scaled * u).astype(bf16), (up.astype(f32) * 0.0625).astype(bf16), dg * scaled


def backward_kernel(
    steps, bounds_ref, q_ref, k_ref, vk_ref, stats_ref, mixed_ref, dg_ref, u_ref, gain_ref, xin_hbm, cot_hbm, slope_hbm,
    *rest,
):
    outs, rest = rest[:HEADS], rest[HEADS:]
    dw_ref, k_all, vk_all, gated_all, du_all, dq_all, dk_all, dv_all, win_acc, wout_acc, sent, sems = rest[:12]
    query2, up2, half0, upper0, half1, upper1, xin_ref, cot_ref, slope_ref, loaded = rest[12:]
    loads = [
        pltpu.make_async_copy(source, target, loaded.at[at])
        for at, (source, target) in enumerate(((xin_hbm, xin_ref), (cot_hbm, cot_ref), (slope_hbm, slope_ref)))
    ]
    g = pl.program_id(0)
    one, two, me = bounds_ref[0, CAP], bounds_ref[0, CAP + 1], bounds_ref[0, SLOTS]
    d = HEAD_DIM

    @pl.when(g == 0)
    def _():
        for load in loads:
            load.start()
        dk_all[...] = jnp.zeros(dk_all.shape, f32)
        dv_all[...] = jnp.zeros(dv_all.shape, f32)
        dq_all[...] = jnp.zeros(dq_all.shape, f32)
        win_acc[...] = jnp.zeros(win_acc.shape, f32)
        wout_acc[...] = jnp.zeros(wout_acc.shape, f32)
        query2[...] = jnp.zeros(query2.shape, bf16)
        up2[...] = jnp.zeros(up2.shape, bf16)

    @pl.when(g < steps)
    def _():
        here = pl.ds(pl.multiple_of(g * BLOCK, BLOCK), BLOCK)
        gated, up, du = middle(stats_ref[...], mixed_ref[...], dg_ref[...], u_ref[...], gain_ref[:, :1])
        gated_all[:, here] = gated
        du_all[:, here] = du
        k_all[:, here] = k_ref[...]
        vk_all[here, :] = vk_ref[...]
        query2[d:, :] = q_ref[...]
        up2[:d, :] = up
        base = g * (BLOCK // TILE)
        total = pair_of(0, base, one, two)[2]

        def front(i, j):
            at = pl.ds(pl.multiple_of((i - base) * TILE, TILE), TILE)
            vk = vk_all[pl.ds(pl.multiple_of(j * TILE, TILE), TILE), :]
            return mm(vk, query2[:, at]), mm(vk, up2[:, at])

        def back(i, j, half, upper, live):
            at = pl.ds(pl.multiple_of((i - base) * TILE, TILE), TILE)
            here = pl.ds(pl.multiple_of(i * TILE, TILE), TILE)
            there = pl.ds(pl.multiple_of(j * TILE, TILE), TILE)
            tanh = jnp.tanh(half)
            plus = 1.0 + tanh
            weights = half * plus
            dscores = upper * (plus + weights * (1.0 - tanh))
            seen = visible(i, jnp.where(live, j, dq_all.shape[1]), one, two, TILE)
            weights = jnp.where(seen, weights, 0.0).astype(bf16)
            dscores = jnp.where(seen, dscores, 0.0).astype(bf16)
            dv_all[:, there] += mm_nt(up2[:d, at], weights)
            dk_all[:, there] += mm_nt(query2[d:, at], dscores)
            dq_all[:, here] += mm(k_all[:, there], dscores)

        half0[...], upper0[...] = front(*pair_of(0, base, one, two)[:2])

        def two_pairs(t, carry):
            p = 2 * t
            now, odd, after = [
                pair_of(jnp.minimum(p + step, total - 1), base, one, two)[:2] for step in range(3)
            ]
            half1[...], upper1[...] = front(*odd)
            back(*now, half0[...], upper0[...], True)
            half0[...], upper0[...] = front(*after)
            back(*odd, half1[...], upper1[...], p + 1 < total)
            return carry

        lax.fori_loop(0, lax.div(total + 1, 2), two_pairs, 0)

    @pl.when(g == steps)
    def _():
        for load in loads:
            load.wait()
        count = sent.shape[2]
        for s in range(HEADS):
            start = pl.multiple_of(lax.rem(me + s, HEADS) * count, 128)
            here = pl.ds(start, count)
            gated = gated_all[:, here]
            dpre = jnp.concatenate(
                [
                    (du_all[:, here] * slope_ref[:d, here]).astype(bf16),
                    (dq_all[:, here] * slope_ref[d : 2 * d, here]).astype(bf16),
                    (dv_all[:, here] * 16.0 * slope_ref[2 * d : 3 * d, here]).astype(bf16),
                    (dk_all[:, here] * 16.0 * slope_ref[3 * d :, here]).astype(bf16),
                ],
                axis=0,
            )
            sent[s, : 4 * d, :] = dpre
            sent[s, 4 * d :, :] = gated
            pltpu.make_async_copy(sent.at[s], outs[s], sems.at[s]).start()
            win_acc[...] += mm(dpre, xin_ref[here, :])
            wout_acc[...] += mm(gated, cot_ref[here, :])
        parts = dw_ref.shape[0]
        turned = jnp.transpose(win_acc[...])
        rows = turned.shape[0] // parts
        for p in range(parts):
            dw_ref[p, :rows, :] = turned[p * rows : (p + 1) * rows]
            dw_ref[p, rows:, :] = wout_acc[8 * (p // 2) : 8 * (p // 2) + 8, 256 * (p % 2) : 256 * (p % 2) + 256]
        for at in range(HEADS):
            pltpu.make_async_copy(sent.at[at], outs[at], sems.at[at]).wait()


def rows_kernel(*refs):
    got = refs[:HEADS]
    win_ref, gain_ref, fetched_ref, cot_ref, row_ref, out_hbm, gated_hbm, whole, gated_ref, out_ref, sems = refs[HEADS:]
    d = HEAD_DIM
    width = fetched_ref.shape[1]
    me = lax.axis_index("seq")
    own = pl.multiple_of(me * d, d)
    targets = [whole.at[pl.ds(block * width + own, d)] for block in ORDER] + [gated_ref.at[pl.ds(own, d)]]
    loads = [
        pltpu.make_async_copy(got[0].at[pl.ds(at * d, d)], target, sems.at[5 + at]) for at, target in enumerate(targets)
    ]
    for load in loads:
        load.start()
    for s in range(1, HEADS):
        at_head = pl.multiple_of(lax.rem(me + HEADS - s, HEADS) * d, d)
        for at, block in enumerate(ORDER):
            whole[pl.ds(block * width + at_head, d), :] = got[s][at * d : (at + 1) * d, :]
        gated_ref[pl.ds(at_head, d), :] = got[s][4 * d :, :]
    for load in loads:
        load.wait()
    copies = [pltpu.make_async_copy(gated_ref, gated_hbm, sems.at[0])]
    copies[0].start()
    dxin = jnp.transpose(mm(win_ref[...], whole[...]))
    normed, inverse = normalize(fetched_ref[...].astype(f32))
    f = dxin * gain_ref[...]
    drow = inverse * (
        f - jnp.mean(f, axis=-1, keepdims=True) - normed * jnp.mean(f * normed, axis=-1, keepdims=True)
    ) + cot_ref[...].astype(f32)
    drow = drow.astype(bf16)
    slots = out_ref.shape[0]
    count = drow.shape[0]
    block = slots // 4
    for at in range(4):
        pick = jnp.where(row_ref[0:1, :] == iota((block, count), 0) + at * block, 1.0, 0.0).astype(bf16)
        here = pl.ds(at * block, block)
        out_ref[here, :] = mm(pick, drow).astype(bf16)
        copies.append(pltpu.make_async_copy(out_ref.at[here], out_hbm.at[here], sems.at[at + 1]))
        copies[-1].start()
    for copy in copies:
        copy.wait()


def table_kernel(row_ref, got_ref, out_ref):
    block = out_ref.shape[0]
    slots = got_ref.shape[0]
    at = pl.program_id(0) * block
    pick = jnp.where(row_ref[0:1, :] == iota((block, slots), 0) + at, 1.0, 0.0).astype(bf16)
    out_ref[...] = mm(pick, got_ref[...])


def weights_kernel(got_ref, win_ref, wout_ref):
    d = HEAD_DIM
    parts = got_ref.shape[1]
    rows = win_ref.shape[0] // parts
    width = win_ref.shape[1] // 4
    for p in range(parts):
        here = slice(p * rows, (p + 1) * rows)
        for at, block in enumerate(ORDER):
            for pair in range(HEADS // 2):
                left = got_ref[2 * pair, p, :rows, at * d : (at + 1) * d].astype(f32)
                right = got_ref[2 * pair + 1, p, :rows, at * d : (at + 1) * d].astype(f32)
                start = block * width + pair * 2 * d
                win_ref[here, start : start + 2 * d] = jnp.concatenate([left, right], axis=1)
        for h in range(HEADS):
            wout_ref[h, p // 2, :, 256 * (p % 2) : 256 * (p % 2) + 256] = got_ref[h, p, rows:, :].astype(f32)


def exchange(x, axis):
    return lax.all_to_all(x, axis, split_axis=0, concat_axis=0, tiled=True)


def struct(shape, dtype):
    return jax.ShapeDtypeStruct(shape, dtype)


def layer_step(item_table, item_ids, segment_ids, weight_in, weight_out, gain_in, gain_mid, cotangent):
    shard_rows, width = item_table.shape
    count = item_ids.shape[1]
    users, seq = lax.axis_size("users"), lax.axis_size("seq")
    devices = users * seq
    length = count * seq
    d = HEAD_DIM
    slots = devices * SLOTS
    upstream = cotangent[0]
    gain_row = gain_in.reshape(1, width)
    head = lax.axis_index("seq")

    cot_all = lax.all_gather(upstream, "seq", axis=0, tiled=True)
    wanted, slot_row, slot_col = call(
        functools.partial(slots_kernel, shard_rows),
        (struct((devices, 128), i32), struct((8, count), i32), struct((count, 128), i32)),
        (item_ids, segment_ids),
        flops=2 * devices * count * count, moved=1 << 19,
    )
    asked = exchange(wanted.reshape(devices, 1, 128), BOTH).reshape(devices, 128)
    steps = 4
    whole = lambda *shape: pl.BlockSpec(shape, lambda g: (0,) * len(shape))
    smem = pl.BlockSpec(memory_space=pltpu.SMEM)
    served, asked_row, bounds, gain_h = call(
        serve_kernel,
        (struct((slots, width), bf16), struct((8, slots), i32), struct((8, 128), i32), struct((d, 128), f32)),
        (asked, item_table, gain_mid.reshape(1, width)),
        grid=(steps,),
        in_specs=[whole(devices, 128), whole(shard_rows, width), whole(1, width)],
        out_specs=[
            pl.BlockSpec((slots // steps, width), lambda g: (g, 0)), whole(8, slots), whole(8, 128), whole(d, 128),
        ],
        scratch=[pltpu.VMEM((slots, 128), f32), pltpu.VMEM((width, 128), f32)],
        flops=2 * slots * shard_rows * width, moved=4 << 20,
    )
    got = exchange(served.reshape(devices, SLOTS, width), BOTH).reshape(slots, width)
    fetched, xin = call(
        arrange_kernel,
        (pltpu.HBM((count, width), bf16), pltpu.HBM((count, width), bf16)),
        (got, slot_col, gain_row),
        mib=24, in_specs=[pl.BlockSpec(memory_space=pltpu.VMEM)] * 3,
        out_specs=[pl.BlockSpec(memory_space=pltpu.HBM)] * 2,
        scratch=[
            pltpu.VMEM((count, width), bf16), pltpu.VMEM((count, width), bf16), pltpu.SemaphoreType.DMA((2,)),
        ], flops=2 * count * slots * width, moved=2 << 20,
    )
    xin_all = lax.all_gather(xin, "seq", axis=0, tiled=True)

    mine = lax.dynamic_index_in_dim(weight_in.reshape(width, 4, HEADS, d), head, 2, keepdims=False)
    win_t = jnp.stack([mine[:, b] for b in ORDER], axis=1).reshape(width, 4 * d).T
    wout_h = lax.dynamic_slice_in_dim(weight_out, head * d, d, axis=0)

    blocks = length // BLOCK
    lane = lambda rows: pl.BlockSpec((rows, BLOCK), lambda g: (0, g))
    rowed = lambda columns: pl.BlockSpec((BLOCK, columns), lambda g: (g, 0))
    dg = mm_nt(wout_h, cot_all)
    q_t, k_t, vk, slope, u, mixed, stats = call(
        forward_kernel,
        (
            struct((d, length), bf16), struct((d, length), bf16), struct((length, 2 * d), bf16),
            struct((4 * d, length), f32), struct((d, length), f32),
            struct((d, length), f32), struct((seq, 4, length), f32),
        ),
        (xin_all, dg, win_t, gain_h, bounds),
        mib=60, grid=(blocks,),
        in_specs=[rowed(width), lane(d), whole(4 * d, width), whole(d, 128), smem],
        out_specs=[lane(d), lane(d), rowed(2 * d), lane(4 * d), lane(d), lane(d),
            pl.BlockSpec((seq, 4, BLOCK), lambda g: (0, 0, g)),
        ],
        scratch=[pltpu.VMEM((2 * d, BLOCK), bf16), pltpu.VMEM((d, length), bf16), pltpu.VMEM((length, 2 * d), bf16)],
        flops=1 << 33, moved=12 << 20,
    )
    stats_all = exchange(stats, "seq")

    early = lambda g: jnp.minimum(g, blocks - 1)
    fixed = lambda *shape: pl.BlockSpec(shape, lambda g, b: (0,) * len(shape))
    lanes = lambda rows: pl.BlockSpec((rows, BLOCK), lambda g, b: (0, early(g)))
    rows = width // users
    result = pl.pallas_call(
        functools.partial(backward_kernel, blocks),
        out_shape=[struct((5 * d, count), bf16)] * HEADS + [struct((users, rows + 8, 4 * d), f32)],
        grid_spec=pltpu.PrefetchScalarGridSpec(
            num_scalar_prefetch=1,
            grid=(blocks + 1,),
            in_specs=[
                lanes(d), lanes(d), pl.BlockSpec((BLOCK, 2 * d), lambda g, b: (early(g), 0)),
                pl.BlockSpec((seq, 4, BLOCK), lambda g, b: (0, 0, early(g))),
                lanes(d), lanes(d), lanes(d), fixed(d, 128),
                *[pl.BlockSpec(memory_space=pl.ANY)] * 3,
            ],
            out_specs=[pl.BlockSpec(memory_space=pl.ANY)] * HEADS + [fixed(users, rows + 8, 4 * d)],
            scratch_shapes=[
                pltpu.VMEM((d, length), bf16), pltpu.VMEM((length, 2 * d), bf16), pltpu.VMEM((d, length), bf16),
                pltpu.VMEM((d, length), f32), pltpu.VMEM((d, length), f32), pltpu.VMEM((d, length), f32),
                pltpu.VMEM((d, length), f32), pltpu.VMEM((4 * d, width), f32), pltpu.VMEM((d, width), f32),
                pltpu.VMEM((HEADS, 5 * d, count), bf16), pltpu.SemaphoreType.DMA((HEADS,)),
                pltpu.VMEM((2 * d, BLOCK), bf16), pltpu.VMEM((2 * d, BLOCK), bf16),
                *[pltpu.VMEM((TILE, TILE), f32)] * 4,
                pltpu.VMEM((length, width), bf16), pltpu.VMEM((length, width), bf16), pltpu.VMEM((4 * d, length), f32),
                pltpu.SemaphoreType.DMA((3,)),
            ],
        ),
        name="backward",
        compiler_params=pltpu.CompilerParams(
            vmem_limit_bytes=60 * 1024 * 1024, dimension_semantics=("arbitrary",)
        ),
        cost_estimate=pl.CostEstimate(flops=1 << 35, bytes_accessed=16 << 20, transcendentals=0),
    )(bounds, q_t, k_t, vk, stats_all, mixed, dg, u, gain_h, xin_all, cot_all, slope)
    dw = result[HEADS]
    pieces = [result[0]]
    for s in range(1, seq):
        pieces.append(lax.ppermute(result[s], "seq", [(i, (i + s) % seq) for i in range(seq)]))
    dw_got = exchange(dw, "users")
    dw_sum = jnp.sum(dw_got, axis=0).astype(bf16)
    dw_wide = jnp.broadcast_to(dw_sum[None], (users, rows + 8, 4 * d))
    dw_head = exchange(dw_wide, "users")
    dw_all = lax.all_gather(dw_head, "seq", axis=0, tiled=False)
    outgoing, gated_mine = call(
        rows_kernel,
        (pltpu.HBM((slots, width), bf16), pltpu.HBM((width, count), bf16)),
        (pltpu.with_memory_space_constraint(pieces[0], pltpu.HBM), *pieces[1:], weight_in, gain_row, fetched, upstream, slot_row),
        mib=24, in_specs=[pl.BlockSpec(memory_space=pltpu.HBM)] + [pl.BlockSpec(memory_space=pltpu.VMEM)] * (HEADS + 4),
        out_specs=[pl.BlockSpec(memory_space=pltpu.HBM)] * 2,
        scratch=[
            pltpu.VMEM((4 * width, count), bf16), pltpu.VMEM((width, count), bf16), pltpu.VMEM((slots, width), bf16),
            pltpu.SemaphoreType.DMA((10,)),
        ],
        flops=2 * count * width * 4 * width, moved=6 << 20,
    )
    layer = (
        fetched.astype(f32)
        + lax.dot_general(gated_mine, weight_out, (((0,), (0,)), ((), ())), preferred_element_type=f32)
    ).astype(bf16)
    incoming = exchange(outgoing.reshape(devices, SLOTS, width), BOTH)
    incoming = incoming.reshape(slots, width)
    tiles = 8
    table_grad = call(
        table_kernel,
        struct((shard_rows, width), f32),
        (asked_row, incoming),
        mib=24, grid=(tiles,),
        in_specs=[whole(8, slots), pl.BlockSpec(memory_space=pltpu.VMEM)],
        out_specs=pl.BlockSpec((shard_rows // tiles, width), lambda g: (g, 0)),
        flops=2 * slots * shard_rows * width, moved=6 << 20,
    )
    group = 4
    win_grad, wout_grad = call(
        weights_kernel,
        (struct((width, 4 * width), f32), struct((HEADS, width // d, 8, width), f32)),
        (dw_all,),
        grid=(users // group,),
        in_specs=[pl.BlockSpec((seq, group, rows + 8, 4 * d), lambda g: (0, g, 0, 0))],
        out_specs=[
            pl.BlockSpec((group * rows, 4 * width), lambda g: (g, 0)),
            pl.BlockSpec((HEADS, group // 2, 8, width), lambda g: (0, g, 0, 0)),
        ],
        flops=1 << 20, moved=8 << 20,
    )
    return (layer[None], table_grad, win_grad, wout_grad.reshape(width, width))


def solution(mesh):
    in_specs = (
        P(BOTH, None),
        P("users", "seq"),
        P("users", "seq"),
        P(),
        P(),
        P(),
        P(),
        P("users", "seq", None),
    )
    out_specs = (P("users", "seq", None), P(BOTH, None), P(), P())
    return jax.shard_map(layer_step, mesh=mesh, in_specs=in_specs, out_specs=out_specs, check_vma=False)
```

```python
import functools
import jax
import jax.numpy as jnp
from jax import lax
from jax.experimental import pallas as pl
from jax.experimental.pallas import tpu as pltpu
from jax.sharding import PartitionSpec as P


HEADS = 8
HEAD_DIM = 64
SLOTS = 8
CAP = 6
BLOCK = 768
TILE = 256
EPSILON = 1e-05
BOTH = ("users", "seq")
ORDER = (0, 2, 1, 3)

f32 = jnp.float32
bf16 = jnp.bfloat16
i32 = jnp.int32


def iota(shape, dim):
    return lax.broadcasted_iota(i32, shape, dim)


def mm(a, b):
    return jnp.dot(a, b, preferred_element_type=f32)


def mm_nt(a, b):
    return lax.dot_general(a, b, (((1,), (1,)), ((), ())), preferred_element_type=f32)


def call(kernel, out_shape, args, *, grid=None, in_specs=None, out_specs=None, scratch=(), flops=0, moved=0, mib=60):
    params = dict(vmem_limit_bytes=mib * 1024 * 1024)
    extra = {}
    if grid is not None:
        params["dimension_semantics"] = ("arbitrary",) * len(grid)
        extra["grid"] = grid
    if in_specs is not None:
        extra["in_specs"] = in_specs
    if out_specs is not None:
        extra["out_specs"] = out_specs
    return pl.pallas_call(
        kernel,
        out_shape=out_shape,
        scratch_shapes=scratch,
        compiler_params=pltpu.CompilerParams(**params),
        cost_estimate=pl.CostEstimate(flops=flops, bytes_accessed=moved, transcendentals=0),
        **extra,
    )(*args)


def normalize(values):
    centred = values - jnp.mean(values, axis=-1, keepdims=True)
    inverse = lax.rsqrt(jnp.mean(centred * centred, axis=-1, keepdims=True) + EPSILON)
    return centred * inverse, inverse


def slots_kernel(shard_rows, ids_ref, seg_ref, wanted_ref, row_ref, col_ref):
    devices, lanes = wanted_ref.shape
    count = ids_ref.shape[1]
    ids = ids_ref[...]
    owner = lax.shift_right_logical(ids, shard_rows.bit_length() - 1)
    local = (ids & (shard_rows - 1)).astype(f32)
    held = owner == iota((devices, count), 0)
    hit = jnp.where(held, 1.0, 0.0)
    earlier = jnp.where(iota((count, count), 0) < iota((count, count), 1), 1.0, 0.0)
    rank = mm(hit.astype(bf16), earlier.astype(bf16))
    marked = jnp.where(held, rank, -1.0)
    lane = iota((devices, lanes), 1)
    wanted = jnp.zeros((devices, lanes), f32)
    for c in range(CAP):
        column = jnp.sum(jnp.where(marked == float(c), local, 0.0), axis=1, keepdims=True)
        wanted = jnp.where(lane == c, column, wanted)
    seg = seg_ref[...]
    below1 = jnp.sum(jnp.where(seg < 1, 1.0, 0.0), axis=1, keepdims=True)
    below2 = jnp.sum(jnp.where(seg < 2, 1.0, 0.0), axis=1, keepdims=True)
    wanted = jnp.where(lane == CAP, below1, wanted)
    wanted = jnp.where(lane == CAP + 1, below2, wanted)
    wanted_ref[...] = wanted.astype(i32)
    slot = owner.astype(f32) * float(SLOTS) + jnp.sum(hit * rank, axis=0, keepdims=True)
    row_ref[...] = jnp.broadcast_to(slot, row_ref.shape).astype(i32)
    col_ref[...] = jnp.transpose(jnp.broadcast_to(slot, (lanes, count))).astype(i32)


def serve_kernel(asked_ref, table_ref, gain_ref, served_ref, row_ref, bounds_ref, mid_ref, col_ref, turn_ref):
    step = pl.program_id(0)
    block = served_ref.shape[0]
    devices, lanes = asked_ref.shape

    @pl.when(step == 0)
    def _():
        asked = asked_ref[...].astype(f32)
        wide = jnp.broadcast_to(asked[:, None, :], (devices, SLOTS, lanes))
        sub = iota((devices, SLOTS, lanes), 1)
        lane = iota((devices, SLOTS, lanes), 2)
        column = jnp.sum(jnp.where(sub == lane, wide, 0.0), axis=2, keepdims=True)
        column = jnp.where(iota((devices, SLOTS, 1), 1) < CAP, column, -1.0)
        column = jnp.broadcast_to(column, (devices, SLOTS, lanes)).reshape(devices * SLOTS, lanes)
        col_ref[...] = column
        row_ref[...] = jnp.transpose(column)[: row_ref.shape[0]].astype(i32)
        group = lax.axis_index("users")
        mine = lax.div(iota((devices, lanes), 0), SLOTS) == group
        bounds = jnp.sum(jnp.where(mine, asked, 0.0), axis=0, keepdims=True)
        bounds = jnp.broadcast_to(bounds, bounds_ref.shape).astype(i32)
        me = lax.axis_index("seq")
        bounds_ref[...] = jnp.where(iota(bounds_ref.shape, 1) == SLOTS, me, bounds)
        turn_ref[...] = jnp.transpose(jnp.broadcast_to(gain_ref[...], (lanes, gain_ref.shape[1])))
        d = mid_ref.shape[0]
        mid_ref[...] = turn_ref[pl.ds(pl.multiple_of(me * d, d), d), :]

    column = col_ref[pl.ds(pl.multiple_of(step * block, block), block), :].astype(i32)
    parts = []
    for at in range(table_ref.shape[0] // lanes):
        parts.append(jnp.where(column == iota((block, lanes), 1) + at * lanes, 1.0, 0.0).astype(bf16))
    served_ref[...] = mm(jnp.concatenate(parts, axis=1), table_ref[...]).astype(bf16)


def arrange_kernel(got_ref, col_ref, gain_ref, fetched_hbm, xin_hbm, fetched_ref, xin_ref, sems):
    slot = col_ref[...]
    count, lanes = slot.shape
    parts = []
    for at in range(got_ref.shape[0] // lanes):
        parts.append(jnp.where(slot == iota((count, lanes), 1) + at * lanes, 1.0, 0.0).astype(bf16))
    fetched = mm(jnp.concatenate(parts, axis=1), got_ref[...])
    fetched_ref[...] = fetched.astype(bf16)
    normed, _ = normalize(fetched)
    xin_ref[...] = (normed * gain_ref[...]).astype(bf16)
    copies = [
        pltpu.make_async_copy(xin_ref, xin_hbm, sems.at[0]), pltpu.make_async_copy(fetched_ref, fetched_hbm, sems.at[1]),
    ]
    for copy in copies:
        copy.start()
    for copy in copies:
        copy.wait()


def seg_start(position, one, two):
    return jnp.where(position < one, 0, jnp.where(position < two, one, two))


def visible(i, j, one, two, block):
    where_q = iota((1, block), 1) + i * block
    start = seg_start(where_q, one, two)
    where_k = iota((block, block), 0) + j * block
    return (where_k >= start) & (where_k <= where_q)


def pair_of(p, base, one, two):
    first = lax.div(seg_start(base * TILE, one, two), TILE)
    i, j = base, first + p
    passed = base - first + 1
    for step in range(1, BLOCK // TILE):
        first = lax.div(seg_start((base + step) * TILE, one, two), TILE)
        later = p >= passed
        i = jnp.where(later, base + step, i)
        j = jnp.where(later, first + p - passed, j)
        passed = passed + base + step - first + 1
    return i, j, passed


def forward_kernel(
    xin_ref, dg_ref, win_ref, gain_ref, bounds_ref,
    q_ref, k_ref, vk_ref, slope_ref, u_ref, mixed_ref, stats_ref,
    q_all, v_all, vk_all,
):
    i = pl.program_id(0)
    one, two = bounds_ref[0, CAP], bounds_ref[0, CAP + 1]
    here = pl.ds(pl.multiple_of(i * BLOCK, BLOCK), BLOCK)
    pre = mm_nt(win_ref[...], xin_ref[...])
    tanh = jnp.tanh(pre * 0.5)
    plus = 1.0 + tanh
    hidden = (0.5 * pre) * plus
    slope_ref[...] = 0.5 * (plus + hidden * (1.0 - tanh))
    d = HEAD_DIM
    u = hidden[:d]
    query = (hidden[d : 2 * d].astype(bf16).astype(f32) * 0.0625).astype(bf16)
    vk = hidden[2 * d :]
    vk_t = vk.astype(bf16)
    turned = jnp.transpose(vk).astype(bf16)
    u_ref[...] = u
    q_ref[...] = query
    k_ref[...] = vk_t[d:]
    vk_ref[...] = turned
    q_all[:d, :] = jnp.zeros((d, BLOCK), bf16)
    q_all[d:, :] = query
    v_all[:, here] = vk_t[:d]
    vk_all[here, :] = turned
    mixed_ref[...] = jnp.zeros(mixed_ref.shape, f32)

    def pair(j, carry):
        there = pl.ds(pl.multiple_of(j * BLOCK, BLOCK), BLOCK)
        half = mm(vk_all[there, :], q_all[...])
        weights = half + half * jnp.tanh(half)
        weights = jnp.where(visible(i, j, one, two, BLOCK), weights, 0.0).astype(bf16)
        mixed_ref[...] += mm(v_all[:, there], weights)
        return carry

    first = lax.div(seg_start(i * BLOCK, one, two), BLOCK)
    lax.fori_loop(first, i + 1, pair, 0)
    dg = dg_ref[...]
    mixed = mixed_ref[...]
    e = dg * u * gain_ref[:, :1]
    mean = jnp.sum(mixed, axis=0, keepdims=True) * (1.0 / d)
    centred = mixed - mean
    spread = jnp.sum(centred * centred, axis=0, keepdims=True)
    sum_e = jnp.sum(e, axis=0, keepdims=True)
    sum_em = jnp.sum(e * centred, axis=0, keepdims=True)
    for h in range(HEADS):
        stats_ref[h, 0:1, :] = mean
        stats_ref[h, 1:2, :] = spread
        stats_ref[h, 2:3, :] = sum_e
        stats_ref[h, 3:4, :] = sum_em


def middle(stats, mixed, dg, u, gain):
    width = HEADS * HEAD_DIM
    means = [stats[h, 0:1] for h in range(HEADS)]
    mean = functools.reduce(jnp.add, means) * (1.0 / HEADS)
    var, m_e, m_em = 0.0, 0.0, 0.0
    for h in range(HEADS):
        off = means[h] - mean
        var = var + stats[h, 1:2] + HEAD_DIM * off * off
        m_e = m_e + stats[h, 2:3]
        m_em = m_em + stats[h, 3:4] + off * stats[h, 2:3]
    inverse = lax.rsqrt(var * (1.0 / width) + EPSILON)
    m_e = m_e * (1.0 / width)
    m_eh = m_em * inverse * (1.0 / width)
    hat = (mixed - mean) * inverse
    scaled = hat * gain
    e = dg * u * gain
    up = (inverse * (e - m_e - hat * m_eh)).astype(bf16)
    return (scaled * u).astype(bf16), (up.astype(f32) * 0.0625).astype(bf16), dg * scaled


def backward_kernel(
    steps, bounds_ref, q_ref, k_ref, vk_ref, stats_ref, mixed_ref, dg_ref, u_ref, gain_ref, xin_hbm, cot_hbm, slope_hbm,
    *rest,
):
    outs, rest = rest[:HEADS], rest[HEADS:]
    dw_ref, k_all, vk_all, gated_all, du_all, dq_all, dk_all, dv_all, win_acc, wout_acc, sent, sems = rest[:12]
    query2, up2, half0, upper0, half1, upper1, xin_ref, cot_ref, slope_ref, loaded = rest[12:]
    loads = [
        pltpu.make_async_copy(source, target, loaded.at[at])
        for at, (source, target) in enumerate(((xin_hbm, xin_ref), (cot_hbm, cot_ref), (slope_hbm, slope_ref)))
    ]
    g = pl.program_id(0)
    one, two, me = bounds_ref[0, CAP], bounds_ref[0, CAP + 1], bounds_ref[0, SLOTS]
    d = HEAD_DIM

    @pl.when(g == 0)
    def _():
        for load in loads:
            load.start()
        dk_all[...] = jnp.zeros(dk_all.shape, f32)
        dv_all[...] = jnp.zeros(dv_all.shape, f32)
        dq_all[...] = jnp.zeros(dq_all.shape, f32)
        win_acc[...] = jnp.zeros(win_acc.shape, f32)
        wout_acc[...] = jnp.zeros(wout_acc.shape, f32)
        query2[...] = jnp.zeros(query2.shape, bf16)
        up2[...] = jnp.zeros(up2.shape, bf16)

    @pl.when(g < steps)
    def _():
        here = pl.ds(pl.multiple_of(g * BLOCK, BLOCK), BLOCK)
        gated, up, du = middle(stats_ref[...], mixed_ref[...], dg_ref[...], u_ref[...], gain_ref[:, :1])
        gated_all[:, here] = gated
        du_all[:, here] = du
        k_all[:, here] = k_ref[...]
        vk_all[here, :] = vk_ref[...]
        query2[d:, :] = q_ref[...]
        up2[:d, :] = up
        base = g * (BLOCK // TILE)
        total = pair_of(0, base, one, two)[2]

        def front(i, j):
            at = pl.ds(pl.multiple_of((i - base) * TILE, TILE), TILE)
            vk = vk_all[pl.ds(pl.multiple_of(j * TILE, TILE), TILE), :]
            return mm(vk, query2[:, at]), mm(vk, up2[:, at])

        def back(i, j, half, upper, live):
            at = pl.ds(pl.multiple_of((i - base) * TILE, TILE), TILE)
            here = pl.ds(pl.multiple_of(i * TILE, TILE), TILE)
            there = pl.ds(pl.multiple_of(j * TILE, TILE), TILE)
            tanh = jnp.tanh(half)
            plus = 1.0 + tanh
            weights = half * plus
            dscores = upper * (plus + weights * (1.0 - tanh))
            seen = visible(i, jnp.where(live, j, dq_all.shape[1]), one, two, TILE)
            weights = jnp.where(seen, weights, 0.0).astype(bf16)
            dscores = jnp.where(seen, dscores, 0.0).astype(bf16)
            dv_all[:, there] += mm_nt(up2[:d, at], weights)
            dk_all[:, there] += mm_nt(query2[d:, at], dscores)
            dq_all[:, here] += mm(k_all[:, there], dscores)

        half0[...], upper0[...] = front(*pair_of(0, base, one, two)[:2])

        def two_pairs(t, carry):
            p = 2 * t
            now, odd, after = [
                pair_of(jnp.minimum(p + step, total - 1), base, one, two)[:2] for step in range(3)
            ]
            half1[...], upper1[...] = front(*odd)
            back(*now, half0[...], upper0[...], True)
            half0[...], upper0[...] = front(*after)
            back(*odd, half1[...], upper1[...], p + 1 < total)
            return carry

        lax.fori_loop(0, lax.div(total + 1, 2), two_pairs, 0)

    @pl.when(g == steps)
    def _():
        for load in loads:
            load.wait()
        count = sent.shape[2]
        for s in range(HEADS):
            start = pl.multiple_of(lax.rem(me + s, HEADS) * count, 128)
            here = pl.ds(start, count)
            gated = gated_all[:, here]
            dpre = jnp.concatenate(
                [
                    (du_all[:, here] * slope_ref[:d, here]).astype(bf16),
                    (dq_all[:, here] * slope_ref[d : 2 * d, here]).astype(bf16),
                    (dv_all[:, here] * 16.0 * slope_ref[2 * d : 3 * d, here]).astype(bf16),
                    (dk_all[:, here] * 16.0 * slope_ref[3 * d :, here]).astype(bf16),
                ],
                axis=0,
            )
            sent[s, : 4 * d, :] = dpre
            sent[s, 4 * d :, :] = gated
            pltpu.make_async_copy(sent.at[s], outs[s], sems.at[s]).start()
            win_acc[...] += mm(dpre, xin_ref[here, :])
            wout_acc[...] += mm(gated, cot_ref[here, :])
        parts = dw_ref.shape[0]
        turned = jnp.transpose(win_acc[...])
        rows = turned.shape[0] // parts
        for p in range(parts):
            dw_ref[p, :rows, :] = turned[p * rows : (p + 1) * rows]
            dw_ref[p, rows:, :] = wout_acc[8 * (p // 2) : 8 * (p // 2) + 8, 256 * (p % 2) : 256 * (p % 2) + 256]
        for at in range(HEADS):
            pltpu.make_async_copy(sent.at[at], outs[at], sems.at[at]).wait()


def rows_kernel(*refs):
    got = refs[:HEADS]
    win_ref, gain_ref, fetched_ref, cot_ref, row_ref, out_hbm, gated_hbm, whole, gated_ref, out_ref, sems = refs[HEADS:]
    d = HEAD_DIM
    width = fetched_ref.shape[1]
    me = lax.axis_index("seq")
    own = pl.multiple_of(me * d, d)
    targets = [whole.at[pl.ds(block * width + own, d)] for block in ORDER] + [gated_ref.at[pl.ds(own, d)]]
    loads = [
        pltpu.make_async_copy(got[0].at[pl.ds(at * d, d)], target, sems.at[5 + at]) for at, target in enumerate(targets)
    ]
    for load in loads:
        load.start()
    for s in range(1, HEADS):
        at_head = pl.multiple_of(lax.rem(me + HEADS - s, HEADS) * d, d)
        for at, block in enumerate(ORDER):
            whole[pl.ds(block * width + at_head, d), :] = got[s][at * d : (at + 1) * d, :]
        gated_ref[pl.ds(at_head, d), :] = got[s][4 * d :, :]
    for load in loads:
        load.wait()
    copies = [pltpu.make_async_copy(gated_ref, gated_hbm, sems.at[0])]
    copies[0].start()
    dxin = jnp.transpose(mm(win_ref[...], whole[...]))
    normed, inverse = normalize(fetched_ref[...].astype(f32))
    f = dxin * gain_ref[...]
    drow = inverse * (
        f - jnp.mean(f, axis=-1, keepdims=True) - normed * jnp.mean(f * normed, axis=-1, keepdims=True)
    ) + cot_ref[...].astype(f32)
    drow = drow.astype(bf16)
    slots = out_ref.shape[0]
    count = drow.shape[0]
    block = slots // 4
    for at in range(4):
        pick = jnp.where(row_ref[0:1, :] == iota((block, count), 0) + at * block, 1.0, 0.0).astype(bf16)
        here = pl.ds(at * block, block)
        out_ref[here, :] = mm(pick, drow).astype(bf16)
        copies.append(pltpu.make_async_copy(out_ref.at[here], out_hbm.at[here], sems.at[at + 1]))
        copies[-1].start()
    for copy in copies:
        copy.wait()


def table_kernel(row_ref, got_ref, out_ref):
    block = out_ref.shape[0]
    slots = got_ref.shape[0]
    at = pl.program_id(0) * block
    pick = jnp.where(row_ref[0:1, :] == iota((block, slots), 0) + at, 1.0, 0.0).astype(bf16)
    out_ref[...] = mm(pick, got_ref[...])


def weights_kernel(got_ref, win_ref, wout_ref):
    d = HEAD_DIM
    parts = got_ref.shape[1]
    rows = win_ref.shape[0] // parts
    width = win_ref.shape[1] // 4
    for p in range(parts):
        here = slice(p * rows, (p + 1) * rows)
        for at, block in enumerate(ORDER):
            for pair in range(HEADS // 2):
                left = got_ref[2 * pair, p, :rows, at * d : (at + 1) * d].astype(f32)
                right = got_ref[2 * pair + 1, p, :rows, at * d : (at + 1) * d].astype(f32)
                start = block * width + pair * 2 * d
                win_ref[here, start : start + 2 * d] = jnp.concatenate([left, right], axis=1)
        for h in range(HEADS):
            wout_ref[h, p // 2, :, 256 * (p % 2) : 256 * (p % 2) + 256] = got_ref[h, p, rows:, :].astype(f32)


def finish_kernel(row_ref, rows_ref, got_ref, table_ref, win_ref, wout_ref):
    table_kernel(row_ref, rows_ref, table_ref)
    weights_kernel(got_ref, win_ref, wout_ref)


def finish(asked_row, incoming, dw_all, shard_rows, tiles):
    slots, width = incoming.shape
    seq, users, tall, columns = dw_all.shape
    rows, group = tall - 8, users // tiles
    d = HEAD_DIM
    whole = lambda *shape: pl.BlockSpec(shape, lambda g: (0,) * len(shape))
    return call(
        finish_kernel,
        (
            struct((shard_rows, width), f32), struct((width, 4 * width), f32), struct((HEADS, width // d, 8, width), f32),
        ),
        (asked_row, incoming, pltpu.with_memory_space_constraint(dw_all, pltpu.HBM)),
        mib=24, grid=(tiles,),
        in_specs=[
            whole(8, slots), pl.BlockSpec(memory_space=pltpu.VMEM),
            pl.BlockSpec((seq, group, tall, columns), lambda g: (0, g, 0, 0)),
        ],
        out_specs=[
            pl.BlockSpec((shard_rows // tiles, width), lambda g: (g, 0)),
            pl.BlockSpec((group * rows, 4 * width), lambda g: (g, 0)),
            pl.BlockSpec((HEADS, group // 2, 8, width), lambda g: (0, g, 0, 0)),
        ],
        flops=2 * slots * shard_rows * width, moved=15 << 20,
    )


def exchange(x, axis):
    return lax.all_to_all(x, axis, split_axis=0, concat_axis=0, tiled=True)


def struct(shape, dtype):
    return jax.ShapeDtypeStruct(shape, dtype)


def layer_step(item_table, item_ids, segment_ids, weight_in, weight_out, gain_in, gain_mid, cotangent):
    shard_rows, width = item_table.shape
    count = item_ids.shape[1]
    users, seq = lax.axis_size("users"), lax.axis_size("seq")
    devices = users * seq
    length = count * seq
    d = HEAD_DIM
    slots = devices * SLOTS
    upstream = cotangent[0]
    gain_row = gain_in.reshape(1, width)
    head = lax.axis_index("seq")

    cot_all = lax.all_gather(upstream, "seq", axis=0, tiled=True)
    wanted, slot_row, slot_col = call(
        functools.partial(slots_kernel, shard_rows),
        (struct((devices, 128), i32), struct((8, count), i32), struct((count, 128), i32)),
        (item_ids, segment_ids),
        flops=2 * devices * count * count, moved=1 << 19,
    )
    asked = exchange(wanted.reshape(devices, 1, 128), BOTH).reshape(devices, 128)
    steps = 1
    whole = lambda *shape: pl.BlockSpec(shape, lambda g: (0,) * len(shape))
    smem = pl.BlockSpec(memory_space=pltpu.SMEM)
    served, asked_row, bounds, gain_h = call(
        serve_kernel,
        (struct((slots, width), bf16), struct((8, slots), i32), struct((8, 128), i32), struct((d, 128), f32)),
        (asked, item_table, gain_mid.reshape(1, width)),
        grid=(steps,),
        in_specs=[whole(devices, 128), whole(shard_rows, width), whole(1, width)],
        out_specs=[
            pl.BlockSpec((slots // steps, width), lambda g: (g, 0)), whole(8, slots), whole(8, 128), whole(d, 128),
        ],
        scratch=[pltpu.VMEM((slots, 128), f32), pltpu.VMEM((width, 128), f32)],
        flops=2 * slots * shard_rows * width, moved=4 << 20,
    )
    got = exchange(served.reshape(devices, SLOTS, width), BOTH).reshape(slots, width)
    fetched, xin = call(
        arrange_kernel,
        (pltpu.HBM((count, width), bf16), pltpu.HBM((count, width), bf16)),
        (got, slot_col, gain_row),
        mib=24, in_specs=[pl.BlockSpec(memory_space=pltpu.VMEM)] * 3,
        out_specs=[pl.BlockSpec(memory_space=pltpu.HBM)] * 2,
        scratch=[
            pltpu.VMEM((count, width), bf16), pltpu.VMEM((count, width), bf16), pltpu.SemaphoreType.DMA((2,)),
        ], flops=2 * count * slots * width, moved=2 << 20,
    )
    xin_all = lax.all_gather(xin, "seq", axis=0, tiled=True)

    mine = lax.dynamic_index_in_dim(weight_in.reshape(width, 4, HEADS, d), head, 2, keepdims=False)
    win_t = jnp.stack([mine[:, b] for b in ORDER], axis=1).reshape(width, 4 * d).T
    wout_h = lax.dynamic_slice_in_dim(weight_out, head * d, d, axis=0)

    blocks = length // BLOCK
    lane = lambda rows: pl.BlockSpec((rows, BLOCK), lambda g: (0, g))
    rowed = lambda columns: pl.BlockSpec((BLOCK, columns), lambda g: (g, 0))
    dg = mm_nt(wout_h, cot_all)
    q_t, k_t, vk, slope, u, mixed, stats = call(
        forward_kernel,
        (
            struct((d, length), bf16), struct((d, length), bf16), struct((length, 2 * d), bf16),
            struct((4 * d, length), f32), struct((d, length), f32),
            struct((d, length), f32), struct((seq, 4, length), f32),
        ),
        (xin_all, dg, win_t, gain_h, bounds),
        mib=60, grid=(blocks,),
        in_specs=[rowed(width), lane(d), whole(4 * d, width), whole(d, 128), smem],
        out_specs=[lane(d), lane(d), rowed(2 * d), lane(4 * d), lane(d), lane(d),
            pl.BlockSpec((seq, 4, BLOCK), lambda g: (0, 0, g)),
        ],
        scratch=[pltpu.VMEM((2 * d, BLOCK), bf16), pltpu.VMEM((d, length), bf16), pltpu.VMEM((length, 2 * d), bf16)],
        flops=1 << 33, moved=12 << 20,
    )
    stats_all = exchange(stats, "seq")

    early = lambda g: jnp.minimum(g, blocks - 1)
    fixed = lambda *shape: pl.BlockSpec(shape, lambda g, b: (0,) * len(shape))
    lanes = lambda rows: pl.BlockSpec((rows, BLOCK), lambda g, b: (0, early(g)))
    rows = width // users
    result = pl.pallas_call(
        functools.partial(backward_kernel, blocks),
        out_shape=[struct((5 * d, count), bf16)] * HEADS + [struct((users, rows + 8, 4 * d), f32)],
        grid_spec=pltpu.PrefetchScalarGridSpec(
            num_scalar_prefetch=1,
            grid=(blocks + 1,),
            in_specs=[
                lanes(d), lanes(d), pl.BlockSpec((BLOCK, 2 * d), lambda g, b: (early(g), 0)),
                pl.BlockSpec((seq, 4, BLOCK), lambda g, b: (0, 0, early(g))),
                lanes(d), lanes(d), lanes(d), fixed(d, 128),
                *[pl.BlockSpec(memory_space=pl.ANY)] * 3,
            ],
            out_specs=[pl.BlockSpec(memory_space=pl.ANY)] * HEADS + [fixed(users, rows + 8, 4 * d)],
            scratch_shapes=[
                pltpu.VMEM((d, length), bf16), pltpu.VMEM((length, 2 * d), bf16), pltpu.VMEM((d, length), bf16),
                pltpu.VMEM((d, length), f32), pltpu.VMEM((d, length), f32), pltpu.VMEM((d, length), f32),
                pltpu.VMEM((d, length), f32), pltpu.VMEM((4 * d, width), f32), pltpu.VMEM((d, width), f32),
                pltpu.VMEM((HEADS, 5 * d, count), bf16), pltpu.SemaphoreType.DMA((HEADS,)),
                pltpu.VMEM((2 * d, BLOCK), bf16), pltpu.VMEM((2 * d, BLOCK), bf16),
                *[pltpu.VMEM((TILE, TILE), f32)] * 4,
                pltpu.VMEM((length, width), bf16), pltpu.VMEM((length, width), bf16), pltpu.VMEM((4 * d, length), f32),
                pltpu.SemaphoreType.DMA((3,)),
            ],
        ),
        name="backward",
        compiler_params=pltpu.CompilerParams(
            vmem_limit_bytes=60 * 1024 * 1024, dimension_semantics=("arbitrary",)
        ),
        cost_estimate=pl.CostEstimate(flops=1 << 35, bytes_accessed=16 << 20, transcendentals=0),
    )(bounds, q_t, k_t, vk, stats_all, mixed, dg, u, gain_h, xin_all, cot_all, slope)
    dw = result[HEADS]
    pieces = [result[0]]
    for s in range(1, seq):
        pieces.append(lax.ppermute(result[s], "seq", [(i, (i + s) % seq) for i in range(seq)]))
    dw_got = exchange(dw, "users")
    dw_sum = jnp.sum(dw_got, axis=0).astype(bf16)
    dw_wide = jnp.broadcast_to(dw_sum[None], (users, rows + 8, 4 * d))
    dw_head = exchange(dw_wide, "users")
    dw_all = lax.all_gather(dw_head, "seq", axis=0, tiled=False)
    outgoing, gated_mine = call(
        rows_kernel,
        (pltpu.HBM((slots, width), bf16), pltpu.HBM((width, count), bf16)),
        (pltpu.with_memory_space_constraint(pieces[0], pltpu.HBM), *pieces[1:], weight_in, gain_row, fetched, upstream, slot_row),
        mib=24, in_specs=[pl.BlockSpec(memory_space=pltpu.HBM)] + [pl.BlockSpec(memory_space=pltpu.VMEM)] * (HEADS + 4),
        out_specs=[pl.BlockSpec(memory_space=pltpu.HBM)] * 2,
        scratch=[
            pltpu.VMEM((4 * width, count), bf16), pltpu.VMEM((width, count), bf16), pltpu.VMEM((slots, width), bf16),
            pltpu.SemaphoreType.DMA((10,)),
        ],
        flops=2 * count * width * 4 * width, moved=6 << 20,
    )
    layer = (
        fetched.astype(f32)
        + lax.dot_general(gated_mine, weight_out, (((0,), (0,)), ((), ())), preferred_element_type=f32)
    ).astype(bf16)
    incoming = exchange(outgoing.reshape(devices, SLOTS, width), BOTH)
    incoming = incoming.reshape(slots, width)
    table_grad, win_grad, wout_grad = finish(asked_row, incoming, dw_all, shard_rows, 4)
    return (layer[None], table_grad, win_grad, wout_grad.reshape(width, width))


def solution(mesh):
    in_specs = (
        P(BOTH, None),
        P("users", "seq"),
        P("users", "seq"),
        P(),
        P(),
        P(),
        P(),
        P("users", "seq", None),
    )
    out_specs = (P("users", "seq", None), P(BOTH, None), P(), P())
    return jax.shard_map(layer_step, mesh=mesh, in_specs=in_specs, out_specs=out_specs, check_vma=False)
```

```python
import functools
import jax
import jax.numpy as jnp
from jax import lax
from jax.experimental import pallas as pl
from jax.experimental.pallas import tpu as pltpu
from jax.sharding import PartitionSpec as P


HEADS = 8
HEAD_DIM = 64
SLOTS = 8
CAP = 6
BLOCK = 768
TILE = 256
EPSILON = 1e-05
BOTH = ("users", "seq")
ORDER = (0, 2, 1, 3)

f32 = jnp.float32
bf16 = jnp.bfloat16
i32 = jnp.int32


def iota(shape, dim):
    return lax.broadcasted_iota(i32, shape, dim)


def mm(a, b):
    return jnp.dot(a, b, preferred_element_type=f32)


def mm_nt(a, b):
    return lax.dot_general(a, b, (((1,), (1,)), ((), ())), preferred_element_type=f32)


def call(kernel, out_shape, args, *, grid=None, in_specs=None, out_specs=None, scratch=(), flops=0, moved=0, mib=60):
    params = dict(vmem_limit_bytes=mib * 1024 * 1024)
    extra = {}
    if grid is not None:
        params["dimension_semantics"] = ("arbitrary",) * len(grid)
        extra["grid"] = grid
    if in_specs is not None:
        extra["in_specs"] = in_specs
    if out_specs is not None:
        extra["out_specs"] = out_specs
    return pl.pallas_call(
        kernel,
        out_shape=out_shape,
        scratch_shapes=scratch,
        compiler_params=pltpu.CompilerParams(**params),
        cost_estimate=pl.CostEstimate(flops=flops, bytes_accessed=moved, transcendentals=0),
        **extra,
    )(*args)


def normalize(values):
    centred = values - jnp.mean(values, axis=-1, keepdims=True)
    inverse = lax.rsqrt(jnp.mean(centred * centred, axis=-1, keepdims=True) + EPSILON)
    return centred * inverse, inverse


def slots_kernel(shard_rows, ids_ref, seg_ref, wanted_ref, row_ref, col_ref):
    devices, lanes = wanted_ref.shape
    count = ids_ref.shape[1]
    ids = ids_ref[...]
    owner = lax.shift_right_logical(ids, shard_rows.bit_length() - 1)
    local = (ids & (shard_rows - 1)).astype(f32)
    held = owner == iota((devices, count), 0)
    hit = jnp.where(held, 1.0, 0.0)
    earlier = jnp.where(iota((count, count), 0) < iota((count, count), 1), 1.0, 0.0)
    rank = mm(hit.astype(bf16), earlier.astype(bf16))
    marked = jnp.where(held, rank, -1.0)
    lane = iota((devices, lanes), 1)
    wanted = jnp.zeros((devices, lanes), f32)
    for c in range(CAP):
        column = jnp.sum(jnp.where(marked == float(c), local, 0.0), axis=1, keepdims=True)
        wanted = jnp.where(lane == c, column, wanted)
    seg = seg_ref[...]
    below1 = jnp.sum(jnp.where(seg < 1, 1.0, 0.0), axis=1, keepdims=True)
    below2 = jnp.sum(jnp.where(seg < 2, 1.0, 0.0), axis=1, keepdims=True)
    wanted = jnp.where(lane == CAP, below1, wanted)
    wanted = jnp.where(lane == CAP + 1, below2, wanted)
    wanted_ref[...] = wanted.astype(i32)
    slot = owner.astype(f32) * float(SLOTS) + jnp.sum(hit * rank, axis=0, keepdims=True)
    row_ref[...] = jnp.broadcast_to(slot, row_ref.shape).astype(i32)
    col_ref[...] = jnp.transpose(jnp.broadcast_to(slot, (lanes, count))).astype(i32)


def serve_kernel(asked_ref, table_ref, gain_ref, served_ref, row_ref, bounds_ref, mid_ref, col_ref, turn_ref):
    step = pl.program_id(0)
    block = served_ref.shape[0]
    devices, lanes = asked_ref.shape

    @pl.when(step == 0)
    def _():
        asked = asked_ref[...].astype(f32)
        wide = jnp.broadcast_to(asked[:, None, :], (devices, SLOTS, lanes))
        sub = iota((devices, SLOTS, lanes), 1)
        lane = iota((devices, SLOTS, lanes), 2)
        column = jnp.sum(jnp.where(sub == lane, wide, 0.0), axis=2, keepdims=True)
        column = jnp.where(iota((devices, SLOTS, 1), 1) < CAP, column, -1.0)
        column = jnp.broadcast_to(column, (devices, SLOTS, lanes)).reshape(devices * SLOTS, lanes)
        col_ref[...] = column
        row_ref[...] = jnp.transpose(column)[: row_ref.shape[0]].astype(i32)
        group = lax.axis_index("users")
        mine = lax.div(iota((devices, lanes), 0), SLOTS) == group
        bounds = jnp.sum(jnp.where(mine, asked, 0.0), axis=0, keepdims=True)
        bounds = jnp.broadcast_to(bounds, bounds_ref.shape).astype(i32)
        me = lax.axis_index("seq")
        bounds_ref[...] = jnp.where(iota(bounds_ref.shape, 1) == SLOTS, me, bounds)
        turn_ref[...] = jnp.transpose(jnp.broadcast_to(gain_ref[...], (lanes, gain_ref.shape[1])))
        d = mid_ref.shape[0]
        mid_ref[...] = turn_ref[pl.ds(pl.multiple_of(me * d, d), d), :]

    column = col_ref[pl.ds(pl.multiple_of(step * block, block), block), :].astype(i32)
    parts = []
    for at in range(table_ref.shape[0] // lanes):
        parts.append(jnp.where(column == iota((block, lanes), 1) + at * lanes, 1.0, 0.0).astype(bf16))
    served_ref[...] = mm(jnp.concatenate(parts, axis=1), table_ref[...]).astype(bf16)


def arrange_kernel(got_ref, col_ref, gain_ref, fetched_hbm, xin_hbm, fetched_ref, xin_ref, sems):
    slot = col_ref[...]
    count, lanes = slot.shape
    parts = []
    for at in range(got_ref.shape[0] // lanes):
        parts.append(jnp.where(slot == iota((count, lanes), 1) + at * lanes, 1.0, 0.0).astype(bf16))
    fetched = mm(jnp.concatenate(parts, axis=1), got_ref[...])
    fetched_ref[...] = fetched.astype(bf16)
    normed, _ = normalize(fetched)
    xin_ref[...] = (normed * gain_ref[...]).astype(bf16)
    copies = [
        pltpu.make_async_copy(xin_ref, xin_hbm, sems.at[0]), pltpu.make_async_copy(fetched_ref, fetched_hbm, sems.at[1]),
    ]
    for copy in copies:
        copy.start()
    for copy in copies:
        copy.wait()


def seg_start(position, one, two):
    return jnp.where(position < one, 0, jnp.where(position < two, one, two))


def visible(i, j, one, two, block):
    where_q = iota((1, block), 1) + i * block
    start = seg_start(where_q, one, two)
    where_k = iota((block, block), 0) + j * block
    return (where_k >= start) & (where_k <= where_q)


def pair_of(p, base, one, two):
    first = lax.div(seg_start(base * TILE, one, two), TILE)
    i, j = base, first + p
    passed = base - first + 1
    for step in range(1, BLOCK // TILE):
        first = lax.div(seg_start((base + step) * TILE, one, two), TILE)
        later = p >= passed
        i = jnp.where(later, base + step, i)
        j = jnp.where(later, first + p - passed, j)
        passed = passed + base + step - first + 1
    return i, j, passed


def forward_kernel(
    xin_ref, dg_ref, win_ref, gain_ref, bounds_ref,
    q_ref, k_ref, vk_ref, slope_ref, u_ref, mixed_ref, stats_ref,
    q_all, v_all, vk_all,
):
    i = pl.program_id(0)
    one, two = bounds_ref[0, CAP], bounds_ref[0, CAP + 1]
    here = pl.ds(pl.multiple_of(i * BLOCK, BLOCK), BLOCK)
    pre = mm_nt(win_ref[...], xin_ref[...])
    tanh = jnp.tanh(pre * 0.5)
    plus = 1.0 + tanh
    hidden = (0.5 * pre) * plus
    slope_ref[...] = 0.5 * (plus + hidden * (1.0 - tanh))
    d = HEAD_DIM
    u = hidden[:d]
    query = (hidden[d : 2 * d].astype(bf16).astype(f32) * 0.0625).astype(bf16)
    vk = hidden[2 * d :]
    vk_t = vk.astype(bf16)
    turned = jnp.transpose(vk).astype(bf16)
    u_ref[...] = u
    q_ref[...] = query
    k_ref[...] = vk_t[d:]
    vk_ref[...] = turned
    q_all[:d, :] = jnp.zeros((d, BLOCK), bf16)
    q_all[d:, :] = query
    v_all[:, here] = vk_t[:d]
    vk_all[here, :] = turned
    mixed_ref[...] = jnp.zeros(mixed_ref.shape, f32)

    def pair(j, carry):
        there = pl.ds(pl.multiple_of(j * BLOCK, BLOCK), BLOCK)
        half = mm(vk_all[there, :], q_all[...])
        weights = half + half * jnp.tanh(half)
        weights = jnp.where(visible(i, j, one, two, BLOCK), weights, 0.0).astype(bf16)
        mixed_ref[...] += mm(v_all[:, there], weights)
        return carry

    first = lax.div(seg_start(i * BLOCK, one, two), BLOCK)
    lax.fori_loop(first, i + 1, pair, 0)
    dg = dg_ref[...]
    mixed = mixed_ref[...]
    e = dg * u * gain_ref[:, :1]
    mean = jnp.sum(mixed, axis=0, keepdims=True) * (1.0 / d)
    centred = mixed - mean
    spread = jnp.sum(centred * centred, axis=0, keepdims=True)
    sum_e = jnp.sum(e, axis=0, keepdims=True)
    sum_em = jnp.sum(e * centred, axis=0, keepdims=True)
    for h in range(HEADS):
        stats_ref[h, 0:1, :] = mean
        stats_ref[h, 1:2, :] = spread
        stats_ref[h, 2:3, :] = sum_e
        stats_ref[h, 3:4, :] = sum_em


def middle(stats, mixed, dg, u, gain):
    width = HEADS * HEAD_DIM
    means = [stats[h, 0:1] for h in range(HEADS)]
    mean = functools.reduce(jnp.add, means) * (1.0 / HEADS)
    var, m_e, m_em = 0.0, 0.0, 0.0
    for h in range(HEADS):
        off = means[h] - mean
        var = var + stats[h, 1:2] + HEAD_DIM * off * off
        m_e = m_e + stats[h, 2:3]
        m_em = m_em + stats[h, 3:4] + off * stats[h, 2:3]
    inverse = lax.rsqrt(var * (1.0 / width) + EPSILON)
    m_e = m_e * (1.0 / width)
    m_eh = m_em * inverse * (1.0 / width)
    hat = (mixed - mean) * inverse
    scaled = hat * gain
    e = dg * u * gain
    up = (inverse * (e - m_e - hat * m_eh)).astype(bf16)
    return (scaled * u).astype(bf16), (up.astype(f32) * 0.0625).astype(bf16), dg * scaled


def backward_kernel(
    steps, bounds_ref, q_ref, k_ref, vk_ref, stats_ref, mixed_ref, dg_ref, u_ref, gain_ref, xin_hbm, cot_hbm, slope_hbm,
    *rest,
):
    outs, rest = rest[:HEADS], rest[HEADS:]
    dw_ref, k_all, vk_all, gated_all, du_all, dq_all, dk_all, dv_all, win_acc, wout_acc, sent, sems = rest[:12]
    query2, up2, half0, upper0, half1, upper1, xin_ref, cot_ref, slope_ref, loaded = rest[12:]
    loads = [
        pltpu.make_async_copy(source, target, loaded.at[at])
        for at, (source, target) in enumerate(((xin_hbm, xin_ref), (cot_hbm, cot_ref), (slope_hbm, slope_ref)))
    ]
    g = pl.program_id(0)
    one, two, me = bounds_ref[0, CAP], bounds_ref[0, CAP + 1], bounds_ref[0, SLOTS]
    d = HEAD_DIM

    @pl.when(g == 0)
    def _():
        for load in loads:
            load.start()
        dk_all[...] = jnp.zeros(dk_all.shape, f32)
        dv_all[...] = jnp.zeros(dv_all.shape, f32)
        dq_all[...] = jnp.zeros(dq_all.shape, f32)
        win_acc[...] = jnp.zeros(win_acc.shape, f32)
        wout_acc[...] = jnp.zeros(wout_acc.shape, f32)
        query2[...] = jnp.zeros(query2.shape, bf16)
        up2[...] = jnp.zeros(up2.shape, bf16)

    @pl.when(g < steps)
    def _():
        here = pl.ds(pl.multiple_of(g * BLOCK, BLOCK), BLOCK)
        gated, up, du = middle(stats_ref[...], mixed_ref[...], dg_ref[...], u_ref[...], gain_ref[:, :1])
        gated_all[:, here] = gated
        du_all[:, here] = du
        k_all[:, here] = k_ref[...]
        vk_all[here, :] = vk_ref[...]
        query2[d:, :] = q_ref[...]
        up2[:d, :] = up
        base = g * (BLOCK // TILE)
        total = pair_of(0, base, one, two)[2]

        def front(i, j):
            at = pl.ds(pl.multiple_of((i - base) * TILE, TILE), TILE)
            vk = vk_all[pl.ds(pl.multiple_of(j * TILE, TILE), TILE), :]
            return mm(vk, query2[:, at]), mm(vk, up2[:, at])

        def back(i, j, half, upper, live):
            at = pl.ds(pl.multiple_of((i - base) * TILE, TILE), TILE)
            here = pl.ds(pl.multiple_of(i * TILE, TILE), TILE)
            there = pl.ds(pl.multiple_of(j * TILE, TILE), TILE)
            tanh = jnp.tanh(half)
            plus = 1.0 + tanh
            weights = half * plus
            dscores = upper * (plus + weights * (1.0 - tanh))
            seen = visible(i, jnp.where(live, j, dq_all.shape[1]), one, two, TILE)
            weights = jnp.where(seen, weights, 0.0).astype(bf16)
            dscores = jnp.where(seen, dscores, 0.0).astype(bf16)
            dv_all[:, there] += mm_nt(up2[:d, at], weights)
            dk_all[:, there] += mm_nt(query2[d:, at], dscores)
            dq_all[:, here] += mm(k_all[:, there], dscores)

        half0[...], upper0[...] = front(*pair_of(0, base, one, two)[:2])

        def two_pairs(t, carry):
            p = 2 * t
            now, odd, after = [
                pair_of(jnp.minimum(p + step, total - 1), base, one, two)[:2] for step in range(3)
            ]
            half1[...], upper1[...] = front(*odd)
            back(*now, half0[...], upper0[...], True)
            half0[...], upper0[...] = front(*after)
            back(*odd, half1[...], upper1[...], p + 1 < total)
            return carry

        lax.fori_loop(0, lax.div(total + 1, 2), two_pairs, 0)

    @pl.when(g == steps)
    def _():
        for load in loads:
            load.wait()
        count = sent.shape[2]
        for s in range(HEADS):
            start = pl.multiple_of(lax.rem(me + s, HEADS) * count, 128)
            here = pl.ds(start, count)
            gated = gated_all[:, here]
            dpre = jnp.concatenate(
                [
                    (du_all[:, here] * slope_ref[:d, here]).astype(bf16),
                    (dq_all[:, here] * slope_ref[d : 2 * d, here]).astype(bf16),
                    (dv_all[:, here] * 16.0 * slope_ref[2 * d : 3 * d, here]).astype(bf16),
                    (dk_all[:, here] * 16.0 * slope_ref[3 * d :, here]).astype(bf16),
                ],
                axis=0,
            )
            sent[s, : 4 * d, :] = dpre
            sent[s, 4 * d :, :] = gated
            pltpu.make_async_copy(sent.at[s], outs[s], sems.at[s]).start()
            win_acc[...] += mm(dpre, xin_ref[here, :])
            wout_acc[...] += mm(gated, cot_ref[here, :])
        parts = dw_ref.shape[0]
        turned = jnp.transpose(win_acc[...])
        rows = turned.shape[0] // parts
        for p in range(parts):
            dw_ref[p, :rows, :] = turned[p * rows : (p + 1) * rows]
            dw_ref[p, rows:, :] = wout_acc[8 * (p // 2) : 8 * (p // 2) + 8, 256 * (p % 2) : 256 * (p % 2) + 256]
        for at in range(HEADS):
            pltpu.make_async_copy(sent.at[at], outs[at], sems.at[at]).wait()


def rows_kernel(*refs):
    got = refs[:HEADS]
    win_hbm, gain_ref, fetched_ref, cot_ref, row_ref, out_hbm, gated_hbm, whole, gated_ref, out_ref, sems = refs[
        HEADS:-2
    ]
    win_ref, win_sems = refs[-2:]
    chunks = win_sems.shape[0]
    tall = win_ref.shape[0] // chunks
    strips = [pl.ds(c * tall, tall) for c in range(chunks)]
    brought = [pltpu.make_async_copy(win_hbm.at[r], win_ref.at[r], win_sems.at[c]) for c, r in enumerate(strips)]
    for load in brought:
        load.start()
    d = HEAD_DIM
    width = fetched_ref.shape[1]
    me = lax.axis_index("seq")
    own = pl.multiple_of(me * d, d)
    targets = [whole.at[pl.ds(block * width + own, d)] for block in ORDER] + [gated_ref.at[pl.ds(own, d)]]
    loads = [
        pltpu.make_async_copy(got[0].at[pl.ds(at * d, d)], target, sems.at[5 + at]) for at, target in enumerate(targets)
    ]
    for load in loads:
        load.start()
    for s in range(1, HEADS):
        at_head = pl.multiple_of(lax.rem(me + HEADS - s, HEADS) * d, d)
        for at, block in enumerate(ORDER):
            whole[pl.ds(block * width + at_head, d), :] = got[s][at * d : (at + 1) * d, :]
        gated_ref[pl.ds(at_head, d), :] = got[s][4 * d :, :]
    for load in loads:
        load.wait()
    copies = [pltpu.make_async_copy(gated_ref, gated_hbm, sems.at[0])]
    copies[0].start()
    columns = []
    for load, strip in zip(brought, strips):
        load.wait()
        columns.append(jnp.transpose(mm(win_ref[strip, :], whole[...])))
    dxin = jnp.concatenate(columns, axis=1)
    normed, inverse = normalize(fetched_ref[...].astype(f32))
    f = dxin * gain_ref[...]
    drow = inverse * (
        f - jnp.mean(f, axis=-1, keepdims=True) - normed * jnp.mean(f * normed, axis=-1, keepdims=True)
    ) + cot_ref[...].astype(f32)
    drow = drow.astype(bf16)
    slots = out_ref.shape[0]
    count = drow.shape[0]
    block = slots // 4
    for at in range(4):
        pick = jnp.where(row_ref[0:1, :] == iota((block, count), 0) + at * block, 1.0, 0.0).astype(bf16)
        here = pl.ds(at * block, block)
        out_ref[here, :] = mm(pick, drow).astype(bf16)
        copies.append(pltpu.make_async_copy(out_ref.at[here], out_hbm.at[here], sems.at[at + 1]))
        copies[-1].start()
    for copy in copies:
        copy.wait()


def table_kernel(row_ref, got_ref, out_ref):
    block = out_ref.shape[0]
    slots = got_ref.shape[0]
    at = pl.program_id(0) * block
    pick = jnp.where(row_ref[0:1, :] == iota((block, slots), 0) + at, 1.0, 0.0).astype(bf16)
    out_ref[...] = mm(pick, got_ref[...])


def weights_kernel(got_ref, win_ref, wout_ref):
    d = HEAD_DIM
    parts = got_ref.shape[1]
    rows = win_ref.shape[0] // parts
    width = win_ref.shape[1] // 4
    for p in range(parts):
        here = slice(p * rows, (p + 1) * rows)
        for at, block in enumerate(ORDER):
            for pair in range(HEADS // 2):
                left = got_ref[2 * pair, p, :rows, at * d : (at + 1) * d].astype(f32)
                right = got_ref[2 * pair + 1, p, :rows, at * d : (at + 1) * d].astype(f32)
                start = block * width + pair * 2 * d
                win_ref[here, start : start + 2 * d] = jnp.concatenate([left, right], axis=1)
        for h in range(HEADS):
            wout_ref[h, p // 2, :, 256 * (p % 2) : 256 * (p % 2) + 256] = got_ref[h, p, rows:, :].astype(f32)


def finish_kernel(row_ref, rows_ref, got_ref, table_ref, win_ref, wout_ref):
    table_kernel(row_ref, rows_ref, table_ref)
    weights_kernel(got_ref, win_ref, wout_ref)


def finish(asked_row, incoming, dw_all, shard_rows, tiles):
    slots, width = incoming.shape
    seq, users, tall, columns = dw_all.shape
    rows, group = tall - 8, users // tiles
    d = HEAD_DIM
    whole = lambda *shape: pl.BlockSpec(shape, lambda g: (0,) * len(shape))
    return call(
        finish_kernel,
        (
            struct((shard_rows, width), f32), struct((width, 4 * width), f32), struct((HEADS, width // d, 8, width), f32),
        ),
        (asked_row, incoming, pltpu.with_memory_space_constraint(dw_all, pltpu.HBM)),
        mib=24, grid=(tiles,),
        in_specs=[
            whole(8, slots), pl.BlockSpec(memory_space=pltpu.VMEM),
            pl.BlockSpec((seq, group, tall, columns), lambda g: (0, g, 0, 0)),
        ],
        out_specs=[
            pl.BlockSpec((shard_rows // tiles, width), lambda g: (g, 0)),
            pl.BlockSpec((group * rows, 4 * width), lambda g: (g, 0)),
            pl.BlockSpec((HEADS, group // 2, 8, width), lambda g: (0, g, 0, 0)),
        ],
        flops=2 * slots * shard_rows * width, moved=15 << 20,
    )


def exchange(x, axis):
    return lax.all_to_all(x, axis, split_axis=0, concat_axis=0, tiled=True)


def struct(shape, dtype):
    return jax.ShapeDtypeStruct(shape, dtype)


def layer_step(item_table, item_ids, segment_ids, weight_in, weight_out, gain_in, gain_mid, cotangent):
    shard_rows, width = item_table.shape
    count = item_ids.shape[1]
    users, seq = lax.axis_size("users"), lax.axis_size("seq")
    devices = users * seq
    length = count * seq
    d = HEAD_DIM
    slots = devices * SLOTS
    upstream = cotangent[0]
    gain_row = gain_in.reshape(1, width)
    head = lax.axis_index("seq")

    cot_all = lax.all_gather(upstream, "seq", axis=0, tiled=True)
    wanted, slot_row, slot_col = call(
        functools.partial(slots_kernel, shard_rows),
        (struct((devices, 128), i32), struct((8, count), i32), struct((count, 128), i32)),
        (item_ids, segment_ids),
        flops=2 * devices * count * count, moved=1 << 19,
    )
    asked = exchange(wanted.reshape(devices, 1, 128), BOTH).reshape(devices, 128)
    steps = 1
    whole = lambda *shape: pl.BlockSpec(shape, lambda g: (0,) * len(shape))
    smem = pl.BlockSpec(memory_space=pltpu.SMEM)
    served, asked_row, bounds, gain_h = call(
        serve_kernel,
        (struct((slots, width), bf16), struct((8, slots), i32), struct((8, 128), i32), struct((d, 128), f32)),
        (asked, item_table, gain_mid.reshape(1, width)),
        grid=(steps,),
        in_specs=[whole(devices, 128), whole(shard_rows, width), whole(1, width)],
        out_specs=[
            pl.BlockSpec((slots // steps, width), lambda g: (g, 0)), whole(8, slots), whole(8, 128), whole(d, 128),
        ],
        scratch=[pltpu.VMEM((slots, 128), f32), pltpu.VMEM((width, 128), f32)],
        flops=2 * slots * shard_rows * width, moved=4 << 20,
    )
    got = exchange(served.reshape(devices, SLOTS, width), BOTH).reshape(slots, width)
    fetched, xin = call(
        arrange_kernel,
        (pltpu.HBM((count, width), bf16), pltpu.HBM((count, width), bf16)),
        (got, slot_col, gain_row),
        mib=24, in_specs=[pl.BlockSpec(memory_space=pltpu.VMEM)] * 3,
        out_specs=[pl.BlockSpec(memory_space=pltpu.HBM)] * 2,
        scratch=[
            pltpu.VMEM((count, width), bf16), pltpu.VMEM((count, width), bf16), pltpu.SemaphoreType.DMA((2,)),
        ], flops=2 * count * slots * width, moved=2 << 20,
    )
    xin_all = lax.all_gather(xin, "seq", axis=0, tiled=True)

    mine = lax.dynamic_index_in_dim(weight_in.reshape(width, 4, HEADS, d), head, 2, keepdims=False)
    win_t = jnp.stack([mine[:, b] for b in ORDER], axis=1).reshape(width, 4 * d).T
    wout_h = lax.dynamic_slice_in_dim(weight_out, head * d, d, axis=0)

    blocks = length // BLOCK
    lane = lambda rows: pl.BlockSpec((rows, BLOCK), lambda g: (0, g))
    rowed = lambda columns: pl.BlockSpec((BLOCK, columns), lambda g: (g, 0))
    dg = mm_nt(wout_h, cot_all)
    q_t, k_t, vk, slope, u, mixed, stats = call(
        forward_kernel,
        (
            struct((d, length), bf16), struct((d, length), bf16), struct((length, 2 * d), bf16),
            struct((4 * d, length), f32), struct((d, length), f32),
            struct((d, length), f32), struct((seq, 4, length), f32),
        ),
        (xin_all, dg, win_t, gain_h, bounds),
        mib=60, grid=(blocks,),
        in_specs=[rowed(width), lane(d), whole(4 * d, width), whole(d, 128), smem],
        out_specs=[lane(d), lane(d), rowed(2 * d), lane(4 * d), lane(d), lane(d),
            pl.BlockSpec((seq, 4, BLOCK), lambda g: (0, 0, g)),
        ],
        scratch=[pltpu.VMEM((2 * d, BLOCK), bf16), pltpu.VMEM((d, length), bf16), pltpu.VMEM((length, 2 * d), bf16)],
        flops=1 << 33, moved=12 << 20,
    )
    stats_all = exchange(stats, "seq")

    early = lambda g: jnp.minimum(g, blocks - 1)
    fixed = lambda *shape: pl.BlockSpec(shape, lambda g, b: (0,) * len(shape))
    lanes = lambda rows: pl.BlockSpec((rows, BLOCK), lambda g, b: (0, early(g)))
    rows = width // users
    result = pl.pallas_call(
        functools.partial(backward_kernel, blocks),
        out_shape=[struct((5 * d, count), bf16)] * HEADS + [struct((users, rows + 8, 4 * d), f32)],
        grid_spec=pltpu.PrefetchScalarGridSpec(
            num_scalar_prefetch=1,
            grid=(blocks + 1,),
            in_specs=[
                lanes(d), lanes(d), pl.BlockSpec((BLOCK, 2 * d), lambda g, b: (early(g), 0)),
                pl.BlockSpec((seq, 4, BLOCK), lambda g, b: (0, 0, early(g))),
                lanes(d), lanes(d), lanes(d), fixed(d, 128),
                *[pl.BlockSpec(memory_space=pl.ANY)] * 3,
            ],
            out_specs=[pl.BlockSpec(memory_space=pl.ANY)] * HEADS + [fixed(users, rows + 8, 4 * d)],
            scratch_shapes=[
                pltpu.VMEM((d, length), bf16), pltpu.VMEM((length, 2 * d), bf16), pltpu.VMEM((d, length), bf16),
                pltpu.VMEM((d, length), f32), pltpu.VMEM((d, length), f32), pltpu.VMEM((d, length), f32),
                pltpu.VMEM((d, length), f32), pltpu.VMEM((4 * d, width), f32), pltpu.VMEM((d, width), f32),
                pltpu.VMEM((HEADS, 5 * d, count), bf16), pltpu.SemaphoreType.DMA((HEADS,)),
                pltpu.VMEM((2 * d, BLOCK), bf16), pltpu.VMEM((2 * d, BLOCK), bf16),
                *[pltpu.VMEM((TILE, TILE), f32)] * 4,
                pltpu.VMEM((length, width), bf16), pltpu.VMEM((length, width), bf16), pltpu.VMEM((4 * d, length), f32),
                pltpu.SemaphoreType.DMA((3,)),
            ],
        ),
        name="backward",
        compiler_params=pltpu.CompilerParams(
            vmem_limit_bytes=60 * 1024 * 1024, dimension_semantics=("arbitrary",)
        ),
        cost_estimate=pl.CostEstimate(flops=1 << 35, bytes_accessed=16 << 20, transcendentals=0),
    )(bounds, q_t, k_t, vk, stats_all, mixed, dg, u, gain_h, xin_all, cot_all, slope)
    dw = result[HEADS]
    pieces = [result[0]]
    for s in range(1, seq):
        pieces.append(lax.ppermute(result[s], "seq", [(i, (i + s) % seq) for i in range(seq)]))
    dw_got = exchange(dw, "users")
    dw_sum = jnp.sum(dw_got, axis=0).astype(bf16)
    dw_wide = jnp.broadcast_to(dw_sum[None], (users, rows + 8, 4 * d))
    dw_head = exchange(dw_wide, "users")
    dw_all = lax.all_gather(dw_head, "seq", axis=0, tiled=False)
    outgoing, gated_mine = call(
        rows_kernel,
        (pltpu.HBM((slots, width), bf16), pltpu.HBM((width, count), bf16)),
        (pltpu.with_memory_space_constraint(pieces[0], pltpu.HBM), *pieces[1:], pltpu.with_memory_space_constraint(weight_in, pltpu.HBM), gain_row, fetched, upstream, slot_row),
        mib=24, in_specs=[pl.BlockSpec(memory_space=pltpu.HBM)] + [pl.BlockSpec(memory_space=pltpu.VMEM)] * (HEADS - 1)
        + [pl.BlockSpec(memory_space=pltpu.HBM)] + [pl.BlockSpec(memory_space=pltpu.VMEM)] * 4,
        out_specs=[pl.BlockSpec(memory_space=pltpu.HBM)] * 2,
        scratch=[
            pltpu.VMEM((4 * width, count), bf16), pltpu.VMEM((width, count), bf16), pltpu.VMEM((slots, width), bf16),
            pltpu.SemaphoreType.DMA((10,)), pltpu.VMEM((width, 4 * width), bf16), pltpu.SemaphoreType.DMA((4,)),
        ],
        flops=2 * count * width * 4 * width, moved=6 << 20,
    )
    layer = (
        fetched.astype(f32)
        + lax.dot_general(gated_mine, weight_out, (((0,), (0,)), ((), ())), preferred_element_type=f32)
    ).astype(bf16)
    incoming = exchange(outgoing.reshape(devices, SLOTS, width), BOTH)
    incoming = incoming.reshape(slots, width)
    table_grad, win_grad, wout_grad = finish(asked_row, incoming, dw_all, shard_rows, 4)
    return (layer[None], table_grad, win_grad, wout_grad.reshape(width, width))


def solution(mesh):
    in_specs = (
        P(BOTH, None),
        P("users", "seq"),
        P("users", "seq"),
        P(),
        P(),
        P(),
        P(),
        P("users", "seq", None),
    )
    out_specs = (P("users", "seq", None), P(BOTH, None), P(), P())
    return jax.shard_map(layer_step, mesh=mesh, in_specs=in_specs, out_specs=out_specs, check_vma=False)
```
